128 devices in a mesh: ctx: 16 (over x, z), batch: 8 (over y, core).
Axes of the slice: x: 4, y: 4, z: 4, core: 2. Of those that a mesh axis runs over, the one named last changes fastest.
Arguments:
- mixer_input: bfloat16 [8, 2048, 10240], P('batch', 'ctx'), may hold values from -6 to 6
- z_gate: bfloat16 [8, 2048, 8192], P('batch', 'ctx'), may hold values from -6 to 6
- time_step: bfloat16 [8, 2048, 128], P('batch', 'ctx'), may hold values from -4.5 to 0.5
- conv_weight: float32 [4, 10240], replicated, may hold values from -3 to 3
- conv_bias: float32 [10240], replicated, may hold values from -3 to 3
- decay_rate: float32 [128], replicated, may hold values from 0.000146484375 to 0.25
- skip_gain: float32 [128], replicated, may hold values from 0.3 to 1.5
- norm_gain: float32 [8192], replicated, may hold values from 0.5 to 1.5
- doc_lengths: int32 [8, 6], replicated, may hold values from 1 to 1536, 2048 in all within a row
- queries: bfloat16 [8, 2048, 4096], P('batch', 'ctx'), may hold values from -101.6466 to 101.6466
- attn_keys: bfloat16 [8, 2048, 1024], P('batch', 'ctx'), may hold values from -5 to 5
- attn_values: bfloat16 [8, 2048, 1024], P('batch', 'ctx'), may hold values from -6 to 6
Outputs:
- mixer_out: bfloat16 [8, 2048, 8192], P('batch', 'ctx')
- attn_out: bfloat16 [8, 2048, 4096], P('batch', 'ctx')
The draws below stay inside these ranges and needn't reach their ends.
Inputs may be any that keep to these rules, and one draw needn't show every extreme that they name: `doc_lengths`: each sequence's 6 lengths sum to 2048, and the longest is exactly 1536.
All inputs are finite; a program needn't handle non-finite values.
Results may differ from the reference program's by a relative error of at most 0.011.
Values may be sent and summed in bfloat16 or wider, within the bound.
No kernel may reach another device: no remote copies, remote signals or barrier semaphores. Data moves between devices by JAX's collectives and lax.ppermute only.
A program may use at most 256 MiB of HBM per device.

```python
import math
import jax
import jax.numpy as jnp
import numpy as np
from jax import lax

HEADS = 128
HEAD_DIM = 64
STATE = 128
GROUPS = 8
QHEADS = 32
KVHEADS = 8
QDIM = 128
CONV = 4
STRETCH = 128
WINDOW = 2048
DOCS = 6
TOK_DEV = 128
SEQS = 8
SEQ_LEN = 2048
MOST = 1536


def draw_time_step(key, part):
    element_key, block_key = jax.random.split(jax.random.fold_in(key, 3))
    element = jax.random.uniform(element_key, (SEQS, SEQ_LEN, HEADS), jnp.float32, -3.5, -0.5)
    offsets = jax.random.uniform(block_key, (SEQS, SEQ_LEN // TOK_DEV, 1, HEADS), jnp.float32, -1.0, 1.0)
    shifted = element.reshape(SEQS, SEQ_LEN // TOK_DEV, TOK_DEV, HEADS) + offsets
    return shifted.reshape(SEQS, SEQ_LEN, HEADS).astype(jnp.bfloat16)


def draw_decay_rate(key, part):
    mix_key = jax.random.fold_in(jax.random.fold_in(key, 5), 0)
    lowest = math.log(0.3 / SEQ_LEN)
    fraction = jax.random.uniform(mix_key, (HEADS,), jnp.float32)
    return jnp.exp(lowest + fraction * (math.log(0.25) - lowest)).astype(jnp.float32)


def attention_pair(key):
    base_key = jax.random.fold_in(key, 11)
    key_key, query_key = jax.random.split(base_key)
    keys_drawn = jnp.clip(jax.random.normal(key_key, (SEQS, SEQ_LEN, KVHEADS, QDIM), jnp.float32), -5.0, 5.0)
    queries_drawn = jnp.clip(jax.random.normal(query_key, (SEQS, SEQ_LEN, KVHEADS, QHEADS // KVHEADS, QDIM), jnp.float32), -5.0, 5.0)
    return (keys_drawn.reshape(SEQS, SEQ_LEN, KVHEADS * QDIM), queries_drawn.reshape(SEQS, SEQ_LEN, QHEADS * QDIM))


def draw_queries(key, part):
    return attention_pair(key)[1].astype(jnp.bfloat16)


def draw_attn_keys(key, part):
    return attention_pair(key)[0].astype(jnp.bfloat16)


def block_levels(rng, extent, cuts, least, high):
    loudness = 1.0
    for dim, parts in cuts:
        draws = jax.random.uniform(jax.random.fold_in(jax.random.fold_in(rng, 6), dim), (parts,), jnp.float32, least / len(cuts), high / len(cuts))
        loudness = loudness * jnp.repeat(jnp.exp(draws), extent[dim] // parts).reshape((-1,) + (1,) * (len(extent) - 1 - dim))
    return loudness


def split_up(count, total, most, lean):
    weights = [(1 << 20) // math.isqrt(rank ** lean) + 1 for rank in range(2, count + 1)]
    surplus, holding = total - most - (count - 1), [1] * (count - 1)
    while surplus > 0:
        free = [i for i in range(count - 1) if holding[i] < most]
        pool, left = sum([weights[i] for i in free]), surplus
        for i in free:
            extra = min(most - holding[i], max(1, left * weights[i] // pool), surplus)
            holding[i] = holding[i] + extra
            surplus = surplus - extra
    return np.array([most] + holding)


def ragged_sizes(stream_key, number_of, total, reach, lean):
    if number_of == 2:
        one = jax.random.randint(stream_key, (), max(1, total - reach), min(reach, total - 1) + 1)
        return jnp.stack([one, total - one])
    sizes = jnp.asarray(split_up(number_of, total, reach, lean), jnp.int32)
    couples = (number_of - 1) // 2
    giver, receiver = sizes[1:1 + 2 * couples:2], sizes[2:2 + 2 * couples:2]
    slack = jnp.minimum(giver - 1, reach - receiver)
    moved = jax.random.randint(jax.random.fold_in(stream_key, 1), (couples,), 0, 1 << 20) % (slack + 1)
    sizes = sizes.at[1:1 + 2 * couples:2].set(giver - moved).at[2:2 + 2 * couples:2].set(receiver + moved)
    return sizes[jax.random.permutation(jax.random.fold_in(stream_key, 2), number_of)]


def bell_draw(rng, shape, scale, most, cuts=(), held_as=jnp.bfloat16):
    loudness = block_levels(rng, shape, cuts, -0.22, 0.18) if cuts else 1.0
    values = jax.random.normal(rng, shape, jnp.float32) * scale * loudness
    return jnp.minimum(jnp.maximum(values, -most), most).astype(held_as)


def setup_inputs(seed: int = 0) -> dict:
    splits = jax.random.split(jax.random.key(seed), 13)
    return {
        "mixer_input": bell_draw(splits[0], (SEQS, SEQ_LEN, HEADS * HEAD_DIM + 2 * GROUPS * STATE), 1.0, 6.0, ((0, 8), (1, 16))),
        "z_gate": bell_draw(splits[1], (SEQS, SEQ_LEN, HEADS * HEAD_DIM), 1.0, 6.0, ((0, 8), (1, 16))),
        "time_step": draw_time_step(jax.random.fold_in(splits[12], 71), 0),
        "conv_weight": bell_draw(splits[3], (CONV, HEADS * HEAD_DIM + 2 * GROUPS * STATE), CONV ** -0.5, 3.0, (), jnp.float32),
        "conv_bias": bell_draw(splits[4], (HEADS * HEAD_DIM + 2 * GROUPS * STATE,), 0.5, 3.0, (), jnp.float32),
        "decay_rate": draw_decay_rate(jax.random.fold_in(splits[12], 71), 0),
        "skip_gain": jnp.clip(jax.random.uniform(splits[6], (HEADS,), jnp.float32, 0.3, 1.5), 0.3, 1.5),
        "norm_gain": jnp.clip(1.0 + 0.1 * jax.random.normal(splits[7], (HEADS * HEAD_DIM,), jnp.float32), 0.5, 1.5),
        "doc_lengths": jax.vmap(lambda own: ragged_sizes(own, DOCS, SEQ_LEN, MOST, 2))(jax.random.split(splits[8], SEQS)).reshape((SEQS, DOCS)).astype(jnp.int32),
        "queries": draw_queries(jax.random.fold_in(splits[12], 71), 0),
        "attn_keys": draw_attn_keys(jax.random.fold_in(splits[12], 71), 0),
        "attn_values": bell_draw(splits[11], (SEQS, SEQ_LEN, KVHEADS * QDIM), 1.0, 6.0, ((0, 8), (1, 16))),
    }


EPSILON = 1e-05
NEGATIVE = -1e+30

def product(pattern, first_op, second_op):
    return jnp.einsum(pattern, first_op.astype(jnp.float32), second_op.astype(jnp.float32), precision=lax.Precision.HIGHEST)

def segment_ids(doc_lengths, positions):
    endings = jnp.cumsum(doc_lengths, axis=-1, dtype=jnp.int32)
    starting = endings - doc_lengths
    return lax.optimization_barrier(jnp.sum((starting[:, None, :] <= positions[None, :, None]).astype(jnp.int32), axis=-1, dtype=jnp.int32)) - 1

def causal_conv(inputs, conv_weight, conv_bias, segments, rim_rows, rim_segments):
    padded = jnp.concatenate([rim_rows, inputs], axis=1).astype(jnp.float32)
    padded_seg = jnp.concatenate([rim_segments, segments], axis=1)
    length = inputs.shape[1]
    kernel_taps = conv_weight.shape[0]
    summed = jnp.zeros(inputs.shape, jnp.float32) + conv_bias
    for offset in range(kernel_taps):
        window_rows = padded[:, offset:offset + length]
        matches = (padded_seg[:, offset:offset + length] == segments)[..., None]
        summed = summed + jnp.where(matches, window_rows * conv_weight[offset], 0.0)
    return jax.nn.silu(summed).astype(jnp.bfloat16)

def ssd_block(carried_in, pieces, decay_rates, skip_gains):
    state_now, prev_seg = carried_in
    head_inputs, step_sizes, input_proj, output_proj, segments = pieces
    log_decay = jnp.cumsum(-step_sizes * decay_rates, axis=1)
    block_len = segments.shape[1]
    position = jnp.arange(block_len, dtype=jnp.int32)
    related = (segments[:, :, None] == segments[:, None, :]) & (position[:, None] >= position[None, :])
    spread = log_decay[:, :, None] - log_decay[:, None, :]
    decays = jnp.where(related[..., None, None], jnp.exp(jnp.minimum(spread, 0.0)), 0.0)
    scores = product('sqgn,skgn->sqkg', output_proj, input_proj)
    weights = (scores[..., None] * decays * step_sizes[:, None]).astype(jnp.bfloat16)
    inner_part = product('sqkgr,skgrp->sqgrp', weights, head_inputs)
    carried = product('sqgn,sgrnp->sqgrp', output_proj, state_now)
    keep_rows = (segments == prev_seg[:, None])[:, :, None, None]
    between = jnp.where(keep_rows, jnp.exp(log_decay), 0.0)[..., None] * carried
    outputs = inner_part + between + skip_gains[..., None] * head_inputs.astype(jnp.float32)
    last_seg = segments[:, -1]
    trailing = jnp.where((segments == last_seg[:, None])[:, :, None, None], jnp.exp(log_decay[:, -1:] - log_decay) * step_sizes, 0.0)
    fresh_state = product('sqgn,sqgrp->sgrnp', input_proj, trailing[..., None] * head_inputs.astype(jnp.float32))
    through = jnp.where((last_seg == prev_seg)[:, None, None], jnp.exp(log_decay[:, -1]), 0.0)
    return ((through[..., None, None] * state_now + fresh_state, last_seg), outputs.astype(jnp.bfloat16))

def run_blocks(head_inputs, step_sizes, input_proj, output_proj, segments, decay_rates, skip_gains, block_len):
    num_seqs, length = segments.shape
    state_zero = jnp.zeros((num_seqs,) + head_inputs.shape[2:4] + (input_proj.shape[-1], head_inputs.shape[-1]), jnp.float32)
    prev_zero = jnp.full((num_seqs,), -1, jnp.int32)

    def advance(carried_in, block_index):
        block_start = block_index * block_len
        pieces = tuple((lax.dynamic_slice_in_dim(array_in, block_start, block_len, 1) for array_in in (head_inputs, step_sizes, input_proj, output_proj, segments)))
        return ssd_block(carried_in, pieces, decay_rates, skip_gains)
    final_carry, outputs = lax.scan(advance, (state_zero, prev_zero), jnp.arange(length // block_len, dtype=jnp.int32))
    return jnp.moveaxis(outputs, 0, 1).reshape(head_inputs.shape)

def reference(mixer_input, z_gate, time_step, conv_weight, conv_bias, decay_rate, skip_gain, norm_gain, doc_lengths, queries, attn_keys, attn_values):
    inner_width = HEADS * HEAD_DIM
    proj_width = GROUPS * STATE
    per_group = HEADS // GROUPS
    segments = segment_ids(doc_lengths, jnp.arange(SEQ_LEN, dtype=jnp.int32))

    def convolve(operands):
        sequence, seq_segments = operands
        rim_rows = jnp.zeros((1, CONV - 1, sequence.shape[-1]), jnp.bfloat16)
        rim_segments = jnp.full((1, CONV - 1), -1, jnp.int32)
        return causal_conv(sequence[None], conv_weight, conv_bias, seq_segments[None], rim_rows, rim_segments)[0]
    activated = lax.map(convolve, (mixer_input, segments))
    head_inputs = activated[:, :, :inner_width].reshape(SEQS, SEQ_LEN, GROUPS, per_group, HEAD_DIM)
    input_proj = activated[:, :, inner_width:inner_width + proj_width].reshape(SEQS, SEQ_LEN, GROUPS, STATE)
    output_proj = activated[:, :, inner_width + proj_width:].reshape(SEQS, SEQ_LEN, GROUPS, STATE)
    step_sizes = jax.nn.softplus(time_step.astype(jnp.float32)).reshape(SEQS, SEQ_LEN, GROUPS, per_group)
    mixed = run_blocks(head_inputs, step_sizes, input_proj, output_proj, segments, decay_rate.reshape(GROUPS, per_group), skip_gain.reshape(GROUPS, per_group), STRETCH)
    mixed = mixed.reshape(SEQS, SEQ_LEN, inner_width)

    def normalize(operands):
        mixed_seq, gate_seq = operands
        gated = mixed_seq.astype(jnp.float32) * jax.nn.silu(gate_seq.astype(jnp.float32))
        grouped = gated.reshape(SEQ_LEN, GROUPS, inner_width // GROUPS)
        scaling = lax.rsqrt(lax.optimization_barrier(jnp.mean(grouped * grouped, axis=-1, keepdims=True)) + EPSILON)
        return ((grouped * scaling).reshape(SEQ_LEN, inner_width) * norm_gain).astype(jnp.bfloat16)
    mixer_out = lax.map(normalize, (mixed, z_gate))
    block_rows = 512 if SEQ_LEN % 512 == 0 else SEQ_LEN
    group_size = QHEADS // KVHEADS
    key_span = block_rows + WINDOW - 1
    scaling = QDIM ** (-0.5)

    def attend_sequence(operands):
        query_seq, key_seq, value_seq, seq_segments = operands
        keys_padded = jnp.concatenate([jnp.zeros((WINDOW - 1, KVHEADS * QDIM), jnp.bfloat16), key_seq], axis=0).reshape(-1, KVHEADS, QDIM)
        values_padded = jnp.concatenate([jnp.zeros((WINDOW - 1, KVHEADS * QDIM), jnp.bfloat16), value_seq], axis=0).reshape(-1, KVHEADS, QDIM)
        segs_padded = jnp.concatenate([jnp.full((WINDOW - 1,), -1, jnp.int32), seq_segments], axis=0)

        def attend_block(block_index):
            query_start = block_index * block_rows
            query_block = lax.dynamic_slice_in_dim(query_seq, query_start, block_rows, 0).reshape(block_rows, KVHEADS, group_size, QDIM)
            key_block = lax.dynamic_slice_in_dim(keys_padded, query_start, key_span, 0)
            value_block = lax.dynamic_slice_in_dim(values_padded, query_start, key_span, 0)
            key_segs = lax.dynamic_slice_in_dim(segs_padded, query_start, key_span, 0)
            query_segs = lax.dynamic_slice_in_dim(seq_segments, query_start, block_rows, 0)
            query_pos = query_start + jnp.arange(block_rows, dtype=jnp.int32)
            key_pos = query_start - (WINDOW - 1) + jnp.arange(key_span, dtype=jnp.int32)
            visible = (key_segs[None, :] == query_segs[:, None]) & (key_pos[None, :] <= query_pos[:, None]) & (query_pos[:, None] - key_pos[None, :] < WINDOW)
            scores = product('qkgd,rkd->kgqr', query_block, key_block) * scaling
            masked = jnp.where(visible, scores, NEGATIVE)
            highest = lax.optimization_barrier(jnp.max(masked, axis=-1, keepdims=True))
            numerators = jnp.where(visible, jnp.exp(masked - highest), 0.0)
            totals = lax.optimization_barrier(jnp.sum(numerators, axis=-1))
            summed = product('kgqr,rkd->qkgd', numerators.astype(jnp.bfloat16), value_block)
            return (summed / jnp.moveaxis(totals, -1, 0)[..., None]).reshape(block_rows, QHEADS * QDIM).astype(jnp.bfloat16)
        blocks = lax.map(attend_block, jnp.arange(SEQ_LEN // block_rows, dtype=jnp.int32))
        return blocks.reshape(SEQ_LEN, QHEADS * QDIM)
    attn_out = lax.map(attend_sequence, (queries, attn_keys, attn_values, segments))
    return (mixer_out, attn_out)
```

```python
import functools

import jax
import jax.numpy as jnp
from jax import lax
from jax.experimental import pallas as pl
from jax.experimental.pallas import tpu as pltpu
from jax.sharding import PartitionSpec as P

HEADS = 128
HEAD_DIM = 64
STATE = 128
GROUPS = 8
QHEADS = 32
KVHEADS = 8
QDIM = 128
CONV = 4
WINDOW = 2048

PER_GROUP = HEADS // GROUPS
WIDTH = PER_GROUP * HEAD_DIM
INNER = HEADS * HEAD_DIM
DOCS = 6
EPSILON = 1e-05
NEGATIVE = -1e30
LOG2E = 1.4426950408889634
EXTRA = 8
KEYS = 512

F32 = jnp.float32
BF16 = jnp.bfloat16
HIGH = lax.Precision.HIGHEST


def dot(a, b, dims=(((1,), (0,)), ((), ())), precision=None):
    return lax.dot_general(a, b, dims, precision=precision, preferred_element_type=F32)


def doc_starts(place_ref, lengths_ref):
    seq = place_ref[1]
    starts = [jnp.int32(0)]
    for d in range(DOCS - 1):
        starts.append(starts[-1] + lengths_ref[seq, d])
    return starts


def row_starts(starts, pos):
    first = jnp.zeros_like(pos)
    for s in starts[1:]:
        first = jnp.where(pos >= s, s, first)
    return first


def scalar_start(starts, pos):
    first = jnp.int32(0)
    for s in starts[1:]:
        first = jnp.where(pos >= s, s, first)
    return first


def expand_heads():
    row = lax.broadcasted_iota(jnp.int32, (PER_GROUP, WIDTH), 0)
    lane = lax.broadcasted_iota(jnp.int32, (PER_GROUP, WIDTH), 1)
    return (lane // HEAD_DIM == row).astype(F32)


def prep_kernel(place_ref, lengths_ref, step_ref, rate_ref, col_ref, row_ref, trail_ref, keep_ref, thr_ref):
    rows = step_ref.shape[0]
    base = place_ref[0] * rows
    starts = doc_starts(place_ref, lengths_ref)
    pos = base + lax.broadcasted_iota(jnp.int32, (rows, HEADS), 0)
    first = row_starts(starts, pos)
    last_first = scalar_start(starts, base + rows - 1)
    t = step_ref[...].astype(F32)
    dt = jnp.maximum(t, 0.0) + jnp.log1p(jnp.exp(-jnp.abs(t)))
    a = dt * rate_ref[...] * (-LOG2E)
    i = lax.broadcasted_iota(jnp.int32, (rows, rows), 0)
    j = lax.broadcasted_iota(jnp.int32, (rows, rows), 1)
    tri = (i >= j).astype(F32)
    cum = dot(tri, a, precision=HIGH)
    total = cum[rows - 1 : rows, :]
    trail = jnp.where(first == last_first, jnp.exp2(total - cum) * dt, 0.0)
    keep = jnp.where(first < base, jnp.exp2(cum), 0.0)
    thr = jnp.where(last_first < base, jnp.exp2(total), 0.0)
    row_ref[...] = jnp.transpose(cum - jnp.log2(dt))
    for g in range(GROUPS):
        part = slice(g * PER_GROUP, (g + 1) * PER_GROUP)
        col_ref[g] = cum[:, part]
        trail_ref[g] = trail[:, part]
        keep_ref[g] = keep[:, part]
        thr_ref[g] = jnp.broadcast_to(thr[:, part], (8, PER_GROUP))


def front_kernel(
    place_ref, lengths_ref, x_ref, b_ref, c_ref, hx_ref, hb_ref, hc_ref,
    wx_ref, wb_ref, wc_ref, ox_ref, ob_ref, oc_ref, trail_ref, thr_ref,
    xa_ref, ba_ref, ca_ref, f_ref, pad_ref,
):
    rows = x_ref.shape[0]
    base = place_ref[0] * rows
    starts = doc_starts(place_ref, lengths_ref)
    pos = base + lax.broadcasted_iota(jnp.int32, (rows, 128), 0)
    rel = pos - row_starts(starts, pos)
    masks = [None] + [rel >= d for d in range(1, CONV)]

    def conv(src, rim, weight, bias, dst, lo):
        at = slice(lo, lo + 128)
        pad_ref[0:8, :] = rim[:, at].astype(F32)
        pad_ref[8 : 8 + rows, :] = src[:, at].astype(F32)
        acc = pad_ref[8 : 8 + rows, :] * weight[3:4, at] + bias[:, at]
        for d in range(1, CONV):
            tap = pad_ref[8 - d : 8 - d + rows, :] * weight[3 - d : 4 - d, at]
            acc = acc + jnp.where(masks[d], tap, 0.0)
        dst[:, at] = (acc / (1.0 + jnp.exp(-acc))).astype(BF16)

    for lo in range(0, WIDTH, 128):
        conv(x_ref, hx_ref, wx_ref, ox_ref, xa_ref, lo)
    conv(b_ref, hb_ref, wb_ref, ob_ref, ba_ref, 0)
    conv(c_ref, hc_ref, wc_ref, oc_ref, ca_ref, 0)

    spread = expand_heads()
    scale = dot(trail_ref[0], spread, precision=HIGH)
    weighted = (xa_ref[...].astype(F32) * scale).astype(BF16)
    fresh = dot(ba_ref[...], weighted, (((0,), (0,)), ((), ()))).astype(BF16)
    thr = dot(thr_ref[0], spread, precision=HIGH)
    upper = thr.astype(BF16)
    lower = (thr - upper.astype(F32)).astype(BF16)
    rowid = lax.broadcasted_iota(jnp.int32, (8, WIDTH), 0)
    extra = jnp.where(rowid == 0, upper.astype(F32), jnp.where(rowid == 1, lower.astype(F32), 0.0)).astype(BF16)
    half = WIDTH // 2
    for k in range(2):
        f_ref[k, 0:STATE, :] = fresh[:, k * half : (k + 1) * half]
        f_ref[k, STATE : STATE + EXTRA, :] = extra[:, k * half : (k + 1) * half]


def inner_kernel(place_ref, lengths_ref, xa_ref, ba_ref, ca_ref, col_ref, row_ref, skip_ref, y_ref):
    rows = xa_ref.shape[0]
    base = place_ref[0] * rows
    starts = doc_starts(place_ref, lengths_ref)
    i = base + lax.broadcasted_iota(jnp.int32, (rows, rows), 0)
    j = base + lax.broadcasted_iota(jnp.int32, (rows, rows), 1)
    first = row_starts(starts, i)
    blocked = jnp.where((j <= i) & (j >= first), 0.0, NEGATIVE)
    scores = dot(ca_ref[...], ba_ref[...], (((1,), (1,)), ((), ())))
    lane = lax.broadcasted_iota(jnp.int32, (rows, 128), 1)
    col = col_ref[0]
    for p in range(PER_GROUP // 2):
        weights = []
        for h in (2 * p, 2 * p + 1):
            spread = (col[:, h : h + 1] + blocked) - row_ref[h : h + 1, :]
            weights.append((scores * jnp.exp2(spread)).astype(BF16))
        at = slice(p * 128, (p + 1) * 128)
        x = xa_ref[:, at]
        zero = jnp.zeros_like(x)
        both = jnp.concatenate(
            [jnp.where(lane < HEAD_DIM, x, zero), jnp.where(lane < HEAD_DIM, zero, x)], axis=0
        )
        y = dot(jnp.concatenate(weights, axis=1), both)
        y_ref[:, at] = y + x.astype(F32) * skip_ref[:, at]


def scan_kernel(f_ref, s_ref):
    blocks = f_ref.shape[0]
    piece = 32

    def body(q, carry):
        at = pl.ds(pl.multiple_of(q * piece, piece), piece)
        state = jnp.zeros((piece, f_ref.shape[2]), F32)
        for r in range(blocks):
            s_ref[r, at, :] = state.astype(BF16)
            if r + 1 < blocks:
                tail = f_ref[r, STATE : STATE + EXTRA, :].astype(F32)
                thr = tail[0:1, :] + tail[1:2, :]
                state = state * thr + f_ref[r, at, :].astype(F32)
        return carry

    lax.fori_loop(0, STATE // piece, body, 0)


def final_kernel(y_ref, s_ref, ca_ref, keep_ref, z_ref, gain_ref, o_ref):
    spread = expand_heads()
    scale = dot(keep_ref[0], spread, precision=HIGH)
    states = jnp.concatenate([s_ref[0], s_ref[1]], axis=1)
    carried = dot(ca_ref[...], states)
    mixed = (y_ref[...] + scale * carried).astype(BF16).astype(F32)
    z = z_ref[...].astype(F32)
    gated = mixed * (z / (1.0 + jnp.exp(-z)))
    mean = jnp.mean(gated * gated, axis=1, keepdims=True)
    o_ref[...] = (gated * lax.rsqrt(mean + EPSILON) * gain_ref[...]).astype(BF16)


def attend_kernel(place_ref, lengths_ref, q_ref, k_ref, v_ref, o_ref, m_ref, l_ref, acc_ref):
    rows = q_ref.shape[0]
    share = q_ref.shape[1] // QDIM
    base = place_ref[0] * rows
    starts = doc_starts(place_ref, lengths_ref)
    pos = base + lax.broadcasted_iota(jnp.int32, (rows, KEYS), 0)
    first = jnp.maximum(row_starts(starts, pos), pos - (WINDOW - 1))
    lane = lax.broadcasted_iota(jnp.int32, (rows, KEYS), 1)
    scaling = QDIM ** (-0.5) * LOG2E
    m_ref[...] = jnp.full_like(m_ref, NEGATIVE)
    l_ref[...] = jnp.zeros_like(l_ref)
    acc_ref[...] = jnp.zeros_like(acc_ref)
    lowest = jnp.maximum(scalar_start(starts, base), base - (WINDOW - 1))

    def step(j, carry):
        at = pl.ds(pl.multiple_of(j * KEYS, KEYS), KEYS)
        k = k_ref[at, :]
        v = v_ref[at, :]
        key = j * KEYS + lane
        visible = (key <= pos) & (key >= first)
        for h in range(share):
            s = dot(q_ref[:, h * QDIM : (h + 1) * QDIM], k, (((1,), (1,)), ((), ()))) * scaling
            s = jnp.where(visible, s, NEGATIVE)
            m_old = m_ref[h]
            m_new = jnp.maximum(m_old, jnp.max(s, axis=1, keepdims=True))
            fade = jnp.exp2(m_old - m_new)
            p = jnp.exp2(s - m_new)
            l_ref[h] = l_ref[h] * fade + jnp.sum(p, axis=1, keepdims=True)
            acc_ref[h] = acc_ref[h] * fade + dot(p.astype(BF16), v)
            m_ref[h] = m_new
        return carry

    lax.fori_loop(lowest // KEYS, (base + rows - 1) // KEYS + 1, step, 0)
    for h in range(share):
        o_ref[:, h * QDIM : (h + 1) * QDIM] = (acc_ref[h] / l_ref[h]).astype(BF16)


def smem():
    return pl.BlockSpec(memory_space=pltpu.SMEM)


def on_device(
    mixer_input, z_gate, time_step, conv_weight, conv_bias, decay_rate, skip_gain,
    norm_gain, doc_lengths, queries, attn_keys, attn_values,
):
    rows = mixer_input.shape[1]
    blocks = lax.axis_size("ctx")
    place = jnp.stack([lax.axis_index("ctx"), lax.axis_index("batch")]).astype(jnp.int32)
    raw = mixer_input[0]
    call = functools.partial(
        pl.pallas_call, compiler_params=pltpu.CompilerParams(vmem_limit_bytes=56 << 20)
    )

    keys_values = jnp.concatenate([attn_keys[0], attn_values[0]], axis=1)
    rim = lax.ppermute(raw[rows - 8 :], "ctx", [(r, r + 1) for r in range(blocks - 1)])
    whole_kv = lax.all_gather(keys_values, "ctx", axis=0, tiled=True)

    col, row, trail, keep, thr = call(
        prep_kernel,
        in_specs=[smem(), smem(), pl.BlockSpec(), pl.BlockSpec()],
        out_shape=[
            jax.ShapeDtypeStruct((GROUPS, rows, PER_GROUP), F32),
            jax.ShapeDtypeStruct((HEADS, rows), F32),
            jax.ShapeDtypeStruct((GROUPS, rows, PER_GROUP), F32),
            jax.ShapeDtypeStruct((GROUPS, rows, PER_GROUP), F32),
            jax.ShapeDtypeStruct((GROUPS, 8, PER_GROUP), F32),
        ],
        name="prep",
    )(place, doc_lengths, time_step[0], decay_rate[None])

    wide = lambda n: pl.BlockSpec((n, WIDTH), lambda g: (0, g))
    b_cols = lambda n: pl.BlockSpec((n, STATE), lambda g: (0, INNER // STATE + g))
    c_cols = lambda n: pl.BlockSpec((n, STATE), lambda g: (0, INNER // STATE + GROUPS + g))
    group_cols = lambda n: pl.BlockSpec((n, STATE), lambda g: (0, g))
    per_group = pl.BlockSpec((1, rows, PER_GROUP), lambda g: (g, 0, 0))
    bias = conv_bias[None]
    half = WIDTH // 2
    x_act, b_act, c_act, fresh = call(
        front_kernel,
        grid=(GROUPS,),
        in_specs=[
            smem(), smem(),
            wide(rows), b_cols(rows), c_cols(rows),
            wide(8), b_cols(8), c_cols(8),
            wide(CONV), b_cols(CONV), c_cols(CONV),
            wide(1), b_cols(1), c_cols(1),
            per_group, pl.BlockSpec((1, 8, PER_GROUP), lambda g: (g, 0, 0)),
        ],
        out_specs=[
            wide(rows), group_cols(rows), group_cols(rows),
            pl.BlockSpec((2, STATE + EXTRA, half), lambda g: (g, 0, 0)),
        ],
        out_shape=[
            jax.ShapeDtypeStruct((rows, INNER), BF16),
            jax.ShapeDtypeStruct((rows, GROUPS * STATE), BF16),
            jax.ShapeDtypeStruct((rows, GROUPS * STATE), BF16),
            jax.ShapeDtypeStruct((2 * GROUPS, STATE + EXTRA, half), BF16),
        ],
        scratch_shapes=[pltpu.VMEM((8 + rows, 128), F32)],
        name="front",
    )(
        place, doc_lengths, raw, raw, raw, rim, rim, rim,
        conv_weight, conv_weight, conv_weight, bias, bias, bias, trail, thr,
    )

    own_fresh = lax.all_to_all(fresh, "ctx", split_axis=0, concat_axis=0, tiled=True)

    local = call(
        inner_kernel,
        grid=(GROUPS,),
        in_specs=[
            smem(), smem(), wide(rows), group_cols(rows), group_cols(rows), per_group,
            pl.BlockSpec((PER_GROUP, rows), lambda g: (g, 0)), wide(1),
        ],
        out_specs=wide(rows),
        out_shape=jax.ShapeDtypeStruct((rows, INNER), F32),
        name="inner",
    )(place, doc_lengths, x_act, b_act, c_act, col, row, jnp.repeat(skip_gain, HEAD_DIM)[None])

    own_states = call(
        scan_kernel,
        out_shape=jax.ShapeDtypeStruct((blocks, STATE, half), BF16),
        name="scan",
    )(own_fresh)
    states = lax.all_to_all(own_states, "ctx", split_axis=0, concat_axis=0, tiled=True)

    share = QHEADS // KVHEADS
    keys = whole_kv.shape[0]
    attn_out = call(
        attend_kernel,
        grid=(KVHEADS,),
        in_specs=[
            smem(), smem(),
            pl.BlockSpec((rows, share * QDIM), lambda h: (0, h)),
            pl.BlockSpec((keys, QDIM), lambda h: (0, h)),
            pl.BlockSpec((keys, QDIM), lambda h: (0, KVHEADS + h)),
        ],
        out_specs=pl.BlockSpec((rows, share * QDIM), lambda h: (0, h)),
        out_shape=jax.ShapeDtypeStruct((rows, QHEADS * QDIM), BF16),
        scratch_shapes=[
            pltpu.VMEM((share, rows, 1), F32),
            pltpu.VMEM((share, rows, 1), F32),
            pltpu.VMEM((share, rows, QDIM), F32),
        ],
        name="attend",
    )(place, doc_lengths, queries[0], whole_kv, whole_kv)

    mixer_out = call(
        final_kernel,
        grid=(GROUPS,),
        in_specs=[
            wide(rows), pl.BlockSpec((2, STATE, half), lambda g: (g, 0, 0)), group_cols(rows),
            per_group, wide(rows), wide(1),
        ],
        out_specs=wide(rows),
        out_shape=jax.ShapeDtypeStruct((rows, INNER), BF16),
        name="final",
    )(local, states, c_act, keep, z_gate[0], norm_gain[None])
    return (mixer_out[None], attn_out[None])


def solution(mesh):
    placed = P("batch", "ctx", None)
    whole = P()
    return jax.shard_map(
        on_device,
        mesh=mesh,
        in_specs=(placed, placed, placed) + (whole,) * 6 + (placed,) * 3,
        out_specs=(placed, placed),
        check_vma=False,
    )
```

```python
import functools

import jax
import jax.numpy as jnp
from jax import lax
from jax.experimental import pallas as pl
from jax.experimental.pallas import tpu as pltpu
from jax.sharding import PartitionSpec as P

HEADS = 128
HEAD_DIM = 64
STATE = 128
GROUPS = 8
QHEADS = 32
KVHEADS = 8
QDIM = 128
CONV = 4
WINDOW = 2048

PER_GROUP = HEADS // GROUPS
WIDTH = PER_GROUP * HEAD_DIM
INNER = HEADS * HEAD_DIM
DOCS = 6
EPSILON = 1e-05
NEGATIVE = -1e30
LOG2E = 1.4426950408889634
EXTRA = 8
KEYS = 256

F32 = jnp.float32
BF16 = jnp.bfloat16
HIGH = lax.Precision.HIGHEST


def dot(a, b, dims=(((1,), (0,)), ((), ())), precision=None):
    return lax.dot_general(a, b, dims, precision=precision, preferred_element_type=F32)


def doc_starts(place_ref, lengths_ref):
    seq = place_ref[1]
    starts = [jnp.int32(0)]
    for d in range(DOCS - 1):
        starts.append(starts[-1] + lengths_ref[seq, d])
    return starts


def row_starts(starts, pos):
    first = jnp.zeros_like(pos)
    for s in starts[1:]:
        first = jnp.where(pos >= s, s, first)
    return first


def scalar_start(starts, pos):
    first = jnp.int32(0)
    for s in starts[1:]:
        first = jnp.where(pos >= s, s, first)
    return first


def expand_heads(copies):
    shape = (copies * PER_GROUP, WIDTH)
    row = lax.broadcasted_iota(jnp.int32, shape, 0) % PER_GROUP
    lane = lax.broadcasted_iota(jnp.int32, shape, 1)
    return jnp.where(lane // HEAD_DIM == row, 1.0, 0.0).astype(BF16)


def halves(x):
    upper = x.astype(BF16)
    return upper, (x - upper.astype(F32)).astype(BF16)


def silu(x):
    return (0.5 * x) * (1.0 + jnp.tanh(0.5 * x))


def prep_kernel(place_ref, lengths_ref, step_ref, rate_ref, col_ref, row_ref, trail_ref, keep_ref, thr_ref):
    rows = step_ref.shape[0]
    base = place_ref[0] * rows
    starts = doc_starts(place_ref, lengths_ref)
    pos = base + lax.broadcasted_iota(jnp.int32, (rows, HEADS), 0)
    first = row_starts(starts, pos)
    last_first = scalar_start(starts, base + rows - 1)
    t = step_ref[...].astype(F32)
    dt = jnp.maximum(t, 0.0) + jnp.log1p(jnp.exp(-jnp.abs(t)))
    a = dt * rate_ref[...] * (-LOG2E)
    i = lax.broadcasted_iota(jnp.int32, (rows, rows), 0)
    j = lax.broadcasted_iota(jnp.int32, (rows, rows), 1)
    tri = (i >= j).astype(F32)
    cum = dot(tri, a, precision=HIGH)
    total = cum[rows - 1 : rows, :]
    trail = halves(jnp.where(first == last_first, jnp.exp2(total - cum) * dt, 0.0))
    keep = halves(jnp.where(first < base, jnp.exp2(cum), 0.0))
    thr = halves(jnp.where(last_first < base, jnp.exp2(total), 0.0))
    row8 = lax.broadcasted_iota(jnp.int32, (8, HEADS), 0)
    thr_rows = jnp.where(
        row8 == 0, thr[0].astype(F32), jnp.where(row8 == 1, thr[1].astype(F32), 0.0)
    ).astype(BF16)
    row_ref[...] = jnp.transpose(cum - jnp.log2(dt))
    for g in range(GROUPS):
        part = slice(g * PER_GROUP, (g + 1) * PER_GROUP)
        col_ref[g] = cum[:, part]
        trail_ref[g] = jnp.concatenate([trail[0][:, part], trail[1][:, part]], axis=1)
        keep_ref[g] = jnp.concatenate([keep[0][:, part], keep[1][:, part]], axis=1)
        thr_ref[g] = thr_rows[:, part]


def front_kernel(
    place_ref, lengths_ref, x_ref, b_ref, c_ref, hx_ref, hb_ref, hc_ref,
    wx_ref, wb_ref, wc_ref, ox_ref, ob_ref, oc_ref, trail_ref, thr_ref,
    xa_ref, ba_ref, ca_ref, f_ref, pad_ref,
):
    rows = x_ref.shape[0]
    base = place_ref[0] * rows
    starts = doc_starts(place_ref, lengths_ref)
    pos = base + lax.broadcasted_iota(jnp.int32, (rows, 128), 0)
    rel = pos - row_starts(starts, pos)
    masks = [None] + [rel >= d for d in range(1, CONV)]

    def conv(src, rim, weight, bias, dst, lo):
        at = slice(lo, lo + 128)
        pad_ref[0:8, :] = rim[:, at].astype(F32)
        pad_ref[8 : 8 + rows, :] = src[:, at].astype(F32)
        acc = pad_ref[8 : 8 + rows, :] * weight[3:4, at] + bias[:, at]
        for d in range(1, CONV):
            tap = pad_ref[8 - d : 8 - d + rows, :] * weight[3 - d : 4 - d, at]
            acc = acc + jnp.where(masks[d], tap, 0.0)
        dst[:, at] = silu(acc).astype(BF16)

    for lo in range(0, WIDTH, 128):
        conv(x_ref, hx_ref, wx_ref, ox_ref, xa_ref, lo)
    conv(b_ref, hb_ref, wb_ref, ob_ref, ba_ref, 0)
    conv(c_ref, hc_ref, wc_ref, oc_ref, ca_ref, 0)

    scale = dot(trail_ref[0], expand_heads(2))
    weighted = (xa_ref[...].astype(F32) * scale).astype(BF16)
    fresh = dot(ba_ref[...], weighted, (((0,), (0,)), ((), ()))).astype(BF16)
    extra = dot(thr_ref[0], expand_heads(1)).astype(BF16)
    half = WIDTH // 2
    for k in range(2):
        f_ref[k, 0:STATE, :] = fresh[:, k * half : (k + 1) * half]
        f_ref[k, STATE : STATE + EXTRA, :] = extra[:, k * half : (k + 1) * half]


def inner_kernel(place_ref, lengths_ref, xa_ref, ba_ref, ca_ref, col_ref, row_ref, skip_ref, y_ref):
    rows = xa_ref.shape[0]
    base = place_ref[0] * rows
    starts = doc_starts(place_ref, lengths_ref)
    i = base + lax.broadcasted_iota(jnp.int32, (rows, rows), 0)
    j = base + lax.broadcasted_iota(jnp.int32, (rows, rows), 1)
    first = row_starts(starts, i)
    blocked = jnp.where((j <= i) & (j >= first), 0.0, NEGATIVE)
    scores = dot(ca_ref[...], ba_ref[...], (((1,), (1,)), ((), ())))
    lane = lax.broadcasted_iota(jnp.int32, (rows, 128), 1)
    col = col_ref[0]
    for p in range(PER_GROUP // 2):
        weights = []
        for h in (2 * p, 2 * p + 1):
            spread = (col[:, h : h + 1] + blocked) - row_ref[h : h + 1, :]
            weights.append((scores * jnp.exp2(spread)).astype(BF16))
        at = slice(p * 128, (p + 1) * 128)
        x = xa_ref[:, at]
        zero = jnp.zeros_like(x)
        both = jnp.concatenate(
            [jnp.where(lane < HEAD_DIM, x, zero), jnp.where(lane < HEAD_DIM, zero, x)], axis=0
        )
        y = dot(jnp.concatenate(weights, axis=1), both)
        y_ref[:, at] = y + x.astype(F32) * skip_ref[:, at]


def scan_kernel(f_ref, o_ref, out_ref):
    blocks, _, width = f_ref.shape
    piece = 32
    for r in range(blocks):
        out_ref[r, :, width:] = o_ref[r]

    def body(q, carry):
        at = pl.ds(pl.multiple_of(q * piece, piece), piece)
        state = jnp.zeros((piece, width), F32)
        for r in range(blocks):
            out_ref[r, at, :width] = state.astype(BF16)
            if r + 1 < blocks:
                tail = f_ref[r, STATE : STATE + EXTRA, :].astype(F32)
                thr = tail[0:1, :] + tail[1:2, :]
                state = state * thr + f_ref[r, at, :].astype(F32)
        return carry

    lax.fori_loop(0, STATE // piece, body, 0)


def final_kernel(y_ref, s_ref, ca_ref, keep_ref, z_ref, gain_ref, o_ref, attn_ref):
    scale = dot(keep_ref[0], expand_heads(2))
    half = WIDTH // 2
    parts = []
    for k in range(2):
        parts.append(dot(ca_ref[...], s_ref[k, :, :half]))
        own = s_ref.shape[2] - half
        attn_ref[:, k * own : (k + 1) * own] = s_ref[k, :, half:]
    carried = jnp.concatenate(parts, axis=1)
    mixed = (y_ref[...] + scale * carried).astype(BF16).astype(F32)
    gated = mixed * silu(z_ref[...].astype(F32))
    mean = jnp.mean(gated * gated, axis=1, keepdims=True)
    o_ref[...] = (gated * lax.rsqrt(mean + EPSILON) * gain_ref[...]).astype(BF16)


def pack_kernel(q_ref, k_ref, v_ref, out_ref):
    parts = out_ref.shape[0]
    width = q_ref.shape[1] // parts
    for d in range(parts):
        at = d * KVHEADS // parts * QDIM
        out_ref[d, :, :width] = q_ref[:, d * width : (d + 1) * width]
        out_ref[d, :, width : width + QDIM] = k_ref[:, at : at + QDIM]
        out_ref[d, :, width + QDIM :] = v_ref[:, at : at + QDIM]


def attend_kernel(place_ref, lengths_ref, qkv_ref, o_ref, s_ref, m_ref, l_ref, acc_ref):
    length = qkv_ref.shape[0]
    q_width = qkv_ref.shape[1] - 2 * QDIM
    heads = q_width // QDIM
    k_cols, v_cols = slice(q_width, q_width + QDIM), slice(q_width + QDIM, q_width + 2 * QDIM)
    starts = doc_starts(place_ref, lengths_ref)
    lane = lax.broadcasted_iota(jnp.int32, (KEYS, KEYS), 1)
    scaling = QDIM ** (-0.5) * LOG2E

    def one_tile(t, outer):
        base = t * KEYS
        here = pl.ds(pl.multiple_of(base, KEYS), KEYS)
        pos = base + lax.broadcasted_iota(jnp.int32, (KEYS, KEYS), 0)
        first = jnp.maximum(row_starts(starts, pos), pos - (WINDOW - 1))
        last = base + KEYS - 1
        lowest = jnp.maximum(scalar_start(starts, base), base - (WINDOW - 1))
        highest = jnp.maximum(scalar_start(starts, last), last - (WINDOW - 1))
        begin = lowest // KEYS
        clear = jnp.minimum((highest + KEYS - 1) // KEYS, t)
        queries = jnp.concatenate([qkv_ref[here, h * QDIM : (h + 1) * QDIM] for h in range(heads)], axis=0)
        m_ref[...] = jnp.full_like(m_ref, NEGATIVE)

        def score(masked, j, carry):
            k = qkv_ref[pl.ds(pl.multiple_of(j * KEYS, KEYS), KEYS), k_cols]
            s = dot(queries, k, (((1,), (1,)), ((), ())))
            if masked:
                key = j * KEYS + lane
                visible = (key <= pos) & (key >= first)
            for h in range(heads):
                at = slice(h * KEYS, (h + 1) * KEYS)
                part = s[at]
                if masked:
                    part = jnp.where(visible, part, NEGATIVE)
                s_ref[j, at, :] = part
                top = m_ref[at, :]
                for c in range(0, KEYS, 128):
                    top = jnp.maximum(top, part[:, c : c + 128])
                m_ref[at, :] = top
            return carry

        lax.fori_loop(begin, clear, functools.partial(score, True), 0)
        lax.fori_loop(clear, t, functools.partial(score, False), 0)
        score(True, t, 0)
        m_ref[...] = jnp.broadcast_to(jnp.max(m_ref[...], axis=1, keepdims=True), m_ref.shape)
        l_ref[...] = jnp.zeros_like(l_ref)
        acc_ref[...] = jnp.zeros_like(acc_ref)

        def gather(j, carry):
            v = qkv_ref[pl.ds(pl.multiple_of(j * KEYS, KEYS), KEYS), v_cols]
            numerators = []
            for h in range(heads):
                at = slice(h * KEYS, (h + 1) * KEYS)
                top = m_ref[at, :]
                total = l_ref[at, :]
                parts = []
                for c in range(0, KEYS, 128):
                    p = jnp.exp2((s_ref[j, at, c : c + 128] - top) * scaling)
                    total = total + p
                    parts.append(p.astype(BF16))
                l_ref[at, :] = total
                numerators.append(jnp.concatenate(parts, axis=1))
            acc_ref[...] += dot(jnp.concatenate(numerators, axis=0), v)
            return carry

        lax.fori_loop(begin, t + 1, gather, 0)
        for h in range(heads):
            at = slice(h * KEYS, (h + 1) * KEYS)
            total = jnp.sum(l_ref[at, :], axis=1, keepdims=True)
            o_ref[here, h * QDIM : (h + 1) * QDIM] = (acc_ref[at, :] / total).astype(BF16)
        return outer

    lax.fori_loop(0, length // KEYS, one_tile, 0)


def work(microseconds):
    return pl.CostEstimate(flops=0, transcendentals=0, bytes_accessed=int(microseconds * 3.5e6))


def smem():
    return pl.BlockSpec(memory_space=pltpu.SMEM)


def on_device(
    mixer_input, z_gate, time_step, conv_weight, conv_bias, decay_rate, skip_gain,
    norm_gain, doc_lengths, queries, attn_keys, attn_values,
):
    rows = mixer_input.shape[1]
    blocks = lax.axis_size("ctx")
    place = jnp.stack([lax.axis_index("ctx"), lax.axis_index("batch")]).astype(jnp.int32)
    raw = mixer_input[0]
    call = functools.partial(
        pl.pallas_call, compiler_params=pltpu.CompilerParams(vmem_limit_bytes=56 << 20)
    )

    o_width = QHEADS * QDIM // blocks
    qkv = call(
        pack_kernel,
        out_shape=jax.ShapeDtypeStruct((blocks, rows, o_width + 2 * QDIM), BF16),
        name="pack",
        cost_estimate=work(3),
    )(queries[0], attn_keys[0], attn_values[0])
    raw, qkv = lax.optimization_barrier((raw, qkv))
    qkv = lax.all_to_all(qkv, "ctx", split_axis=0, concat_axis=0, tiled=True)
    rim = lax.ppermute(raw[rows - 8 :], "ctx", [(r, r + 1) for r in range(blocks - 1)])

    col, row, trail, keep, thr = call(
        prep_kernel,
        in_specs=[smem(), smem(), pl.BlockSpec(), pl.BlockSpec()],
        out_shape=[
            jax.ShapeDtypeStruct((GROUPS, rows, PER_GROUP), F32),
            jax.ShapeDtypeStruct((HEADS, rows), F32),
            jax.ShapeDtypeStruct((GROUPS, rows, 2 * PER_GROUP), BF16),
            jax.ShapeDtypeStruct((GROUPS, rows, 2 * PER_GROUP), BF16),
            jax.ShapeDtypeStruct((GROUPS, 8, PER_GROUP), BF16),
        ],
        name="prep",
        cost_estimate=work(3),
    )(place, doc_lengths, time_step[0], decay_rate[None])

    wide = lambda n: pl.BlockSpec((n, WIDTH), lambda g: (0, g))
    b_cols = lambda n: pl.BlockSpec((n, STATE), lambda g: (0, INNER // STATE + g))
    c_cols = lambda n: pl.BlockSpec((n, STATE), lambda g: (0, INNER // STATE + GROUPS + g))
    group_cols = lambda n: pl.BlockSpec((n, STATE), lambda g: (0, g))
    per_group = pl.BlockSpec((1, rows, PER_GROUP), lambda g: (g, 0, 0))
    per_group_two = pl.BlockSpec((1, rows, 2 * PER_GROUP), lambda g: (g, 0, 0))
    bias = conv_bias[None]
    half = WIDTH // 2
    x_act, b_act, c_act, fresh = call(
        front_kernel,
        grid=(GROUPS,),
        in_specs=[
            smem(), smem(),
            wide(rows), b_cols(rows), c_cols(rows),
            wide(8), b_cols(8), c_cols(8),
            wide(CONV), b_cols(CONV), c_cols(CONV),
            wide(1), b_cols(1), c_cols(1),
            per_group_two, pl.BlockSpec((1, 8, PER_GROUP), lambda g: (g, 0, 0)),
        ],
        out_specs=[
            wide(rows), group_cols(rows), group_cols(rows),
            pl.BlockSpec((2, STATE + EXTRA, half), lambda g: (g, 0, 0)),
        ],
        out_shape=[
            jax.ShapeDtypeStruct((rows, INNER), BF16),
            jax.ShapeDtypeStruct((rows, GROUPS * STATE), BF16),
            jax.ShapeDtypeStruct((rows, GROUPS * STATE), BF16),
            jax.ShapeDtypeStruct((2 * GROUPS, STATE + EXTRA, half), BF16),
        ],
        scratch_shapes=[pltpu.VMEM((8 + rows, 128), F32)],
        name="front",
        cost_estimate=work(40),
    )(
        place, doc_lengths, raw, raw, raw, rim, rim, rim,
        conv_weight, conv_weight, conv_weight, bias, bias, bias, trail, thr,
    )

    local = call(
        inner_kernel,
        grid=(GROUPS,),
        in_specs=[
            smem(), smem(), wide(rows), group_cols(rows), group_cols(rows), per_group,
            pl.BlockSpec((PER_GROUP, rows), lambda g: (g, 0)), wide(1),
        ],
        out_specs=wide(rows),
        out_shape=jax.ShapeDtypeStruct((rows, INNER), F32),
        name="inner",
        cost_estimate=work(9),
    )(place, doc_lengths, x_act, b_act, c_act, col, row, jnp.repeat(skip_gain, HEAD_DIM)[None])

    fresh, qkv, local = lax.optimization_barrier((fresh, qkv, local))
    own_fresh = lax.all_to_all(fresh, "ctx", split_axis=0, concat_axis=0, tiled=True)

    tall = o_width // QDIM * KEYS
    attended = call(
        attend_kernel,
        in_specs=[smem(), smem(), pl.BlockSpec()],
        out_shape=jax.ShapeDtypeStruct((blocks * rows, o_width), BF16),
        scratch_shapes=[
            pltpu.VMEM((blocks * rows // KEYS, tall, KEYS), F32),
            pltpu.VMEM((tall, 128), F32),
            pltpu.VMEM((tall, 128), F32),
            pltpu.VMEM((tall, QDIM), F32),
        ],
        name="attend",
        cost_estimate=work(30),
    )(place, doc_lengths, qkv.reshape(blocks * rows, o_width + 2 * QDIM))
    own_states = call(
        scan_kernel,
        out_shape=jax.ShapeDtypeStruct((blocks, STATE, half + o_width), BF16),
        name="scan",
        cost_estimate=work(4),
    )(own_fresh, attended.reshape(blocks, rows, o_width))
    states = lax.all_to_all(own_states, "ctx", split_axis=0, concat_axis=0, tiled=True)

    mixer_out, attn_out = call(
        final_kernel,
        grid=(GROUPS,),
        in_specs=[
            wide(rows), pl.BlockSpec((2, STATE, half + o_width), lambda g: (g, 0, 0)), group_cols(rows),
            per_group_two, wide(rows), wide(1),
        ],
        out_specs=[wide(rows), pl.BlockSpec((rows, 2 * o_width), lambda g: (0, g))],
        out_shape=[
            jax.ShapeDtypeStruct((rows, INNER), BF16),
            jax.ShapeDtypeStruct((rows, QHEADS * QDIM), BF16),
        ],
        name="final",
        cost_estimate=work(7),
    )(local, states, c_act, keep, z_gate[0], norm_gain[None])
    return (mixer_out[None], attn_out[None])


def solution(mesh):
    placed = P("batch", "ctx", None)
    whole = P()
    return jax.shard_map(
        on_device,
        mesh=mesh,
        in_specs=(placed, placed, placed) + (whole,) * 6 + (placed,) * 3,
        out_specs=(placed, placed),
        check_vma=False,
    )
```

```python
import functools

import jax
import jax.numpy as jnp
from jax import lax
from jax.experimental import pallas as pl
from jax.experimental.pallas import tpu as pltpu
from jax.sharding import PartitionSpec as P

HEADS = 128
HEAD_DIM = 64
STATE = 128
GROUPS = 8
QHEADS = 32
KVHEADS = 8
QDIM = 128
CONV = 4
WINDOW = 2048

PER_GROUP = HEADS // GROUPS
WIDTH = PER_GROUP * HEAD_DIM
INNER = HEADS * HEAD_DIM
DOCS = 6
EPSILON = 1e-05
NEGATIVE = -1e30
LOG2E = 1.4426950408889634
EXTRA = 8
KEYS = 256
PIECE = 32

F32 = jnp.float32
BF16 = jnp.bfloat16
HIGH = lax.Precision.HIGHEST


def dot(a, b, dims=(((1,), (0,)), ((), ())), precision=None):
    return lax.dot_general(a, b, dims, precision=precision, preferred_element_type=F32)


def doc_starts(place_ref, lengths_ref):
    seq = place_ref[1]
    starts = [jnp.int32(0)]
    for d in range(DOCS - 1):
        starts.append(starts[-1] + lengths_ref[seq, d])
    return starts


def row_starts(starts, pos):
    first = jnp.zeros_like(pos)
    for s in starts[1:]:
        first = jnp.where(pos >= s, s, first)
    return first


def scalar_start(starts, pos):
    first = jnp.int32(0)
    for s in starts[1:]:
        first = jnp.where(pos >= s, s, first)
    return first


def expand_heads(copies):
    shape = (copies * PER_GROUP, WIDTH)
    row = lax.broadcasted_iota(jnp.int32, shape, 0) % PER_GROUP
    lane = lax.broadcasted_iota(jnp.int32, shape, 1)
    return jnp.where(lane // HEAD_DIM == row, 1.0, 0.0).astype(BF16)


def halves(x):
    upper = x.astype(BF16)
    return upper, (x - upper.astype(F32)).astype(BF16)


def silu(x):
    return (0.5 * x) * (1.0 + jnp.tanh(0.5 * x))


def prep_kernel(place_ref, lengths_ref, step_ref, rate_ref, col_ref, row_ref, trail_ref, keep_ref, thr_ref):
    rows = step_ref.shape[0]
    base = place_ref[0] * rows
    starts = doc_starts(place_ref, lengths_ref)
    pos = base + lax.broadcasted_iota(jnp.int32, (rows, HEADS), 0)
    first = row_starts(starts, pos)
    last_first = scalar_start(starts, base + rows - 1)
    t = step_ref[...].astype(F32)
    dt = jnp.maximum(t, 0.0) + jnp.log1p(jnp.exp(-jnp.abs(t)))
    a = dt * rate_ref[...] * (-LOG2E)
    i = lax.broadcasted_iota(jnp.int32, (rows, rows), 0)
    j = lax.broadcasted_iota(jnp.int32, (rows, rows), 1)
    tri = (i >= j).astype(F32)
    cum = dot(tri, a, precision=HIGH)
    total = cum[rows - 1 : rows, :]
    trail = halves(jnp.where(first == last_first, jnp.exp2(total - cum) * dt, 0.0))
    keep = halves(jnp.where(first < base, jnp.exp2(cum), 0.0))
    thr = halves(jnp.where(last_first < base, jnp.exp2(total), 0.0))
    row8 = lax.broadcasted_iota(jnp.int32, (8, HEADS), 0)
    thr_rows = jnp.where(
        row8 == 0, thr[0].astype(F32), jnp.where(row8 == 1, thr[1].astype(F32), 0.0)
    ).astype(BF16)
    row_ref[...] = jnp.transpose(cum - jnp.log2(dt))
    for g in range(GROUPS):
        part = slice(g * PER_GROUP, (g + 1) * PER_GROUP)
        col_ref[g] = cum[:, part]
        trail_ref[g] = jnp.concatenate([trail[0][:, part], trail[1][:, part]], axis=1)
        keep_ref[g] = jnp.concatenate([keep[0][:, part], keep[1][:, part]], axis=1)
        thr_ref[g] = thr_rows[:, part]


def front_kernel(
    place_ref, lengths_ref, x_ref, b_ref, c_ref, hx_ref, hb_ref, hc_ref,
    wx_ref, wb_ref, wc_ref, ox_ref, ob_ref, oc_ref, trail_ref, thr_ref,
    xa_ref, ba_ref, ca_ref, f_ref, pad_ref,
):
    rows = x_ref.shape[0]
    base = place_ref[0] * rows
    starts = doc_starts(place_ref, lengths_ref)
    pos = base + lax.broadcasted_iota(jnp.int32, (rows, 128), 0)
    rel = pos - row_starts(starts, pos)
    masks = [None] + [rel >= d for d in range(1, CONV)]

    def conv(src, rim, weight, bias, dst, lo):
        at = slice(lo, lo + 128)
        pad_ref[0:8, :] = rim[:, at].astype(F32)
        pad_ref[8 : 8 + rows, :] = src[:, at].astype(F32)
        acc = pad_ref[8 : 8 + rows, :] * weight[3:4, at] + bias[:, at]
        for d in range(1, CONV):
            tap = pad_ref[8 - d : 8 - d + rows, :] * weight[3 - d : 4 - d, at]
            acc = acc + jnp.where(masks[d], tap, 0.0)
        dst[:, at] = silu(acc).astype(BF16)

    for lo in range(0, WIDTH, 128):
        conv(x_ref, hx_ref, wx_ref, ox_ref, xa_ref, lo)
    conv(b_ref, hb_ref, wb_ref, ob_ref, ba_ref, 0)
    conv(c_ref, hc_ref, wc_ref, oc_ref, ca_ref, 0)

    scale = dot(trail_ref[0], expand_heads(2))
    weighted = (xa_ref[...].astype(F32) * scale).astype(BF16)
    fresh = dot(ba_ref[...], weighted, (((0,), (0,)), ((), ()))).astype(BF16)
    extra = dot(thr_ref[0], expand_heads(1)).astype(BF16)
    half = WIDTH // 2
    for k in range(2):
        f_ref[k, 0:STATE, :] = fresh[:, k * half : (k + 1) * half]
        f_ref[k, STATE : STATE + EXTRA, :] = extra[:, k * half : (k + 1) * half]


def inner_kernel(place_ref, lengths_ref, xa_ref, ba_ref, ca_ref, col_ref, row_ref, skip_ref, y_ref):
    rows = xa_ref.shape[0]
    base = place_ref[0] * rows
    starts = doc_starts(place_ref, lengths_ref)
    i = base + lax.broadcasted_iota(jnp.int32, (rows, rows), 0)
    j = base + lax.broadcasted_iota(jnp.int32, (rows, rows), 1)
    first = row_starts(starts, i)
    blocked = jnp.where((j <= i) & (j >= first), 0.0, NEGATIVE)
    scores = dot(ca_ref[...], ba_ref[...], (((1,), (1,)), ((), ())))
    lane = lax.broadcasted_iota(jnp.int32, (rows, 128), 1)
    col = col_ref[0]
    for p in range(PER_GROUP // 2):
        weights = []
        for h in (2 * p, 2 * p + 1):
            spread = (col[:, h : h + 1] + blocked) - row_ref[h : h + 1, :]
            weights.append((scores * jnp.exp2(spread)).astype(BF16))
        at = slice(p * 128, (p + 1) * 128)
        x = xa_ref[:, at]
        zero = jnp.zeros_like(x)
        both = jnp.concatenate(
            [jnp.where(lane < HEAD_DIM, x, zero), jnp.where(lane < HEAD_DIM, zero, x)], axis=0
        )
        y = dot(jnp.concatenate(weights, axis=1), both)
        y_ref[:, at] = y + x.astype(F32) * skip_ref[:, at]


def scan_kernel(f_ref, o_ref, out_ref, tail_ref, held_ref, sems, tail_sem):
    blocks, _, width = f_ref.shape
    pieces, _, piece, _ = held_ref.shape

    def copy(q):
        at = pl.ds(q * piece, piece)
        return pltpu.make_async_copy(f_ref.at[:, at, :], held_ref.at[q], sems.at[q])

    tail = pltpu.make_async_copy(f_ref.at[:, pl.ds(STATE, EXTRA), :], tail_ref, tail_sem)

    @pl.when(pl.program_id(0) == 0)
    def _():
        tail.start()
        for q in range(pieces):
            copy(q).start()
        tail.wait()

    step = pl.program_id(0)
    copy(step).wait()
    out_ref[:, :, width:] = o_ref[...]
    state = jnp.zeros((piece, width), F32)
    for r in range(blocks):
        out_ref[r, :, :width] = state.astype(BF16)
        if r + 1 < blocks:
            ends = tail_ref[r].astype(F32)
            state = state * (ends[0:1, :] + ends[1:2, :]) + held_ref[step, r].astype(F32)


def final_kernel(y_ref, s_ref, ca_ref, keep_ref, z_ref, gain_ref, o_ref, attn_ref):
    scale = dot(keep_ref[0], expand_heads(2))
    half = WIDTH // 2
    parts = []
    for k in range(2):
        parts.append(dot(ca_ref[...], s_ref[k, :, :half]))
        own = s_ref.shape[2] - half
        attn_ref[:, k * own : (k + 1) * own] = s_ref[k, :, half:]
    carried = jnp.concatenate(parts, axis=1)
    mixed = (y_ref[...] + scale * carried).astype(BF16).astype(F32)
    gated = mixed * silu(z_ref[...].astype(F32))
    mean = jnp.mean(gated * gated, axis=1, keepdims=True)
    o_ref[...] = (gated * lax.rsqrt(mean + EPSILON) * gain_ref[...]).astype(BF16)


def pack_kernel(q_ref, k_ref, v_ref, out_ref):
    parts = out_ref.shape[0]
    width = q_ref.shape[1] // parts
    for d in range(parts):
        at = d * KVHEADS // parts * QDIM
        out_ref[d, :, :width] = q_ref[:, d * width : (d + 1) * width]
        out_ref[d, :, width : width + QDIM] = k_ref[:, at : at + QDIM]
        out_ref[d, :, width + QDIM :] = v_ref[:, at : at + QDIM]


def attend_kernel(place_ref, lengths_ref, far_ref, o_ref, qkv_ref, sem, s_ref, m_ref, l_ref, acc_ref):
    copy = pltpu.make_async_copy(far_ref, qkv_ref, sem)
    copy.start()
    copy.wait()
    length = qkv_ref.shape[0]
    q_width = qkv_ref.shape[1] - 2 * QDIM
    heads = q_width // QDIM
    k_cols, v_cols = slice(q_width, q_width + QDIM), slice(q_width + QDIM, q_width + 2 * QDIM)
    starts = doc_starts(place_ref, lengths_ref)
    lane = lax.broadcasted_iota(jnp.int32, (KEYS, KEYS), 1)
    scaling = QDIM ** (-0.5) * LOG2E

    def one_tile(t, outer):
        base = t * KEYS
        here = pl.ds(pl.multiple_of(base, KEYS), KEYS)
        pos = base + lax.broadcasted_iota(jnp.int32, (KEYS, KEYS), 0)
        first = jnp.maximum(row_starts(starts, pos), pos - (WINDOW - 1))
        last = base + KEYS - 1
        lowest = jnp.maximum(scalar_start(starts, base), base - (WINDOW - 1))
        highest = jnp.maximum(scalar_start(starts, last), last - (WINDOW - 1))
        begin = lowest // KEYS
        clear = jnp.minimum((highest + KEYS - 1) // KEYS, t)
        queries = jnp.concatenate([qkv_ref[here, h * QDIM : (h + 1) * QDIM] for h in range(heads)], axis=0)
        m_ref[...] = jnp.full_like(m_ref, NEGATIVE)

        def score(masked, j, carry):
            k = qkv_ref[pl.ds(pl.multiple_of(j * KEYS, KEYS), KEYS), k_cols]
            s = dot(queries, k, (((1,), (1,)), ((), ())))
            if masked:
                key = j * KEYS + lane
                visible = (key <= pos) & (key >= first)
            for h in range(heads):
                at = slice(h * KEYS, (h + 1) * KEYS)
                part = s[at]
                if masked:
                    part = jnp.where(visible, part, NEGATIVE)
                s_ref[j, at, :] = part
                top = m_ref[at, :]
                for c in range(0, KEYS, 128):
                    top = jnp.maximum(top, part[:, c : c + 128])
                m_ref[at, :] = top
            return carry

        lax.fori_loop(begin, clear, functools.partial(score, True), 0)
        lax.fori_loop(clear, t, functools.partial(score, False), 0)
        score(True, t, 0)
        m_ref[...] = jnp.broadcast_to(jnp.max(m_ref[...], axis=1, keepdims=True), m_ref.shape)
        l_ref[...] = jnp.zeros_like(l_ref)
        acc_ref[...] = jnp.zeros_like(acc_ref)

        def gather(j, carry):
            v = qkv_ref[pl.ds(pl.multiple_of(j * KEYS, KEYS), KEYS), v_cols]
            numerators = []
            for h in range(heads):
                at = slice(h * KEYS, (h + 1) * KEYS)
                top = m_ref[at, :]
                total = l_ref[at, :]
                parts = []
                for c in range(0, KEYS, 128):
                    p = jnp.exp2((s_ref[j, at, c : c + 128] - top) * scaling)
                    total = total + p
                    parts.append(p.astype(BF16))
                l_ref[at, :] = total
                numerators.append(jnp.concatenate(parts, axis=1))
            acc_ref[...] += dot(jnp.concatenate(numerators, axis=0), v)
            return carry

        lax.fori_loop(begin, t + 1, gather, 0)
        for h in range(heads):
            at = slice(h * KEYS, (h + 1) * KEYS)
            total = jnp.sum(l_ref[at, :], axis=1, keepdims=True)
            o_ref[here, h * QDIM : (h + 1) * QDIM] = (acc_ref[at, :] / total).astype(BF16)
        return outer

    lax.fori_loop(0, length // KEYS, one_tile, 0)


def work(microseconds):
    return pl.CostEstimate(flops=0, transcendentals=0, bytes_accessed=int(microseconds * 3.5e6))


def smem():
    return pl.BlockSpec(memory_space=pltpu.SMEM)


def on_device(
    mixer_input, z_gate, time_step, conv_weight, conv_bias, decay_rate, skip_gain,
    norm_gain, doc_lengths, queries, attn_keys, attn_values,
):
    rows = mixer_input.shape[1]
    blocks = lax.axis_size("ctx")
    place = jnp.stack([lax.axis_index("ctx"), lax.axis_index("batch")]).astype(jnp.int32)
    raw = mixer_input[0]
    call = functools.partial(
        pl.pallas_call, compiler_params=pltpu.CompilerParams(vmem_limit_bytes=63 << 20)
    )

    o_width = QHEADS * QDIM // blocks
    qkv = call(
        pack_kernel,
        out_shape=jax.ShapeDtypeStruct((blocks, rows, o_width + 2 * QDIM), BF16),
        name="pack",
        cost_estimate=work(3),
    )(queries[0], attn_keys[0], attn_values[0])
    rim = lax.ppermute(raw[rows - 8 :], "ctx", [(r, r + 1) for r in range(blocks - 1)])
    rim, qkv = lax.optimization_barrier((rim, qkv))
    qkv = lax.all_to_all(qkv, "ctx", split_axis=0, concat_axis=0, tiled=True)

    col, row, trail, keep, thr = call(
        prep_kernel,
        in_specs=[smem(), smem(), pl.BlockSpec(), pl.BlockSpec()],
        out_shape=[
            jax.ShapeDtypeStruct((GROUPS, rows, PER_GROUP), F32),
            jax.ShapeDtypeStruct((HEADS, rows), F32),
            jax.ShapeDtypeStruct((GROUPS, rows, 2 * PER_GROUP), BF16),
            jax.ShapeDtypeStruct((GROUPS, rows, 2 * PER_GROUP), BF16),
            jax.ShapeDtypeStruct((GROUPS, 8, PER_GROUP), BF16),
        ],
        name="prep",
        cost_estimate=work(3),
    )(place, doc_lengths, time_step[0], decay_rate[None])

    wide = lambda n: pl.BlockSpec((n, WIDTH), lambda g: (0, g))
    b_cols = lambda n: pl.BlockSpec((n, STATE), lambda g: (0, INNER // STATE + g))
    c_cols = lambda n: pl.BlockSpec((n, STATE), lambda g: (0, INNER // STATE + GROUPS + g))
    group_cols = lambda n: pl.BlockSpec((n, STATE), lambda g: (0, g))
    per_group = pl.BlockSpec((1, rows, PER_GROUP), lambda g: (g, 0, 0))
    per_group_two = pl.BlockSpec((1, rows, 2 * PER_GROUP), lambda g: (g, 0, 0))
    bias = conv_bias[None]
    half = WIDTH // 2
    x_act, b_act, c_act, fresh = call(
        front_kernel,
        grid=(GROUPS,),
        in_specs=[
            smem(), smem(),
            wide(rows), b_cols(rows), c_cols(rows),
            wide(8), b_cols(8), c_cols(8),
            wide(CONV), b_cols(CONV), c_cols(CONV),
            wide(1), b_cols(1), c_cols(1),
            per_group_two, pl.BlockSpec((1, 8, PER_GROUP), lambda g: (g, 0, 0)),
        ],
        out_specs=[
            wide(rows), group_cols(rows), group_cols(rows),
            pl.BlockSpec((2, STATE + EXTRA, half), lambda g: (g, 0, 0)),
        ],
        out_shape=[
            jax.ShapeDtypeStruct((rows, INNER), BF16),
            jax.ShapeDtypeStruct((rows, GROUPS * STATE), BF16),
            jax.ShapeDtypeStruct((rows, GROUPS * STATE), BF16),
            jax.ShapeDtypeStruct((2 * GROUPS, STATE + EXTRA, half), BF16),
        ],
        scratch_shapes=[pltpu.VMEM((8 + rows, 128), F32)],
        name="front",
        cost_estimate=work(40),
    )(
        place, doc_lengths, raw, raw, raw, rim, rim, rim,
        conv_weight, conv_weight, conv_weight, bias, bias, bias, trail, thr,
    )

    local = call(
        inner_kernel,
        grid=(GROUPS,),
        in_specs=[
            smem(), smem(), wide(rows), group_cols(rows), group_cols(rows), per_group,
            pl.BlockSpec((PER_GROUP, rows), lambda g: (g, 0)), wide(1),
        ],
        out_specs=wide(rows),
        out_shape=jax.ShapeDtypeStruct((rows, INNER), F32),
        name="inner",
        cost_estimate=work(9),
    )(place, doc_lengths, x_act, b_act, c_act, col, row, jnp.repeat(skip_gain, HEAD_DIM)[None])

    fresh, qkv, local = lax.optimization_barrier((fresh, qkv, local))
    own_fresh = lax.all_to_all(fresh, "ctx", split_axis=0, concat_axis=0, tiled=True)

    tall = o_width // QDIM * KEYS
    attended = call(
        attend_kernel,
        in_specs=[smem(), smem(), pl.BlockSpec(memory_space=pl.ANY)],
        out_shape=jax.ShapeDtypeStruct((blocks * rows, o_width), BF16),
        scratch_shapes=[
            pltpu.VMEM((blocks * rows, o_width + 2 * QDIM), BF16),
            pltpu.SemaphoreType.DMA,
            pltpu.VMEM((blocks * rows // KEYS, tall, KEYS), F32),
            pltpu.VMEM((tall, 128), F32),
            pltpu.VMEM((tall, 128), F32),
            pltpu.VMEM((tall, QDIM), F32),
        ],
        name="attend",
        cost_estimate=work(30),
    )(place, doc_lengths, qkv.reshape(blocks * rows, o_width + 2 * QDIM))
    own_states = call(
        scan_kernel,
        grid=(STATE // PIECE,),
        in_specs=[
            pl.BlockSpec(memory_space=pl.ANY),
            pl.BlockSpec((blocks, PIECE, o_width), lambda q: (0, q, 0)),
        ],
        out_specs=pl.BlockSpec((blocks, PIECE, half + o_width), lambda q: (0, q, 0)),
        out_shape=jax.ShapeDtypeStruct((blocks, STATE, half + o_width), BF16),
        scratch_shapes=[
            pltpu.VMEM((blocks, EXTRA, half), BF16),
            pltpu.VMEM((STATE // PIECE, blocks, PIECE, half), BF16),
            pltpu.SemaphoreType.DMA((STATE // PIECE,)),
            pltpu.SemaphoreType.DMA,
        ],
        name="scan",
        cost_estimate=work(4),
    )(own_fresh, attended.reshape(blocks, rows, o_width))
    states = lax.all_to_all(own_states, "ctx", split_axis=0, concat_axis=0, tiled=True)

    mixer_out, attn_out = call(
        final_kernel,
        grid=(GROUPS,),
        in_specs=[
            wide(rows), pl.BlockSpec((2, STATE, half + o_width), lambda g: (g, 0, 0)), group_cols(rows),
            per_group_two, wide(rows), wide(1),
        ],
        out_specs=[wide(rows), pl.BlockSpec((rows, 2 * o_width), lambda g: (0, g))],
        out_shape=[
            jax.ShapeDtypeStruct((rows, INNER), BF16),
            jax.ShapeDtypeStruct((rows, QHEADS * QDIM), BF16),
        ],
        name="final",
        cost_estimate=work(7),
    )(local, states, c_act, keep, z_gate[0], norm_gain[None])
    return (mixer_out[None], attn_out[None])


def solution(mesh):
    placed = P("batch", "ctx", None)
    whole = P()
    return jax.shard_map(
        on_device,
        mesh=mesh,
        in_specs=(placed, placed, placed) + (whole,) * 6 + (placed,) * 3,
        out_specs=(placed, placed),
        check_vma=False,
    )
```

```python
import functools

import jax
import jax.numpy as jnp
from jax import lax
from jax.experimental import pallas as pl
from jax.experimental.pallas import tpu as pltpu
from jax.sharding import PartitionSpec as P

HEADS = 128
HEAD_DIM = 64
STATE = 128
GROUPS = 8
QHEADS = 32
KVHEADS = 8
QDIM = 128
CONV = 4
WINDOW = 2048

PER_GROUP = HEADS // GROUPS
WIDTH = PER_GROUP * HEAD_DIM
INNER = HEADS * HEAD_DIM
DOCS = 6
EPSILON = 1e-05
NEGATIVE = -1e30
LOG2E = 1.4426950408889634
EXTRA = 8
KEYS = 256
PIECE = 32
CHUNK = 16

F32 = jnp.float32
BF16 = jnp.bfloat16
HIGH = lax.Precision.HIGHEST


def dot(a, b, dims=(((1,), (0,)), ((), ())), precision=None):
    return lax.dot_general(a, b, dims, precision=precision, preferred_element_type=F32)


def doc_starts(place_ref, lengths_ref):
    seq = place_ref[1]
    starts = [jnp.int32(0)]
    for d in range(DOCS - 1):
        starts.append(starts[-1] + lengths_ref[seq, d])
    return starts


def row_starts(starts, pos):
    first = jnp.zeros_like(pos)
    for s in starts[1:]:
        first = jnp.where(pos >= s, s, first)
    return first


def scalar_start(starts, pos):
    first = jnp.int32(0)
    for s in starts[1:]:
        first = jnp.where(pos >= s, s, first)
    return first


def expand_heads(copies):
    shape = (copies * PER_GROUP, WIDTH)
    row = lax.broadcasted_iota(jnp.int32, shape, 0) % PER_GROUP
    lane = lax.broadcasted_iota(jnp.int32, shape, 1)
    return jnp.where(lane // HEAD_DIM == row, 1.0, 0.0).astype(BF16)


def halves(x):
    upper = x.astype(BF16)
    return upper, (x - upper.astype(F32)).astype(BF16)


def silu(x):
    return (0.5 * x) * (1.0 + jnp.tanh(0.5 * x))


def prep_kernel(place_ref, lengths_ref, step_ref, rate_ref, col_ref, row_ref, trail_ref, keep_ref, thr_ref):
    rows = step_ref.shape[0]
    base = place_ref[0] * rows
    starts = doc_starts(place_ref, lengths_ref)
    pos = base + lax.broadcasted_iota(jnp.int32, (rows, HEADS), 0)
    first = row_starts(starts, pos)
    last_first = scalar_start(starts, base + rows - 1)
    t = step_ref[...].astype(F32)
    dt = jnp.maximum(t, 0.0) + jnp.log1p(jnp.exp(-jnp.abs(t)))
    a = dt * rate_ref[...] * (-LOG2E)
    i = lax.broadcasted_iota(jnp.int32, (rows, rows), 0)
    j = lax.broadcasted_iota(jnp.int32, (rows, rows), 1)
    tri = (i >= j).astype(F32)
    cum = dot(tri, a, precision=HIGH)
    total = cum[rows - 1 : rows, :]
    trail = halves(jnp.where(first == last_first, jnp.exp2(total - cum) * dt, 0.0))
    keep = halves(jnp.where(first < base, jnp.exp2(cum), 0.0))
    thr = halves(jnp.where(last_first < base, jnp.exp2(total), 0.0))
    row8 = lax.broadcasted_iota(jnp.int32, (8, HEADS), 0)
    thr_rows = jnp.where(
        row8 == 0, thr[0].astype(F32), jnp.where(row8 == 1, thr[1].astype(F32), 0.0)
    ).astype(BF16)
    row_ref[...] = jnp.transpose(cum - jnp.log2(dt))
    for g in range(GROUPS):
        part = slice(g * PER_GROUP, (g + 1) * PER_GROUP)
        col_ref[g] = cum[:, part]
        trail_ref[g] = jnp.concatenate([trail[0][:, part], trail[1][:, part]], axis=1)
        keep_ref[g] = jnp.concatenate([keep[0][:, part], keep[1][:, part]], axis=1)
        thr_ref[g] = thr_rows[:, part]


def front_kernel(
    place_ref, lengths_ref, x_ref, b_ref, c_ref, hx_ref, hb_ref, hc_ref,
    wx_ref, wb_ref, wc_ref, ox_ref, ob_ref, oc_ref, trail_ref, thr_ref,
    xa_ref, ba_ref, ca_ref, f_ref, pad_ref,
):
    rows = x_ref.shape[0]
    base = place_ref[0] * rows
    starts = doc_starts(place_ref, lengths_ref)
    pos = base + lax.broadcasted_iota(jnp.int32, (rows, 128), 0)
    rel = pos - row_starts(starts, pos)
    masks = [None] + [rel >= d for d in range(1, CONV)]

    def conv(src, rim, weight, bias, dst, lo):
        at = slice(lo, lo + 128)
        pad_ref[0:8, :] = rim[:, at].astype(F32)
        pad_ref[8 : 8 + rows, :] = src[:, at].astype(F32)
        acc = pad_ref[8 : 8 + rows, :] * weight[3:4, at] + bias[:, at]
        for d in range(1, CONV):
            tap = pad_ref[8 - d : 8 - d + rows, :] * weight[3 - d : 4 - d, at]
            acc = acc + jnp.where(masks[d], tap, 0.0)
        dst[:, at] = silu(acc).astype(BF16)

    for lo in range(0, WIDTH, 128):
        conv(x_ref, hx_ref, wx_ref, ox_ref, xa_ref, lo)
    conv(b_ref, hb_ref, wb_ref, ob_ref, ba_ref, 0)
    conv(c_ref, hc_ref, wc_ref, oc_ref, ca_ref, 0)

    scale = dot(trail_ref[0], expand_heads(2))
    weighted = (xa_ref[...].astype(F32) * scale).astype(BF16)
    fresh = dot(ba_ref[...], weighted, (((0,), (0,)), ((), ()))).astype(BF16)
    extra = dot(thr_ref[0], expand_heads(1)).astype(BF16)
    half = WIDTH // 2
    for k in range(2):
        f_ref[k, 0:STATE, :] = fresh[:, k * half : (k + 1) * half]
        f_ref[k, STATE : STATE + EXTRA, :] = extra[:, k * half : (k + 1) * half]


def inner_kernel(place_ref, lengths_ref, xa_ref, ba_ref, ca_ref, col_ref, row_ref, skip_ref, y_ref):
    rows = xa_ref.shape[0]
    base = place_ref[0] * rows
    starts = doc_starts(place_ref, lengths_ref)
    i = base + lax.broadcasted_iota(jnp.int32, (rows, rows), 0)
    j = base + lax.broadcasted_iota(jnp.int32, (rows, rows), 1)
    first = row_starts(starts, i)
    blocked = jnp.where((j <= i) & (j >= first), 0.0, NEGATIVE)
    scores = dot(ca_ref[...], ba_ref[...], (((1,), (1,)), ((), ())))
    lane = lax.broadcasted_iota(jnp.int32, (rows, 128), 1)
    col = col_ref[0]
    for p in range(PER_GROUP // 2):
        weights = []
        for h in (2 * p, 2 * p + 1):
            spread = (col[:, h : h + 1] + blocked) - row_ref[h : h + 1, :]
            weights.append((scores * jnp.exp2(spread)).astype(BF16))
        at = slice(p * 128, (p + 1) * 128)
        x = xa_ref[:, at]
        zero = jnp.zeros_like(x)
        both = jnp.concatenate(
            [jnp.where(lane < HEAD_DIM, x, zero), jnp.where(lane < HEAD_DIM, zero, x)], axis=0
        )
        y = dot(jnp.concatenate(weights, axis=1), both)
        y_ref[:, at] = y + x.astype(F32) * skip_ref[:, at]


def scan_kernel(f_ref, held_out_ref, out_ref, tail_ref, held_ref, state_ref, sems, out_sems, tail_sem):
    blocks, _, width = f_ref.shape
    pieces, _, piece, _ = held_ref.shape
    tail = pltpu.make_async_copy(f_ref.at[:, pl.ds(STATE, EXTRA), :], tail_ref, tail_sem)
    loads = [
        pltpu.make_async_copy(f_ref.at[:, pl.ds(q * piece, piece), :], held_ref.at[q], sems.at[q])
        for q in range(pieces)
    ]
    stores = [
        pltpu.make_async_copy(
            state_ref.at[q], out_ref.at[:, pl.ds(q * piece, piece), pl.ds(0, width)], out_sems.at[q]
        )
        for q in range(pieces)
    ]
    tail.start()
    for load in loads:
        load.start()
    tail.wait()
    for q in range(pieces):
        loads[q].wait()
        state = jnp.zeros((piece, width), F32)
        for r in range(blocks):
            state_ref[q, r] = state.astype(BF16)
            if r + 1 < blocks:
                ends = tail_ref[r].astype(F32)
                state = state * (ends[0:1, :] + ends[1:2, :]) + held_ref[q, r].astype(F32)
        stores[q].start()
    for store in stores:
        store.wait()


def final_kernel(y_ref, s_ref, ca_ref, keep_ref, z_ref, gain_ref, o_ref, attn_ref, scale_ref, carried_ref):
    half = WIDTH // 2
    scale_ref[...] = dot(keep_ref[0], expand_heads(2))
    for k in range(2):
        carried_ref[:, k * half : (k + 1) * half] = dot(ca_ref[...], s_ref[k, :, :half])
        own = s_ref.shape[2] - half
        attn_ref[:, k * own : (k + 1) * own] = s_ref[k, :, half:]
    gain = gain_ref[...]
    for lo in range(0, y_ref.shape[0], CHUNK):
        at = slice(lo, lo + CHUNK)
        mixed = (y_ref[at, :] + scale_ref[at, :] * carried_ref[at, :]).astype(BF16).astype(F32)
        gated = mixed * silu(z_ref[at, :].astype(F32))
        mean = jnp.mean(gated * gated, axis=1, keepdims=True)
        o_ref[at, :] = (gated * lax.rsqrt(mean + EPSILON) * gain).astype(BF16)


def pack_kernel(q_ref, k_ref, v_ref, out_ref):
    parts = out_ref.shape[0]
    width = q_ref.shape[1] // parts
    for d in range(parts):
        at = d * KVHEADS // parts * QDIM
        out_ref[d, :, :width] = q_ref[:, d * width : (d + 1) * width]
        out_ref[d, :, width : width + QDIM] = k_ref[:, at : at + QDIM]
        out_ref[d, :, width + QDIM :] = v_ref[:, at : at + QDIM]


def attend_kernel(place_ref, lengths_ref, far_ref, out_ref, qkv_ref, o_ref, sems, s_ref, m_ref, l_ref, acc_ref):
    copy = pltpu.make_async_copy(far_ref, qkv_ref, sems.at[0])
    copy.start()
    copy.wait()
    length = qkv_ref.shape[0]
    q_width = qkv_ref.shape[1] - 2 * QDIM
    heads = q_width // QDIM
    k_cols, v_cols = slice(q_width, q_width + QDIM), slice(q_width + QDIM, q_width + 2 * QDIM)
    starts = doc_starts(place_ref, lengths_ref)
    lane = lax.broadcasted_iota(jnp.int32, (KEYS, KEYS), 1)
    scaling = QDIM ** (-0.5) * LOG2E

    def one_tile(t, outer):
        base = t * KEYS
        here = pl.ds(pl.multiple_of(base, KEYS), KEYS)
        pos = base + lax.broadcasted_iota(jnp.int32, (KEYS, KEYS), 0)
        first = jnp.maximum(row_starts(starts, pos), pos - (WINDOW - 1))
        last = base + KEYS - 1
        lowest = jnp.maximum(scalar_start(starts, base), base - (WINDOW - 1))
        highest = jnp.maximum(scalar_start(starts, last), last - (WINDOW - 1))
        begin = lowest // KEYS
        clear = jnp.minimum((highest + KEYS - 1) // KEYS, t)
        queries = jnp.concatenate([qkv_ref[here, h * QDIM : (h + 1) * QDIM] for h in range(heads)], axis=0)
        m_ref[...] = jnp.full_like(m_ref, NEGATIVE)

        def score(masked, j, carry):
            k = qkv_ref[pl.ds(pl.multiple_of(j * KEYS, KEYS), KEYS), k_cols]
            s = dot(queries, k, (((1,), (1,)), ((), ())))
            if masked:
                key = j * KEYS + lane
                visible = (key <= pos) & (key >= first)
            for h in range(heads):
                at = slice(h * KEYS, (h + 1) * KEYS)
                part = s[at]
                if masked:
                    part = jnp.where(visible, part, NEGATIVE)
                s_ref[j, at, :] = part
                top = m_ref[at, :]
                for c in range(0, KEYS, 128):
                    top = jnp.maximum(top, part[:, c : c + 128])
                m_ref[at, :] = top
            return carry

        lax.fori_loop(begin, clear, functools.partial(score, True), 0)
        lax.fori_loop(clear, t, functools.partial(score, False), 0)
        score(True, t, 0)
        m_ref[...] = jnp.broadcast_to(jnp.max(m_ref[...], axis=1, keepdims=True), m_ref.shape)
        l_ref[...] = jnp.zeros_like(l_ref)
        acc_ref[...] = jnp.zeros_like(acc_ref)

        def gather(j, carry):
            v = qkv_ref[pl.ds(pl.multiple_of(j * KEYS, KEYS), KEYS), v_cols]
            numerators = []
            for h in range(heads):
                at = slice(h * KEYS, (h + 1) * KEYS)
                top = m_ref[at, :]
                total = l_ref[at, :]
                parts = []
                for c in range(0, KEYS, 128):
                    p = jnp.exp2((s_ref[j, at, c : c + 128] - top) * scaling)
                    total = total + p
                    parts.append(p.astype(BF16))
                l_ref[at, :] = total
                numerators.append(jnp.concatenate(parts, axis=1))
            acc_ref[...] += dot(jnp.concatenate(numerators, axis=0), v)
            return carry

        lax.fori_loop(begin, t + 1, gather, 0)
        for h in range(heads):
            at = slice(h * KEYS, (h + 1) * KEYS)
            total = jnp.sum(l_ref[at, :], axis=1, keepdims=True)
            o_ref[here, h * QDIM : (h + 1) * QDIM] = (acc_ref[at, :] / total).astype(BF16)
        return outer

    lax.fori_loop(0, length // KEYS, one_tile, 0)
    blocks, rows, out_width = out_ref.shape
    sends = [
        pltpu.make_async_copy(
            o_ref.at[pl.ds(r * rows, rows), :],
            out_ref.at[r, :, pl.ds(out_width - q_width, q_width)],
            sems.at[1 + r],
        )
        for r in range(blocks)
    ]
    for send in sends:
        send.start()
    for send in sends:
        send.wait()


def work(microseconds):
    return pl.CostEstimate(flops=0, transcendentals=0, bytes_accessed=int(microseconds * 3.5e6))


def smem():
    return pl.BlockSpec(memory_space=pltpu.SMEM)


def on_device(
    mixer_input, z_gate, time_step, conv_weight, conv_bias, decay_rate, skip_gain,
    norm_gain, doc_lengths, queries, attn_keys, attn_values,
):
    rows = mixer_input.shape[1]
    blocks = lax.axis_size("ctx")
    place = jnp.stack([lax.axis_index("ctx"), lax.axis_index("batch")]).astype(jnp.int32)
    raw = mixer_input[0]
    call = functools.partial(
        pl.pallas_call, compiler_params=pltpu.CompilerParams(vmem_limit_bytes=63 << 20)
    )

    o_width = QHEADS * QDIM // blocks
    qkv = call(
        pack_kernel,
        out_shape=jax.ShapeDtypeStruct((blocks, rows, o_width + 2 * QDIM), BF16),
        name="pack",
        cost_estimate=work(3),
    )(queries[0], attn_keys[0], attn_values[0])
    rim = lax.ppermute(raw[rows - 8 :], "ctx", [(r, r + 1) for r in range(blocks - 1)])
    rim, qkv = lax.optimization_barrier((rim, qkv))
    qkv = lax.all_to_all(qkv, "ctx", split_axis=0, concat_axis=0, tiled=True)

    col, row, trail, keep, thr = call(
        prep_kernel,
        in_specs=[smem(), smem(), pl.BlockSpec(), pl.BlockSpec()],
        out_shape=[
            jax.ShapeDtypeStruct((GROUPS, rows, PER_GROUP), F32),
            jax.ShapeDtypeStruct((HEADS, rows), F32),
            jax.ShapeDtypeStruct((GROUPS, rows, 2 * PER_GROUP), BF16),
            jax.ShapeDtypeStruct((GROUPS, rows, 2 * PER_GROUP), BF16),
            jax.ShapeDtypeStruct((GROUPS, 8, PER_GROUP), BF16),
        ],
        name="prep",
        cost_estimate=work(3),
    )(place, doc_lengths, time_step[0], decay_rate[None])

    wide = lambda n: pl.BlockSpec((n, WIDTH), lambda g: (0, g))
    b_cols = lambda n: pl.BlockSpec((n, STATE), lambda g: (0, INNER // STATE + g))
    c_cols = lambda n: pl.BlockSpec((n, STATE), lambda g: (0, INNER // STATE + GROUPS + g))
    group_cols = lambda n: pl.BlockSpec((n, STATE), lambda g: (0, g))
    per_group = pl.BlockSpec((1, rows, PER_GROUP), lambda g: (g, 0, 0))
    per_group_two = pl.BlockSpec((1, rows, 2 * PER_GROUP), lambda g: (g, 0, 0))
    bias = conv_bias[None]
    half = WIDTH // 2
    x_act, b_act, c_act, fresh = call(
        front_kernel,
        grid=(GROUPS,),
        in_specs=[
            smem(), smem(),
            wide(rows), b_cols(rows), c_cols(rows),
            wide(8), b_cols(8), c_cols(8),
            wide(CONV), b_cols(CONV), c_cols(CONV),
            wide(1), b_cols(1), c_cols(1),
            per_group_two, pl.BlockSpec((1, 8, PER_GROUP), lambda g: (g, 0, 0)),
        ],
        out_specs=[
            wide(rows), group_cols(rows), group_cols(rows),
            pl.BlockSpec((2, STATE + EXTRA, half), lambda g: (g, 0, 0)),
        ],
        out_shape=[
            jax.ShapeDtypeStruct((rows, INNER), BF16),
            jax.ShapeDtypeStruct((rows, GROUPS * STATE), BF16),
            jax.ShapeDtypeStruct((rows, GROUPS * STATE), BF16),
            jax.ShapeDtypeStruct((2 * GROUPS, STATE + EXTRA, half), BF16),
        ],
        scratch_shapes=[pltpu.VMEM((8 + rows, 128), F32)],
        name="front",
        cost_estimate=work(40),
    )(
        place, doc_lengths, raw, raw, raw, rim, rim, rim,
        conv_weight, conv_weight, conv_weight, bias, bias, bias, trail, thr,
    )

    local = call(
        inner_kernel,
        grid=(GROUPS,),
        in_specs=[
            smem(), smem(), wide(rows), group_cols(rows), group_cols(rows), per_group,
            pl.BlockSpec((PER_GROUP, rows), lambda g: (g, 0)), wide(1),
        ],
        out_specs=wide(rows),
        out_shape=jax.ShapeDtypeStruct((rows, INNER), F32),
        name="inner",
        cost_estimate=work(9),
    )(place, doc_lengths, x_act, b_act, c_act, col, row, jnp.repeat(skip_gain, HEAD_DIM)[None])

    fresh, qkv, local = lax.optimization_barrier((fresh, qkv, local))
    own_fresh = lax.all_to_all(fresh, "ctx", split_axis=0, concat_axis=0, tiled=True)

    tall = o_width // QDIM * KEYS
    attended = call(
        attend_kernel,
        in_specs=[smem(), smem(), pl.BlockSpec(memory_space=pl.ANY)],
        out_specs=pl.BlockSpec(memory_space=pl.ANY),
        out_shape=jax.ShapeDtypeStruct((blocks, rows, half + o_width), BF16),
        scratch_shapes=[
            pltpu.VMEM((blocks * rows, o_width + 2 * QDIM), BF16),
            pltpu.VMEM((blocks * rows, o_width), BF16),
            pltpu.SemaphoreType.DMA((1 + blocks,)),
            pltpu.VMEM((blocks * rows // KEYS, tall, KEYS), F32),
            pltpu.VMEM((tall, 128), F32),
            pltpu.VMEM((tall, 128), F32),
            pltpu.VMEM((tall, QDIM), F32),
        ],
        name="attend",
        cost_estimate=work(30),
    )(place, doc_lengths, qkv.reshape(blocks * rows, o_width + 2 * QDIM))
    own_states = call(
        scan_kernel,
        in_specs=[pl.BlockSpec(memory_space=pl.ANY)] * 2,
        out_specs=pl.BlockSpec(memory_space=pl.ANY),
        out_shape=jax.ShapeDtypeStruct((blocks, STATE, half + o_width), BF16),
        input_output_aliases={1: 0},
        scratch_shapes=[
            pltpu.VMEM((blocks, EXTRA, half), BF16),
            pltpu.VMEM((STATE // PIECE, blocks, PIECE, half), BF16),
            pltpu.VMEM((STATE // PIECE, blocks, PIECE, half), BF16),
            pltpu.SemaphoreType.DMA((STATE // PIECE,)),
            pltpu.SemaphoreType.DMA((STATE // PIECE,)),
            pltpu.SemaphoreType.DMA,
        ],
        name="scan",
        cost_estimate=work(4),
    )(own_fresh, attended)
    states = lax.all_to_all(own_states, "ctx", split_axis=0, concat_axis=0, tiled=True)

    mixer_out, attn_out = call(
        final_kernel,
        grid=(GROUPS,),
        in_specs=[
            wide(rows), pl.BlockSpec((2, STATE, half + o_width), lambda g: (g, 0, 0)), group_cols(rows),
            per_group_two, wide(rows), wide(1),
        ],
        out_specs=[wide(rows), pl.BlockSpec((rows, 2 * o_width), lambda g: (0, g))],
        out_shape=[
            jax.ShapeDtypeStruct((rows, INNER), BF16),
            jax.ShapeDtypeStruct((rows, QHEADS * QDIM), BF16),
        ],
        scratch_shapes=[pltpu.VMEM((rows, WIDTH), F32), pltpu.VMEM((rows, WIDTH), F32)],
        name="final",
        cost_estimate=work(7),
    )(local, states, c_act, keep, z_gate[0], norm_gain[None])
    return (mixer_out[None], attn_out[None])


def solution(mesh):
    placed = P("batch", "ctx", None)
    whole = P()
    return jax.shard_map(
        on_device,
        mesh=mesh,
        in_specs=(placed, placed, placed) + (whole,) * 6 + (placed,) * 3,
        out_specs=(placed, placed),
        check_vma=False,
    )
```

```python
import functools

import jax
import jax.numpy as jnp
from jax import lax
from jax.experimental import pallas as pl
from jax.experimental.pallas import tpu as pltpu
from jax.sharding import PartitionSpec as P

HEADS = 128
HEAD_DIM = 64
STATE = 128
GROUPS = 8
QHEADS = 32
KVHEADS = 8
QDIM = 128
CONV = 4
WINDOW = 2048

PER_GROUP = HEADS // GROUPS
WIDTH = PER_GROUP * HEAD_DIM
INNER = HEADS * HEAD_DIM
DOCS = 6
EPSILON = 1e-05
NEGATIVE = -1e30
LOG2E = 1.4426950408889634
EXTRA = 8
KEYS = 256
PIECE = 32
CHUNK = 16

F32 = jnp.float32
BF16 = jnp.bfloat16
HIGH = lax.Precision.HIGHEST


def dot(a, b, dims=(((1,), (0,)), ((), ())), precision=None):
    return lax.dot_general(a, b, dims, precision=precision, preferred_element_type=F32)


def doc_starts(place_ref, lengths_ref):
    seq = place_ref[1]
    starts = [jnp.int32(0)]
    for d in range(DOCS - 1):
        starts.append(starts[-1] + lengths_ref[seq, d])
    return starts


def row_starts(starts, pos):
    first = jnp.zeros_like(pos)
    for s in starts[1:]:
        first = jnp.where(pos >= s, s, first)
    return first


def scalar_start(starts, pos):
    first = jnp.int32(0)
    for s in starts[1:]:
        first = jnp.where(pos >= s, s, first)
    return first


def expand_heads(copies):
    shape = (copies * PER_GROUP, WIDTH)
    row = lax.broadcasted_iota(jnp.int32, shape, 0) % PER_GROUP
    lane = lax.broadcasted_iota(jnp.int32, shape, 1)
    return jnp.where(lane // HEAD_DIM == row, 1.0, 0.0).astype(BF16)


def halves(x):
    upper = x.astype(BF16)
    return upper, (x - upper.astype(F32)).astype(BF16)


def silu(x):
    return (0.5 * x) * (1.0 + jnp.tanh(0.5 * x))


def prep_kernel(place_ref, lengths_ref, step_ref, rate_ref, col_ref, row_ref, trail_ref, keep_ref, thr_ref):
    rows = step_ref.shape[0]
    base = place_ref[0] * rows
    starts = doc_starts(place_ref, lengths_ref)
    pos = base + lax.broadcasted_iota(jnp.int32, (rows, HEADS), 0)
    first = row_starts(starts, pos)
    last_first = scalar_start(starts, base + rows - 1)
    t = step_ref[...].astype(F32)
    dt = jnp.maximum(t, 0.0) + jnp.log1p(jnp.exp(-jnp.abs(t)))
    a = dt * rate_ref[...] * (-LOG2E)
    i = lax.broadcasted_iota(jnp.int32, (rows, rows), 0)
    j = lax.broadcasted_iota(jnp.int32, (rows, rows), 1)
    tri = (i >= j).astype(F32)
    cum = dot(tri, a, precision=HIGH)
    total = cum[rows - 1 : rows, :]
    trail = halves(jnp.where(first == last_first, jnp.exp2(total - cum) * dt, 0.0))
    keep = halves(jnp.where(first < base, jnp.exp2(cum), 0.0))
    thr = halves(jnp.where(last_first < base, jnp.exp2(total), 0.0))
    row8 = lax.broadcasted_iota(jnp.int32, (8, HEADS), 0)
    thr_rows = jnp.where(
        row8 == 0, thr[0].astype(F32), jnp.where(row8 == 1, thr[1].astype(F32), 0.0)
    ).astype(BF16)
    row_ref[...] = jnp.transpose(cum - jnp.log2(dt))
    for g in range(GROUPS):
        part = slice(g * PER_GROUP, (g + 1) * PER_GROUP)
        col_ref[g] = cum[:, part]
        trail_ref[g] = jnp.concatenate([trail[0][:, part], trail[1][:, part]], axis=1)
        keep_ref[g] = jnp.concatenate([keep[0][:, part], keep[1][:, part]], axis=1)
        thr_ref[g] = thr_rows[:, part]


def front_kernel(
    place_ref, lengths_ref, x_ref, b_ref, c_ref, hx_ref, hb_ref, hc_ref,
    wx_ref, wb_ref, wc_ref, ox_ref, ob_ref, oc_ref, trail_ref, thr_ref,
    xa_ref, ba_ref, ca_ref, f_ref, pad_ref,
):
    rows = x_ref.shape[0]
    base = place_ref[0] * rows
    starts = doc_starts(place_ref, lengths_ref)
    pos = base + lax.broadcasted_iota(jnp.int32, (rows, 128), 0)
    rel = pos - row_starts(starts, pos)
    masks = [None] + [rel >= d for d in range(1, CONV)]

    def conv(src, rim, weight, bias, dst, lo):
        at = slice(lo, lo + 128)
        pad_ref[0:8, :] = rim[:, at].astype(F32)
        pad_ref[8 : 8 + rows, :] = src[:, at].astype(F32)
        acc = pad_ref[8 : 8 + rows, :] * weight[3:4, at] + bias[:, at]
        for d in range(1, CONV):
            tap = pad_ref[8 - d : 8 - d + rows, :] * weight[3 - d : 4 - d, at]
            acc = acc + jnp.where(masks[d], tap, 0.0)
        dst[:, at] = silu(acc).astype(BF16)

    for lo in range(0, WIDTH, 128):
        conv(x_ref, hx_ref, wx_ref, ox_ref, xa_ref, lo)
    conv(b_ref, hb_ref, wb_ref, ob_ref, ba_ref, 0)
    conv(c_ref, hc_ref, wc_ref, oc_ref, ca_ref, 0)

    scale = dot(trail_ref[0], expand_heads(2))
    weighted = (xa_ref[...].astype(F32) * scale).astype(BF16)
    fresh = dot(ba_ref[...], weighted, (((0,), (0,)), ((), ()))).astype(BF16)
    extra = dot(thr_ref[0], expand_heads(1)).astype(BF16)
    half = WIDTH // 2
    for k in range(2):
        f_ref[k, 0:STATE, :] = fresh[:, k * half : (k + 1) * half]
        f_ref[k, STATE : STATE + EXTRA, :] = extra[:, k * half : (k + 1) * half]


def inner_kernel(place_ref, lengths_ref, xa_ref, ba_ref, ca_ref, col_ref, row_ref, skip_ref, y_ref):
    rows = xa_ref.shape[0]
    base = place_ref[0] * rows
    starts = doc_starts(place_ref, lengths_ref)
    i = base + lax.broadcasted_iota(jnp.int32, (rows, rows), 0)
    j = base + lax.broadcasted_iota(jnp.int32, (rows, rows), 1)
    first = row_starts(starts, i)
    blocked = jnp.where((j <= i) & (j >= first), 0.0, NEGATIVE)
    scores = dot(ca_ref[...], ba_ref[...], (((1,), (1,)), ((), ())))
    lane = lax.broadcasted_iota(jnp.int32, (rows, 128), 1)
    col = col_ref[0]
    for p in range(PER_GROUP // 2):
        weights = []
        for h in (2 * p, 2 * p + 1):
            spread = (col[:, h : h + 1] + blocked) - row_ref[h : h + 1, :]
            weights.append((scores * jnp.exp2(spread)).astype(BF16))
        at = slice(p * 128, (p + 1) * 128)
        x = xa_ref[:, at]
        zero = jnp.zeros_like(x)
        both = jnp.concatenate(
            [jnp.where(lane < HEAD_DIM, x, zero), jnp.where(lane < HEAD_DIM, zero, x)], axis=0
        )
        y = dot(jnp.concatenate(weights, axis=1), both)
        y_ref[:, at] = y + x.astype(F32) * skip_ref[:, at]


def scan_kernel(f_ref, held_out_ref, out_ref, tail_ref, held_ref, state_ref, sems, out_sems, tail_sem):
    blocks, _, width = f_ref.shape
    pieces, _, piece, _ = held_ref.shape
    tail = pltpu.make_async_copy(f_ref.at[:, pl.ds(STATE, EXTRA), :], tail_ref, tail_sem)
    loads = [
        pltpu.make_async_copy(f_ref.at[:, pl.ds(q * piece, piece), :], held_ref.at[q], sems.at[q])
        for q in range(pieces)
    ]
    stores = [
        pltpu.make_async_copy(
            state_ref.at[q], out_ref.at[:, pl.ds(q * piece, piece), pl.ds(0, width)], out_sems.at[q]
        )
        for q in range(pieces)
    ]
    tail.start()
    for load in loads:
        load.start()
    tail.wait()
    for q in range(pieces):
        loads[q].wait()
        state = jnp.zeros((piece, width), F32)
        for r in range(blocks):
            state_ref[q, r] = state.astype(BF16)
            if r + 1 < blocks:
                ends = tail_ref[r].astype(F32)
                state = state * (ends[0:1, :] + ends[1:2, :]) + held_ref[q, r].astype(F32)
        stores[q].start()
    for store in stores:
        store.wait()


def final_kernel(
    y_far, s_far, z_far, ca_ref, keep_ref, gain_ref, o_ref, attn_ref,
    y_ref, s_ref, z_ref, scale_ref, carried_ref, sems,
):
    half = WIDTH // 2

    def copies(g):
        cols = pl.ds(pl.multiple_of(g * WIDTH, WIDTH), WIDTH)
        return (
            pltpu.make_async_copy(s_far.at[pl.ds(2 * g, 2)], s_ref.at[g], sems.at[0, g]),
            pltpu.make_async_copy(y_far.at[:, cols], y_ref.at[g], sems.at[1, g]),
            pltpu.make_async_copy(z_far.at[:, cols], z_ref.at[g], sems.at[2, g]),
        )

    @pl.when(pl.program_id(0) == 0)
    def _():
        for group in range(GROUPS):
            for copy in copies(group):
                copy.start()

    g = pl.program_id(0)
    scale_ref[...] = dot(keep_ref[g], expand_heads(2))
    state_copy, y_copy, z_copy = copies(g)
    state_copy.wait()
    ca = ca_ref[:, pl.ds(pl.multiple_of(g * STATE, STATE), STATE)]
    for k in range(2):
        carried_ref[:, k * half : (k + 1) * half] = dot(ca, s_ref[g, k, :, :half])
        own = s_ref.shape[3] - half
        attn_ref[:, k * own : (k + 1) * own] = s_ref[g, k, :, half:]
    y_copy.wait()
    z_copy.wait()
    gain = gain_ref[:, pl.ds(pl.multiple_of(g * WIDTH, WIDTH), WIDTH)]
    for lo in range(0, y_far.shape[0], CHUNK):
        at = slice(lo, lo + CHUNK)
        mixed = (y_ref[g, at, :] + scale_ref[at, :] * carried_ref[at, :]).astype(BF16).astype(F32)
        gated = mixed * silu(z_ref[g, at, :].astype(F32))
        mean = jnp.mean(gated * gated, axis=1, keepdims=True)
        o_ref[at, :] = (gated * lax.rsqrt(mean + EPSILON) * gain).astype(BF16)


def pack_kernel(q_ref, k_ref, v_ref, out_ref, sems):
    parts = out_ref.shape[0]
    width = q_ref.shape[1] // parts
    copies = []
    for d in range(parts):
        at = pl.ds(d * KVHEADS // parts * QDIM, QDIM)
        q_cols = pl.ds(d * width, width)
        copies += [
            pltpu.make_async_copy(q_ref.at[:, q_cols], out_ref.at[d, :, pl.ds(0, width)], sems.at[0, d]),
            pltpu.make_async_copy(k_ref.at[:, at], out_ref.at[d, :, pl.ds(width, QDIM)], sems.at[1, d]),
            pltpu.make_async_copy(v_ref.at[:, at], out_ref.at[d, :, pl.ds(width + QDIM, QDIM)], sems.at[2, d]),
        ]
    for copy in copies:
        copy.start()
    for copy in copies:
        copy.wait()


def attend_kernel(place_ref, lengths_ref, far_ref, out_ref, qkv_ref, o_ref, sems, s_ref, m_ref, l_ref, acc_ref):
    copy = pltpu.make_async_copy(far_ref, qkv_ref, sems.at[0])
    copy.start()
    copy.wait()
    length = qkv_ref.shape[0]
    q_width = qkv_ref.shape[1] - 2 * QDIM
    heads = q_width // QDIM
    k_cols, v_cols = slice(q_width, q_width + QDIM), slice(q_width + QDIM, q_width + 2 * QDIM)
    starts = doc_starts(place_ref, lengths_ref)
    lane = lax.broadcasted_iota(jnp.int32, (KEYS, KEYS), 1)
    scaling = QDIM ** (-0.5) * LOG2E

    def one_tile(t, outer):
        base = t * KEYS
        here = pl.ds(pl.multiple_of(base, KEYS), KEYS)
        pos = base + lax.broadcasted_iota(jnp.int32, (KEYS, KEYS), 0)
        first = jnp.maximum(row_starts(starts, pos), pos - (WINDOW - 1))
        last = base + KEYS - 1
        lowest = jnp.maximum(scalar_start(starts, base), base - (WINDOW - 1))
        highest = jnp.maximum(scalar_start(starts, last), last - (WINDOW - 1))
        begin = lowest // KEYS
        clear = jnp.minimum((highest + KEYS - 1) // KEYS, t)
        queries = jnp.concatenate([qkv_ref[here, h * QDIM : (h + 1) * QDIM] for h in range(heads)], axis=0)
        m_ref[...] = jnp.full_like(m_ref, NEGATIVE)

        def score(masked, j, carry):
            k = qkv_ref[pl.ds(pl.multiple_of(j * KEYS, KEYS), KEYS), k_cols]
            s = dot(queries, k, (((1,), (1,)), ((), ())))
            if masked:
                key = j * KEYS + lane
                visible = (key <= pos) & (key >= first)
            for h in range(heads):
                at = slice(h * KEYS, (h + 1) * KEYS)
                part = s[at]
                if masked:
                    part = jnp.where(visible, part, NEGATIVE)
                s_ref[j, at, :] = part
                top = m_ref[at, :]
                for c in range(0, KEYS, 128):
                    top = jnp.maximum(top, part[:, c : c + 128])
                m_ref[at, :] = top
            return carry

        lax.fori_loop(begin, clear, functools.partial(score, True), 0)
        lax.fori_loop(clear, t, functools.partial(score, False), 0)
        score(True, t, 0)
        m_ref[...] = jnp.broadcast_to(jnp.max(m_ref[...], axis=1, keepdims=True), m_ref.shape)
        l_ref[...] = jnp.zeros_like(l_ref)
        acc_ref[...] = jnp.zeros_like(acc_ref)

        def gather(j, carry):
            v = qkv_ref[pl.ds(pl.multiple_of(j * KEYS, KEYS), KEYS), v_cols]
            numerators = []
            for h in range(heads):
                at = slice(h * KEYS, (h + 1) * KEYS)
                top = m_ref[at, :]
                total = l_ref[at, :]
                parts = []
                for c in range(0, KEYS, 128):
                    p = jnp.exp2((s_ref[j, at, c : c + 128] - top) * scaling)
                    total = total + p
                    parts.append(p.astype(BF16))
                l_ref[at, :] = total
                numerators.append(jnp.concatenate(parts, axis=1))
            acc_ref[...] += dot(jnp.concatenate(numerators, axis=0), v)
            return carry

        lax.fori_loop(begin, t + 1, gather, 0)
        for h in range(heads):
            at = slice(h * KEYS, (h + 1) * KEYS)
            total = jnp.sum(l_ref[at, :], axis=1, keepdims=True)
            o_ref[here, h * QDIM : (h + 1) * QDIM] = (acc_ref[at, :] / total).astype(BF16)
        return outer

    lax.fori_loop(0, length // KEYS, one_tile, 0)
    blocks, rows, out_width = out_ref.shape
    sends = [
        pltpu.make_async_copy(
            o_ref.at[pl.ds(r * rows, rows), :],
            out_ref.at[r, :, pl.ds(out_width - q_width, q_width)],
            sems.at[1 + r],
        )
        for r in range(blocks)
    ]
    for send in sends:
        send.start()
    for send in sends:
        send.wait()


def work(microseconds):
    return pl.CostEstimate(flops=0, transcendentals=0, bytes_accessed=int(microseconds * 3.5e6))


def smem():
    return pl.BlockSpec(memory_space=pltpu.SMEM)


def on_device(
    mixer_input, z_gate, time_step, conv_weight, conv_bias, decay_rate, skip_gain,
    norm_gain, doc_lengths, queries, attn_keys, attn_values,
):
    rows = mixer_input.shape[1]
    blocks = lax.axis_size("ctx")
    place = jnp.stack([lax.axis_index("ctx"), lax.axis_index("batch")]).astype(jnp.int32)
    raw = mixer_input[0]
    call = functools.partial(
        pl.pallas_call, compiler_params=pltpu.CompilerParams(vmem_limit_bytes=63 << 20)
    )

    o_width = QHEADS * QDIM // blocks
    qkv = call(
        pack_kernel,
        in_specs=[pl.BlockSpec(memory_space=pl.ANY)] * 3,
        out_specs=pl.BlockSpec(memory_space=pl.ANY),
        scratch_shapes=[pltpu.SemaphoreType.DMA((3, blocks))],
        out_shape=jax.ShapeDtypeStruct((blocks, rows, o_width + 2 * QDIM), BF16),
        name="pack",
        cost_estimate=work(3),
    )(queries[0], attn_keys[0], attn_values[0])
    rim = lax.ppermute(raw[rows - 8 :], "ctx", [(r, r + 1) for r in range(blocks - 1)])
    rim, qkv = lax.optimization_barrier((rim, qkv))
    qkv = lax.all_to_all(qkv, "ctx", split_axis=0, concat_axis=0, tiled=True)

    col, row, trail, keep, thr = call(
        prep_kernel,
        in_specs=[smem(), smem(), pl.BlockSpec(), pl.BlockSpec()],
        out_shape=[
            jax.ShapeDtypeStruct((GROUPS, rows, PER_GROUP), F32),
            jax.ShapeDtypeStruct((HEADS, rows), F32),
            jax.ShapeDtypeStruct((GROUPS, rows, 2 * PER_GROUP), BF16),
            jax.ShapeDtypeStruct((GROUPS, rows, 2 * PER_GROUP), BF16),
            jax.ShapeDtypeStruct((GROUPS, 8, PER_GROUP), BF16),
        ],
        name="prep",
        cost_estimate=work(3),
    )(place, doc_lengths, time_step[0], decay_rate[None])

    wide = lambda n: pl.BlockSpec((n, WIDTH), lambda g: (0, g))
    b_cols = lambda n: pl.BlockSpec((n, STATE), lambda g: (0, INNER // STATE + g))
    c_cols = lambda n: pl.BlockSpec((n, STATE), lambda g: (0, INNER // STATE + GROUPS + g))
    group_cols = lambda n: pl.BlockSpec((n, STATE), lambda g: (0, g))
    per_group = pl.BlockSpec((1, rows, PER_GROUP), lambda g: (g, 0, 0))
    per_group_two = pl.BlockSpec((1, rows, 2 * PER_GROUP), lambda g: (g, 0, 0))
    bias = conv_bias[None]
    half = WIDTH // 2
    x_act, b_act, c_act, fresh = call(
        front_kernel,
        grid=(GROUPS,),
        in_specs=[
            smem(), smem(),
            wide(rows), b_cols(rows), c_cols(rows),
            wide(8), b_cols(8), c_cols(8),
            wide(CONV), b_cols(CONV), c_cols(CONV),
            wide(1), b_cols(1), c_cols(1),
            per_group_two, pl.BlockSpec((1, 8, PER_GROUP), lambda g: (g, 0, 0)),
        ],
        out_specs=[
            wide(rows), group_cols(rows), group_cols(rows),
            pl.BlockSpec((2, STATE + EXTRA, half), lambda g: (g, 0, 0)),
        ],
        out_shape=[
            jax.ShapeDtypeStruct((rows, INNER), BF16),
            jax.ShapeDtypeStruct((rows, GROUPS * STATE), BF16),
            jax.ShapeDtypeStruct((rows, GROUPS * STATE), BF16),
            jax.ShapeDtypeStruct((2 * GROUPS, STATE + EXTRA, half), BF16),
        ],
        scratch_shapes=[pltpu.VMEM((8 + rows, 128), F32)],
        name="front",
        cost_estimate=work(40),
    )(
        place, doc_lengths, raw, raw, raw, rim, rim, rim,
        conv_weight, conv_weight, conv_weight, bias, bias, bias, trail, thr,
    )

    local = call(
        inner_kernel,
        grid=(GROUPS,),
        in_specs=[
            smem(), smem(), wide(rows), group_cols(rows), group_cols(rows), per_group,
            pl.BlockSpec((PER_GROUP, rows), lambda g: (g, 0)), wide(1),
        ],
        out_specs=wide(rows),
        out_shape=jax.ShapeDtypeStruct((rows, INNER), F32),
        name="inner",
        cost_estimate=work(9),
    )(place, doc_lengths, x_act, b_act, c_act, col, row, jnp.repeat(skip_gain, HEAD_DIM)[None])

    fresh, qkv, local = lax.optimization_barrier((fresh, qkv, local))
    own_fresh = lax.all_to_all(fresh, "ctx", split_axis=0, concat_axis=0, tiled=True)

    tall = o_width // QDIM * KEYS
    attended = call(
        attend_kernel,
        in_specs=[smem(), smem(), pl.BlockSpec(memory_space=pl.ANY)],
        out_specs=pl.BlockSpec(memory_space=pl.ANY),
        out_shape=jax.ShapeDtypeStruct((blocks, rows, half + o_width), BF16),
        scratch_shapes=[
            pltpu.VMEM((blocks * rows, o_width + 2 * QDIM), BF16),
            pltpu.VMEM((blocks * rows, o_width), BF16),
            pltpu.SemaphoreType.DMA((1 + blocks,)),
            pltpu.VMEM((blocks * rows // KEYS, tall, KEYS), F32),
            pltpu.VMEM((tall, 128), F32),
            pltpu.VMEM((tall, 128), F32),
            pltpu.VMEM((tall, QDIM), F32),
        ],
        name="attend",
        cost_estimate=work(30),
    )(place, doc_lengths, qkv.reshape(blocks * rows, o_width + 2 * QDIM))
    own_states = call(
        scan_kernel,
        in_specs=[pl.BlockSpec(memory_space=pl.ANY)] * 2,
        out_specs=pl.BlockSpec(memory_space=pl.ANY),
        out_shape=jax.ShapeDtypeStruct((blocks, STATE, half + o_width), BF16),
        input_output_aliases={1: 0},
        scratch_shapes=[
            pltpu.VMEM((blocks, EXTRA, half), BF16),
            pltpu.VMEM((STATE // PIECE, blocks, PIECE, half), BF16),
            pltpu.VMEM((STATE // PIECE, blocks, PIECE, half), BF16),
            pltpu.SemaphoreType.DMA((STATE // PIECE,)),
            pltpu.SemaphoreType.DMA((STATE // PIECE,)),
            pltpu.SemaphoreType.DMA,
        ],
        name="scan",
        cost_estimate=work(4),
    )(own_fresh, attended)
    states = lax.all_to_all(own_states, "ctx", split_axis=0, concat_axis=0, tiled=True)

    mixer_out, attn_out = call(
        final_kernel,
        grid=(GROUPS,),
        in_specs=[pl.BlockSpec(memory_space=pl.ANY)] * 3
        + [
            pl.BlockSpec((rows, GROUPS * STATE), lambda g: (0, 0)),
            pl.BlockSpec((GROUPS, rows, 2 * PER_GROUP), lambda g: (0, 0, 0)),
            pl.BlockSpec((1, INNER), lambda g: (0, 0)),
        ],
        out_specs=[wide(rows), pl.BlockSpec((rows, 2 * o_width), lambda g: (0, g))],
        out_shape=[
            jax.ShapeDtypeStruct((rows, INNER), BF16),
            jax.ShapeDtypeStruct((rows, QHEADS * QDIM), BF16),
        ],
        scratch_shapes=[
            pltpu.VMEM((GROUPS, rows, WIDTH), F32),
            pltpu.VMEM((GROUPS, 2, STATE, half + o_width), BF16),
            pltpu.VMEM((GROUPS, rows, WIDTH), BF16),
            pltpu.VMEM((rows, WIDTH), F32),
            pltpu.VMEM((rows, WIDTH), F32),
            pltpu.SemaphoreType.DMA((3, GROUPS)),
        ],
        name="final",
        cost_estimate=work(7),
    )(local, states, z_gate[0], c_act, keep, norm_gain[None])
    return (mixer_out[None], attn_out[None])


def solution(mesh):
    placed = P("batch", "ctx", None)
    whole = P()
    return jax.shard_map(
        on_device,
        mesh=mesh,
        in_specs=(placed, placed, placed) + (whole,) * 6 + (placed,) * 3,
        out_specs=(placed, placed),
        check_vma=False,
    )
```

```python
import functools

import jax
import jax.numpy as jnp
from jax import lax
from jax.experimental import pallas as pl
from jax.experimental.pallas import tpu as pltpu
from jax.sharding import PartitionSpec as P

HEADS = 128
HEAD_DIM = 64
STATE = 128
GROUPS = 8
QHEADS = 32
KVHEADS = 8
QDIM = 128
CONV = 4
WINDOW = 2048

PER_GROUP = HEADS // GROUPS
WIDTH = PER_GROUP * HEAD_DIM
INNER = HEADS * HEAD_DIM
DOCS = 6
EPSILON = 1e-05
NEGATIVE = -1e30
LOG2E = 1.4426950408889634
EXTRA = 8
KEYS = 256
PIECE = 32
CHUNK = 16

F32 = jnp.float32
BF16 = jnp.bfloat16
HIGH = lax.Precision.HIGHEST


def dot(a, b, dims=(((1,), (0,)), ((), ())), precision=None):
    return lax.dot_general(a, b, dims, precision=precision, preferred_element_type=F32)


def doc_starts(place_ref, lengths_ref):
    seq = place_ref[1]
    starts = [jnp.int32(0)]
    for d in range(DOCS - 1):
        starts.append(starts[-1] + lengths_ref[seq, d])
    return starts


def row_starts(starts, pos):
    first = jnp.zeros_like(pos)
    for s in starts[1:]:
        first = jnp.where(pos >= s, s, first)
    return first


def scalar_start(starts, pos):
    first = jnp.int32(0)
    for s in starts[1:]:
        first = jnp.where(pos >= s, s, first)
    return first


def expand_heads(copies):
    shape = (copies * PER_GROUP, WIDTH)
    row = lax.broadcasted_iota(jnp.int32, shape, 0) % PER_GROUP
    lane = lax.broadcasted_iota(jnp.int32, shape, 1)
    return jnp.where(lane // HEAD_DIM == row, 1.0, 0.0).astype(BF16)


def halves(x):
    upper = x.astype(BF16)
    return upper, (x - upper.astype(F32)).astype(BF16)


def silu(x):
    return (0.5 * x) * (1.0 + jnp.tanh(0.5 * x))


def prep_kernel(place_ref, lengths_ref, step_ref, rate_ref, col_ref, row_ref, trail_ref, keep_ref, thr_ref):
    rows = step_ref.shape[0]
    base = place_ref[0] * rows
    starts = doc_starts(place_ref, lengths_ref)
    pos = base + lax.broadcasted_iota(jnp.int32, (rows, HEADS), 0)
    first = row_starts(starts, pos)
    last_first = scalar_start(starts, base + rows - 1)
    t = step_ref[...].astype(F32)
    dt = jnp.maximum(t, 0.0) + jnp.log1p(jnp.exp(-jnp.abs(t)))
    a = dt * rate_ref[...] * (-LOG2E)
    i = lax.broadcasted_iota(jnp.int32, (rows, rows), 0)
    j = lax.broadcasted_iota(jnp.int32, (rows, rows), 1)
    tri = (i >= j).astype(F32)
    cum = dot(tri, a, precision=HIGH)
    total = cum[rows - 1 : rows, :]
    trail = halves(jnp.where(first == last_first, jnp.exp2(total - cum) * dt, 0.0))
    keep = halves(jnp.where(first < base, jnp.exp2(cum), 0.0))
    thr = halves(jnp.where(last_first < base, jnp.exp2(total), 0.0))
    row8 = lax.broadcasted_iota(jnp.int32, (8, HEADS), 0)
    thr_rows = jnp.where(
        row8 == 0, thr[0].astype(F32), jnp.where(row8 == 1, thr[1].astype(F32), 0.0)
    ).astype(BF16)
    row_ref[...] = jnp.transpose(cum - jnp.log2(dt))
    for g in range(GROUPS):
        part = slice(g * PER_GROUP, (g + 1) * PER_GROUP)
        col_ref[g] = cum[:, part]
        trail_ref[g] = jnp.concatenate([trail[0][:, part], trail[1][:, part]], axis=1)
        keep_ref[g] = jnp.concatenate([keep[0][:, part], keep[1][:, part]], axis=1)
        thr_ref[g] = thr_rows[:, part]


def front_kernel(
    place_ref, lengths_ref, x_ref, b_ref, c_ref, hx_ref, hb_ref, hc_ref,
    wx_ref, wb_ref, wc_ref, ox_ref, ob_ref, oc_ref, trail_ref, thr_ref,
    xa_ref, ba_ref, ca_ref, f_ref, pad_ref,
):
    rows = x_ref.shape[0]
    base = place_ref[0] * rows
    starts = doc_starts(place_ref, lengths_ref)
    pos = base + lax.broadcasted_iota(jnp.int32, (rows, 128), 0)
    rel = pos - row_starts(starts, pos)
    masks = [None] + [rel >= d for d in range(1, CONV)]

    def conv(src, rim, weight, bias, dst, lo):
        at = slice(lo, lo + 128)
        pad_ref[0:8, :] = rim[:, at].astype(F32)
        pad_ref[8 : 8 + rows, :] = src[:, at].astype(F32)
        acc = pad_ref[8 : 8 + rows, :] * weight[3:4, at] + bias[:, at]
        for d in range(1, CONV):
            tap = pad_ref[8 - d : 8 - d + rows, :] * weight[3 - d : 4 - d, at]
            acc = acc + jnp.where(masks[d], tap, 0.0)
        dst[:, at] = silu(acc).astype(BF16)

    for lo in range(0, WIDTH, 128):
        conv(x_ref, hx_ref, wx_ref, ox_ref, xa_ref, lo)
    conv(b_ref, hb_ref, wb_ref, ob_ref, ba_ref, 0)
    conv(c_ref, hc_ref, wc_ref, oc_ref, ca_ref, 0)

    scale = dot(trail_ref[0], expand_heads(2))
    weighted = (xa_ref[...].astype(F32) * scale).astype(BF16)
    fresh = dot(ba_ref[...], weighted, (((0,), (0,)), ((), ()))).astype(BF16)
    extra = dot(thr_ref[0], expand_heads(1)).astype(BF16)
    half = WIDTH // 2
    for k in range(2):
        f_ref[k, 0:STATE, :] = fresh[:, k * half : (k + 1) * half]
        f_ref[k, STATE : STATE + EXTRA, :] = extra[:, k * half : (k + 1) * half]


def inner_kernel(place_ref, lengths_ref, xa_ref, ba_ref, ca_ref, col_ref, row_ref, skip_ref, y_ref):
    rows = xa_ref.shape[0]
    base = place_ref[0] * rows
    starts = doc_starts(place_ref, lengths_ref)
    i = base + lax.broadcasted_iota(jnp.int32, (rows, rows), 0)
    j = base + lax.broadcasted_iota(jnp.int32, (rows, rows), 1)
    first = row_starts(starts, i)
    blocked = jnp.where((j <= i) & (j >= first), 0.0, NEGATIVE)
    scores = dot(ca_ref[...], ba_ref[...], (((1,), (1,)), ((), ())))
    lane = lax.broadcasted_iota(jnp.int32, (rows, 128), 1)
    col = col_ref[0]
    for p in range(PER_GROUP // 2):
        weights = []
        for h in (2 * p, 2 * p + 1):
            spread = (col[:, h : h + 1] + blocked) - row_ref[h : h + 1, :]
            weights.append((scores * jnp.exp2(spread)).astype(BF16))
        at = slice(p * 128, (p + 1) * 128)
        x = xa_ref[:, at]
        zero = jnp.zeros_like(x)
        both = jnp.concatenate(
            [jnp.where(lane < HEAD_DIM, x, zero), jnp.where(lane < HEAD_DIM, zero, x)], axis=0
        )
        y = dot(jnp.concatenate(weights, axis=1), both)
        y_ref[:, at] = (y + x.astype(F32) * skip_ref[:, at]).astype(BF16)


def scan_kernel(f_ref, held_out_ref, out_ref, tail_ref, held_ref, state_ref, sems, out_sems, tail_sem):
    blocks, _, width = f_ref.shape
    pieces, _, piece, _ = held_ref.shape
    tail = pltpu.make_async_copy(f_ref.at[:, pl.ds(STATE, EXTRA), :], tail_ref, tail_sem)
    loads = [
        pltpu.make_async_copy(f_ref.at[:, pl.ds(q * piece, piece), :], held_ref.at[q], sems.at[q])
        for q in range(pieces)
    ]
    stores = [
        pltpu.make_async_copy(
            state_ref.at[q], out_ref.at[:, pl.ds(q * piece, piece), pl.ds(0, width)], out_sems.at[q]
        )
        for q in range(pieces)
    ]
    tail.start()
    for load in loads:
        load.start()
    tail.wait()
    for q in range(pieces):
        loads[q].wait()
        state = jnp.zeros((piece, width), F32)
        for r in range(blocks):
            state_ref[q, r] = state.astype(BF16)
            if r + 1 < blocks:
                ends = tail_ref[r].astype(F32)
                state = state * (ends[0:1, :] + ends[1:2, :]) + held_ref[q, r].astype(F32)
        stores[q].start()
    for store in stores:
        store.wait()


def final_kernel(
    y_far, s_far, z_far, ca_ref, keep_ref, gain_ref, o_far, attn_far,
    y_ref, s_ref, z_ref, o_ref, spread_ref, scale_ref, carried_ref, sems,
):
    half = WIDTH // 2
    own = s_ref.shape[3] - half

    def loads(g):
        cols = pl.ds(pl.multiple_of(g * WIDTH, WIDTH), WIDTH)
        return (
            pltpu.make_async_copy(s_far.at[pl.ds(2 * g, 2)], s_ref.at[g], sems.at[0, g]),
            pltpu.make_async_copy(y_far.at[:, cols], y_ref.at[g], sems.at[1, g]),
            pltpu.make_async_copy(z_far.at[:, cols], z_ref.at[g], sems.at[2, g]),
        )

    def stores(g):
        cols = pl.ds(pl.multiple_of(g * WIDTH, WIDTH), WIDTH)
        found = [pltpu.make_async_copy(o_ref.at[g], o_far.at[:, cols], sems.at[3, g])]
        for k in range(2):
            at = pl.ds(pl.multiple_of((2 * g + k) * own, own), own)
            source = s_ref.at[g, k, :, pl.ds(half, own)]
            found.append(pltpu.make_async_copy(source, attn_far.at[:, at], sems.at[4 + k, g]))
        return found

    g = pl.program_id(0)

    @pl.when(g == 0)
    def _():
        for group in range(GROUPS):
            for copy in loads(group):
                copy.start()
        spread_ref[...] = expand_heads(2)

    scale_ref[...] = dot(keep_ref[g], spread_ref[...])
    state_copy, y_copy, z_copy = loads(g)
    mixer_store, *attn_stores = stores(g)
    state_copy.wait()
    for copy in attn_stores:
        copy.start()
    ca = ca_ref[:, pl.ds(pl.multiple_of(g * STATE, STATE), STATE)]
    for k in range(2):
        carried_ref[:, k * half : (k + 1) * half] = dot(ca, s_ref[g, k, :, :half])
    y_copy.wait()
    z_copy.wait()
    gain = gain_ref[:, pl.ds(pl.multiple_of(g * WIDTH, WIDTH), WIDTH)]
    for lo in range(0, y_far.shape[0], CHUNK):
        at = slice(lo, lo + CHUNK)
        mixed = (y_ref[g, at, :].astype(F32) + scale_ref[at, :] * carried_ref[at, :]).astype(BF16).astype(F32)
        gated = mixed * silu(z_ref[g, at, :].astype(F32))
        mean = jnp.mean(gated * gated, axis=1, keepdims=True)
        o_ref[g, at, :] = (gated * lax.rsqrt(mean + EPSILON) * gain).astype(BF16)
    mixer_store.start()

    @pl.when(g == GROUPS - 1)
    def _():
        for group in range(GROUPS):
            for copy in stores(group):
                copy.wait()


def pack_kernel(q_ref, k_ref, v_ref, out_ref, held_ref, sems):
    parts = out_ref.shape[0]
    width = q_ref.shape[1] // parts
    loads, stores = [], []
    for d in range(parts):
        at = pl.ds(d * KVHEADS // parts * QDIM, QDIM)
        q_cols = pl.ds(d * width, width)
        loads += [
            pltpu.make_async_copy(q_ref.at[:, q_cols], held_ref.at[d, :, pl.ds(0, width)], sems.at[0, d]),
            pltpu.make_async_copy(k_ref.at[:, at], held_ref.at[d, :, pl.ds(width, QDIM)], sems.at[1, d]),
            pltpu.make_async_copy(v_ref.at[:, at], held_ref.at[d, :, pl.ds(width + QDIM, QDIM)], sems.at[2, d]),
        ]
        stores.append(pltpu.make_async_copy(held_ref.at[d], out_ref.at[d], sems.at[3, d]))
    for load in loads:
        load.start()
    for d in range(parts):
        for load in loads[3 * d : 3 * d + 3]:
            load.wait()
        stores[d].start()
    for store in stores:
        store.wait()


def attend_kernel(place_ref, lengths_ref, far_ref, out_ref, qkv_ref, o_ref, sems, s_ref, m_ref, l_ref, acc_ref):
    copy = pltpu.make_async_copy(far_ref, qkv_ref, sems.at[0])
    copy.start()
    copy.wait()
    length = qkv_ref.shape[0]
    q_width = qkv_ref.shape[1] - 2 * QDIM
    heads = q_width // QDIM
    k_cols, v_cols = slice(q_width, q_width + QDIM), slice(q_width + QDIM, q_width + 2 * QDIM)
    starts = doc_starts(place_ref, lengths_ref)
    lane = lax.broadcasted_iota(jnp.int32, (KEYS, KEYS), 1)
    scaling = QDIM ** (-0.5) * LOG2E

    def one_tile(t, outer):
        base = t * KEYS
        here = pl.ds(pl.multiple_of(base, KEYS), KEYS)
        pos = base + lax.broadcasted_iota(jnp.int32, (KEYS, KEYS), 0)
        first = jnp.maximum(row_starts(starts, pos), pos - (WINDOW - 1))
        last = base + KEYS - 1
        lowest = jnp.maximum(scalar_start(starts, base), base - (WINDOW - 1))
        highest = jnp.maximum(scalar_start(starts, last), last - (WINDOW - 1))
        begin = lowest // KEYS
        clear = jnp.minimum((highest + KEYS - 1) // KEYS, t)
        queries = jnp.concatenate([qkv_ref[here, h * QDIM : (h + 1) * QDIM] for h in range(heads)], axis=0)
        m_ref[...] = jnp.full_like(m_ref, NEGATIVE)

        def score(masked, j, carry):
            k = qkv_ref[pl.ds(pl.multiple_of(j * KEYS, KEYS), KEYS), k_cols]
            s = dot(queries, k, (((1,), (1,)), ((), ())))
            if masked:
                key = j * KEYS + lane
                visible = (key <= pos) & (key >= first)
            for h in range(heads):
                at = slice(h * KEYS, (h + 1) * KEYS)
                part = s[at]
                if masked:
                    part = jnp.where(visible, part, NEGATIVE)
                s_ref[j, at, :] = part
                top = m_ref[at, :]
                for c in range(0, KEYS, 128):
                    top = jnp.maximum(top, part[:, c : c + 128])
                m_ref[at, :] = top
            return carry

        lax.fori_loop(begin, clear, functools.partial(score, True), 0)
        lax.fori_loop(clear, t, functools.partial(score, False), 0)
        score(True, t, 0)
        m_ref[...] = jnp.broadcast_to(jnp.max(m_ref[...], axis=1, keepdims=True), m_ref.shape)
        l_ref[...] = jnp.zeros_like(l_ref)
        acc_ref[...] = jnp.zeros_like(acc_ref)

        def gather(j, carry):
            v = qkv_ref[pl.ds(pl.multiple_of(j * KEYS, KEYS), KEYS), v_cols]
            numerators = []
            for h in range(heads):
                at = slice(h * KEYS, (h + 1) * KEYS)
                top = m_ref[at, :]
                total = l_ref[at, :]
                parts = []
                for c in range(0, KEYS, 128):
                    p = jnp.exp2((s_ref[j, at, c : c + 128] - top) * scaling)
                    total = total + p
                    parts.append(p.astype(BF16))
                l_ref[at, :] = total
                numerators.append(jnp.concatenate(parts, axis=1))
            acc_ref[...] += dot(jnp.concatenate(numerators, axis=0), v)
            return carry

        lax.fori_loop(begin, t + 1, gather, 0)
        for h in range(heads):
            at = slice(h * KEYS, (h + 1) * KEYS)
            total = jnp.sum(l_ref[at, :], axis=1, keepdims=True)
            o_ref[here, h * QDIM : (h + 1) * QDIM] = (acc_ref[at, :] / total).astype(BF16)
        return outer

    lax.fori_loop(0, length // KEYS, one_tile, 0)
    blocks, rows, out_width = out_ref.shape
    sends = [
        pltpu.make_async_copy(
            o_ref.at[pl.ds(r * rows, rows), :],
            out_ref.at[r, :, pl.ds(out_width - q_width, q_width)],
            sems.at[1 + r],
        )
        for r in range(blocks)
    ]
    for send in sends:
        send.start()
    for send in sends:
        send.wait()


def work(microseconds):
    return pl.CostEstimate(flops=0, transcendentals=0, bytes_accessed=int(microseconds * 3.5e6))


def smem():
    return pl.BlockSpec(memory_space=pltpu.SMEM)


def on_device(
    mixer_input, z_gate, time_step, conv_weight, conv_bias, decay_rate, skip_gain,
    norm_gain, doc_lengths, queries, attn_keys, attn_values,
):
    rows = mixer_input.shape[1]
    blocks = lax.axis_size("ctx")
    place = jnp.stack([lax.axis_index("ctx"), lax.axis_index("batch")]).astype(jnp.int32)
    raw = mixer_input[0]
    call = functools.partial(
        pl.pallas_call, compiler_params=pltpu.CompilerParams(vmem_limit_bytes=63 << 20)
    )

    o_width = QHEADS * QDIM // blocks
    qkv = call(
        pack_kernel,
        in_specs=[pl.BlockSpec(memory_space=pl.ANY)] * 3,
        out_specs=pl.BlockSpec(memory_space=pl.ANY),
        scratch_shapes=[
            pltpu.VMEM((blocks, rows, o_width + 2 * QDIM), BF16),
            pltpu.SemaphoreType.DMA((4, blocks)),
        ],
        out_shape=jax.ShapeDtypeStruct((blocks, rows, o_width + 2 * QDIM), BF16),
        name="pack",
        cost_estimate=work(3),
    )(queries[0], attn_keys[0], attn_values[0])
    rim = lax.ppermute(raw[rows - 8 :], "ctx", [(r, r + 1) for r in range(blocks - 1)])
    rim, qkv = lax.optimization_barrier((rim, qkv))
    qkv = lax.all_to_all(qkv, "ctx", split_axis=0, concat_axis=0, tiled=True)

    col, row, trail, keep, thr = call(
        prep_kernel,
        in_specs=[smem(), smem(), pl.BlockSpec(), pl.BlockSpec()],
        out_shape=[
            jax.ShapeDtypeStruct((GROUPS, rows, PER_GROUP), F32),
            jax.ShapeDtypeStruct((HEADS, rows), F32),
            jax.ShapeDtypeStruct((GROUPS, rows, 2 * PER_GROUP), BF16),
            jax.ShapeDtypeStruct((GROUPS, rows, 2 * PER_GROUP), BF16),
            jax.ShapeDtypeStruct((GROUPS, 8, PER_GROUP), BF16),
        ],
        name="prep",
        cost_estimate=work(3),
    )(place, doc_lengths, time_step[0], decay_rate[None])

    wide = lambda n: pl.BlockSpec((n, WIDTH), lambda g: (0, g))
    b_cols = lambda n: pl.BlockSpec((n, STATE), lambda g: (0, INNER // STATE + g))
    c_cols = lambda n: pl.BlockSpec((n, STATE), lambda g: (0, INNER // STATE + GROUPS + g))
    group_cols = lambda n: pl.BlockSpec((n, STATE), lambda g: (0, g))
    per_group = pl.BlockSpec((1, rows, PER_GROUP), lambda g: (g, 0, 0))
    per_group_two = pl.BlockSpec((1, rows, 2 * PER_GROUP), lambda g: (g, 0, 0))
    bias = conv_bias[None]
    half = WIDTH // 2
    x_act, b_act, c_act, fresh = call(
        front_kernel,
        grid=(GROUPS,),
        in_specs=[
            smem(), smem(),
            wide(rows), b_cols(rows), c_cols(rows),
            wide(8), b_cols(8), c_cols(8),
            wide(CONV), b_cols(CONV), c_cols(CONV),
            wide(1), b_cols(1), c_cols(1),
            per_group_two, pl.BlockSpec((1, 8, PER_GROUP), lambda g: (g, 0, 0)),
        ],
        out_specs=[
            wide(rows), group_cols(rows), group_cols(rows),
            pl.BlockSpec((2, STATE + EXTRA, half), lambda g: (g, 0, 0)),
        ],
        out_shape=[
            jax.ShapeDtypeStruct((rows, INNER), BF16),
            jax.ShapeDtypeStruct((rows, GROUPS * STATE), BF16),
            jax.ShapeDtypeStruct((rows, GROUPS * STATE), BF16),
            jax.ShapeDtypeStruct((2 * GROUPS, STATE + EXTRA, half), BF16),
        ],
        scratch_shapes=[pltpu.VMEM((8 + rows, 128), F32)],
        name="front",
        cost_estimate=work(40),
    )(
        place, doc_lengths, raw, raw, raw, rim, rim, rim,
        conv_weight, conv_weight, conv_weight, bias, bias, bias, trail, thr,
    )

    local = call(
        inner_kernel,
        grid=(GROUPS,),
        in_specs=[
            smem(), smem(), wide(rows), group_cols(rows), group_cols(rows), per_group,
            pl.BlockSpec((PER_GROUP, rows), lambda g: (g, 0)), wide(1),
        ],
        out_specs=wide(rows),
        out_shape=jax.ShapeDtypeStruct((rows, INNER), BF16),
        name="inner",
        cost_estimate=work(9),
    )(place, doc_lengths, x_act, b_act, c_act, col, row, jnp.repeat(skip_gain, HEAD_DIM)[None])

    fresh, qkv, local = lax.optimization_barrier((fresh, qkv, local))
    own_fresh = lax.all_to_all(fresh, "ctx", split_axis=0, concat_axis=0, tiled=True)

    tall = o_width // QDIM * KEYS
    attended = call(
        attend_kernel,
        in_specs=[smem(), smem(), pl.BlockSpec(memory_space=pl.ANY)],
        out_specs=pl.BlockSpec(memory_space=pl.ANY),
        out_shape=jax.ShapeDtypeStruct((blocks, rows, half + o_width), BF16),
        scratch_shapes=[
            pltpu.VMEM((blocks * rows, o_width + 2 * QDIM), BF16),
            pltpu.VMEM((blocks * rows, o_width), BF16),
            pltpu.SemaphoreType.DMA((1 + blocks,)),
            pltpu.VMEM((blocks * rows // KEYS, tall, KEYS), F32),
            pltpu.VMEM((tall, 128), F32),
            pltpu.VMEM((tall, 128), F32),
            pltpu.VMEM((tall, QDIM), F32),
        ],
        name="attend",
        cost_estimate=work(30),
    )(place, doc_lengths, qkv.reshape(blocks * rows, o_width + 2 * QDIM))
    own_states = call(
        scan_kernel,
        in_specs=[pl.BlockSpec(memory_space=pl.ANY)] * 2,
        out_specs=pl.BlockSpec(memory_space=pl.ANY),
        out_shape=jax.ShapeDtypeStruct((blocks, STATE, half + o_width), BF16),
        input_output_aliases={1: 0},
        scratch_shapes=[
            pltpu.VMEM((blocks, EXTRA, half), BF16),
            pltpu.VMEM((STATE // PIECE, blocks, PIECE, half), BF16),
            pltpu.VMEM((STATE // PIECE, blocks, PIECE, half), BF16),
            pltpu.SemaphoreType.DMA((STATE // PIECE,)),
            pltpu.SemaphoreType.DMA((STATE // PIECE,)),
            pltpu.SemaphoreType.DMA,
        ],
        name="scan",
        cost_estimate=work(4),
    )(own_fresh, attended)
    states = lax.all_to_all(own_states, "ctx", split_axis=0, concat_axis=0, tiled=True)

    mixer_out, attn_out = call(
        final_kernel,
        grid=(GROUPS,),
        in_specs=[pl.BlockSpec(memory_space=pl.ANY)] * 3
        + [
            pl.BlockSpec((rows, GROUPS * STATE), lambda g: (0, 0)),
            pl.BlockSpec((GROUPS, rows, 2 * PER_GROUP), lambda g: (0, 0, 0)),
            pl.BlockSpec((1, INNER), lambda g: (0, 0)),
        ],
        out_specs=[pl.BlockSpec(memory_space=pl.ANY)] * 2,
        out_shape=[
            jax.ShapeDtypeStruct((rows, INNER), BF16),
            jax.ShapeDtypeStruct((rows, QHEADS * QDIM), BF16),
        ],
        scratch_shapes=[
            pltpu.VMEM((GROUPS, rows, WIDTH), BF16),
            pltpu.VMEM((GROUPS, 2, STATE, half + o_width), BF16),
            pltpu.VMEM((GROUPS, rows, WIDTH), BF16),
            pltpu.VMEM((GROUPS, rows, WIDTH), BF16),
            pltpu.VMEM((2 * PER_GROUP, WIDTH), BF16),
            pltpu.VMEM((rows, WIDTH), F32),
            pltpu.VMEM((rows, WIDTH), F32),
            pltpu.SemaphoreType.DMA((6, GROUPS)),
        ],
        name="final",
        cost_estimate=work(7),
    )(local, states, z_gate[0], c_act, keep, norm_gain[None])
    return (mixer_out[None], attn_out[None])


def solution(mesh):
    placed = P("batch", "ctx", None)
    whole = P()
    return jax.shard_map(
        on_device,
        mesh=mesh,
        in_specs=(placed, placed, placed) + (whole,) * 6 + (placed,) * 3,
        out_specs=(placed, placed),
        check_vma=False,
    )
```

```python
import functools

import jax
import jax.numpy as jnp
from jax import lax
from jax.experimental import pallas as pl
from jax.experimental.pallas import tpu as pltpu
from jax.sharding import PartitionSpec as P

HEADS = 128
HEAD_DIM = 64
STATE = 128
GROUPS = 8
QHEADS = 32
KVHEADS = 8
QDIM = 128
CONV = 4
WINDOW = 2048

PER_GROUP = HEADS // GROUPS
WIDTH = PER_GROUP * HEAD_DIM
INNER = HEADS * HEAD_DIM
DOCS = 6
EPSILON = 1e-05
NEGATIVE = -1e30
LOG2E = 1.4426950408889634
EXTRA = 8
KEYS = 256
PIECE = 32
CHUNK = 16

F32 = jnp.float32
BF16 = jnp.bfloat16
HIGH = lax.Precision.HIGHEST


def dot(a, b, dims=(((1,), (0,)), ((), ())), precision=None):
    return lax.dot_general(a, b, dims, precision=precision, preferred_element_type=F32)


def doc_starts(place_ref, lengths_ref):
    seq = place_ref[1]
    starts = [jnp.int32(0)]
    for d in range(DOCS - 1):
        starts.append(starts[-1] + lengths_ref[seq, d])
    return starts


def row_starts(starts, pos):
    first = jnp.zeros_like(pos)
    for s in starts[1:]:
        first = jnp.where(pos >= s, s, first)
    return first


def scalar_start(starts, pos):
    first = jnp.int32(0)
    for s in starts[1:]:
        first = jnp.where(pos >= s, s, first)
    return first


def expand_heads(copies):
    shape = (copies * PER_GROUP, WIDTH)
    row = lax.broadcasted_iota(jnp.int32, shape, 0) % PER_GROUP
    lane = lax.broadcasted_iota(jnp.int32, shape, 1)
    return jnp.where(lane // HEAD_DIM == row, 1.0, 0.0).astype(BF16)


def halves(x):
    upper = x.astype(BF16)
    return upper, (x - upper.astype(F32)).astype(BF16)


def silu(x):
    return (0.5 * x) * (1.0 + jnp.tanh(0.5 * x))


def prep_kernel(place_ref, lengths_ref, step_ref, rate_ref, col_ref, row_ref, trail_ref, keep_ref, thr_ref):
    rows = step_ref.shape[0]
    base = place_ref[0] * rows
    starts = doc_starts(place_ref, lengths_ref)
    pos = base + lax.broadcasted_iota(jnp.int32, (rows, HEADS), 0)
    first = row_starts(starts, pos)
    last_first = scalar_start(starts, base + rows - 1)
    t = step_ref[...].astype(F32)
    dt = jnp.maximum(t, 0.0) + jnp.log1p(jnp.exp(-jnp.abs(t)))
    a = dt * rate_ref[...] * (-LOG2E)
    i = lax.broadcasted_iota(jnp.int32, (rows, rows), 0)
    j = lax.broadcasted_iota(jnp.int32, (rows, rows), 1)
    tri = (i >= j).astype(F32)
    cum = dot(tri, a, precision=HIGH)
    total = cum[rows - 1 : rows, :]
    trail = halves(jnp.where(first == last_first, jnp.exp2(total - cum) * dt, 0.0))
    keep = halves(jnp.where(first < base, jnp.exp2(cum), 0.0))
    thr = halves(jnp.where(last_first < base, jnp.exp2(total), 0.0))
    row8 = lax.broadcasted_iota(jnp.int32, (8, HEADS), 0)
    thr_rows = jnp.where(
        row8 == 0, thr[0].astype(F32), jnp.where(row8 == 1, thr[1].astype(F32), 0.0)
    ).astype(BF16)
    row_ref[...] = jnp.transpose(cum - jnp.log2(dt))
    for g in range(GROUPS):
        part = slice(g * PER_GROUP, (g + 1) * PER_GROUP)
        col_ref[g] = cum[:, part]
        trail_ref[g] = jnp.concatenate([trail[0][:, part], trail[1][:, part]], axis=1)
        keep_ref[g] = jnp.concatenate([keep[0][:, part], keep[1][:, part]], axis=1)
        thr_ref[g] = thr_rows[:, part]


def front_kernel(
    place_ref, lengths_ref, x_ref, b_ref, c_ref, hx_ref, hb_ref, hc_ref,
    wx_ref, wb_ref, wc_ref, ox_ref, ob_ref, oc_ref, trail_ref, thr_ref,
    xa_ref, ba_ref, ca_ref, f_ref, pad_ref,
):
    rows = x_ref.shape[0]
    base = place_ref[0] * rows
    starts = doc_starts(place_ref, lengths_ref)
    pos = base + lax.broadcasted_iota(jnp.int32, (rows, 128), 0)
    rel = pos - row_starts(starts, pos)
    masks = [None] + [rel >= d for d in range(1, CONV)]

    def conv(src, rim, weight, bias, dst, lo):
        at = slice(lo, lo + 128)
        pad_ref[0:8, :] = rim[:, at].astype(F32)
        pad_ref[8 : 8 + rows, :] = src[:, at].astype(F32)
        acc = pad_ref[8 : 8 + rows, :] * weight[3:4, at] + bias[:, at]
        for d in range(1, CONV):
            tap = pad_ref[8 - d : 8 - d + rows, :] * weight[3 - d : 4 - d, at]
            acc = acc + jnp.where(masks[d], tap, 0.0)
        dst[:, at] = silu(acc).astype(BF16)

    for lo in range(0, WIDTH, 128):
        conv(x_ref, hx_ref, wx_ref, ox_ref, xa_ref, lo)
    conv(b_ref, hb_ref, wb_ref, ob_ref, ba_ref, 0)
    conv(c_ref, hc_ref, wc_ref, oc_ref, ca_ref, 0)

    scale = dot(trail_ref[0], expand_heads(2))
    weighted = (xa_ref[...].astype(F32) * scale).astype(BF16)
    fresh = dot(ba_ref[...], weighted, (((0,), (0,)), ((), ()))).astype(BF16)
    extra = dot(thr_ref[0], expand_heads(1)).astype(BF16)
    half = WIDTH // 2
    for k in range(2):
        f_ref[k, 0:STATE, :] = fresh[:, k * half : (k + 1) * half]
        f_ref[k, STATE : STATE + EXTRA, :] = extra[:, k * half : (k + 1) * half]


def inner_kernel(place_ref, lengths_ref, xa_ref, ba_ref, ca_ref, col_ref, row_ref, skip_ref, y_ref):
    rows = xa_ref.shape[0]
    base = place_ref[0] * rows
    starts = doc_starts(place_ref, lengths_ref)
    i = base + lax.broadcasted_iota(jnp.int32, (rows, rows), 0)
    j = base + lax.broadcasted_iota(jnp.int32, (rows, rows), 1)
    first = row_starts(starts, i)
    blocked = jnp.where((j <= i) & (j >= first), 0.0, NEGATIVE)
    scores = dot(ca_ref[...], ba_ref[...], (((1,), (1,)), ((), ())))
    lane = lax.broadcasted_iota(jnp.int32, (rows, 128), 1)
    col = col_ref[0]
    for p in range(PER_GROUP // 2):
        weights = []
        for h in (2 * p, 2 * p + 1):
            spread = (col[:, h : h + 1] + blocked) - row_ref[h : h + 1, :]
            weights.append((scores * jnp.exp2(spread)).astype(BF16))
        at = slice(p * 128, (p + 1) * 128)
        x = xa_ref[:, at]
        zero = jnp.zeros_like(x)
        both = jnp.concatenate(
            [jnp.where(lane < HEAD_DIM, x, zero), jnp.where(lane < HEAD_DIM, zero, x)], axis=0
        )
        y = dot(jnp.concatenate(weights, axis=1), both)
        y_ref[:, at] = (y + x.astype(F32) * skip_ref[:, at]).astype(BF16)


def scan_kernel(f_ref, held_out_ref, out_ref, tail_ref, held_ref, state_ref, sems, out_sems, tail_sem):
    blocks, _, width = f_ref.shape
    pieces, _, piece, _ = held_ref.shape
    tail = pltpu.make_async_copy(f_ref.at[:, pl.ds(STATE, EXTRA), :], tail_ref, tail_sem)
    loads = [
        pltpu.make_async_copy(f_ref.at[:, pl.ds(q * piece, piece), :], held_ref.at[q], sems.at[q])
        for q in range(pieces)
    ]
    stores = [
        pltpu.make_async_copy(
            state_ref.at[q], out_ref.at[:, pl.ds(q * piece, piece), pl.ds(0, width)], out_sems.at[q]
        )
        for q in range(pieces)
    ]
    tail.start()
    for load in loads:
        load.start()
    tail.wait()
    for q in range(pieces):
        loads[q].wait()
        state = jnp.zeros((piece, width), F32)
        for r in range(blocks):
            state_ref[q, r] = state.astype(BF16)
            if r + 1 < blocks:
                ends = tail_ref[r].astype(F32)
                state = state * (ends[0:1, :] + ends[1:2, :]) + held_ref[q, r].astype(F32)
        stores[q].start()
    for store in stores:
        store.wait()


def final_kernel(
    y_far, s_far, z_far, ca_far, keep_far, gain_far, o_far, attn_far,
    y_ref, s_ref, z_ref, o_ref, ca_ref, keep_ref, gain_ref, scale_ref, even_ref, odd_ref, square_ref, sems,
):
    rows = y_far.shape[0]
    half = WIDTH // 2
    own = s_ref.shape[3] - half
    small = (
        pltpu.make_async_copy(keep_far, keep_ref, sems.at[6, 0]),
        pltpu.make_async_copy(ca_far, ca_ref, sems.at[6, 1]),
        pltpu.make_async_copy(gain_far, gain_ref, sems.at[6, 2]),
    )
    loads, stores = [], []
    for g in range(GROUPS):
        cols = pl.ds(g * WIDTH, WIDTH)
        loads.append((
            pltpu.make_async_copy(s_far.at[pl.ds(2 * g, 2)], s_ref.at[g], sems.at[0, g]),
            pltpu.make_async_copy(y_far.at[:, cols], y_ref.at[g], sems.at[1, g]),
            pltpu.make_async_copy(z_far.at[:, cols], z_ref.at[g], sems.at[2, g]),
        ))
        stores.append([pltpu.make_async_copy(o_ref.at[g], o_far.at[:, cols], sems.at[3, g])])
        for k in range(2):
            source = s_ref.at[g, k, :, pl.ds(half, own)]
            target = attn_far.at[:, pl.ds((2 * g + k) * own, own)]
            stores[g].append(pltpu.make_async_copy(source, target, sems.at[4 + k, g]))
    for copy in small:
        copy.start()
    for group in loads:
        for copy in group:
            copy.start()
    spread = expand_heads(2)
    for copy in small:
        copy.wait()
    for g in range(GROUPS):
        scale_ref[g] = dot(keep_ref[g], spread)

    def carry(g, into_ref):
        loads[g][0].wait()
        for copy in stores[g][1:]:
            copy.start()
        ca = ca_ref[:, g * STATE : (g + 1) * STATE]
        for k in range(2):
            into_ref[:, k * half : (k + 1) * half] = dot(ca, s_ref[g, k, :, :half])

    carry(0, even_ref)
    for g in range(GROUPS):
        here_ref, next_ref = (even_ref, odd_ref) if g % 2 == 0 else (odd_ref, even_ref)
        if g + 1 < GROUPS:
            carry(g + 1, next_ref)
        for copy in loads[g][1:]:
            copy.wait()
        for lo in range(0, rows, CHUNK):
            at = slice(lo, lo + CHUNK)
            mixed = (y_ref[g, at, :].astype(F32) + scale_ref[g, at, :] * here_ref[at, :]).astype(BF16).astype(F32)
            gated = mixed * silu(z_ref[g, at, :].astype(F32))
            here_ref[at, :] = gated
            total = gated[:, :128] * gated[:, :128]
            for c in range(128, WIDTH, 128):
                total = total + gated[:, c : c + 128] * gated[:, c : c + 128]
            square_ref[at, :] = total
        mean = jnp.sum(square_ref[...], axis=1, keepdims=True) * (1.0 / WIDTH)
        square_ref[...] = jnp.broadcast_to(lax.rsqrt(mean + EPSILON), square_ref.shape)
        for lo in range(0, rows, CHUNK):
            at = slice(lo, lo + CHUNK)
            factor = square_ref[at, :]
            for c in range(0, WIDTH, 128):
                gain = gain_ref[:, g * WIDTH + c : g * WIDTH + c + 128]
                o_ref[g, at, c : c + 128] = (here_ref[at, c : c + 128] * factor * gain).astype(BF16)
        stores[g][0].start()
    for group in stores:
        for copy in group:
            copy.wait()


def pack_kernel(q_ref, k_ref, v_ref, out_ref, held_ref, sems):
    parts = out_ref.shape[0]
    width = q_ref.shape[1] // parts
    loads, stores = [], []
    for d in range(parts):
        at = pl.ds(d * KVHEADS // parts * QDIM, QDIM)
        q_cols = pl.ds(d * width, width)
        loads += [
            pltpu.make_async_copy(q_ref.at[:, q_cols], held_ref.at[d, :, pl.ds(0, width)], sems.at[0, d]),
            pltpu.make_async_copy(k_ref.at[:, at], held_ref.at[d, :, pl.ds(width, QDIM)], sems.at[1, d]),
            pltpu.make_async_copy(v_ref.at[:, at], held_ref.at[d, :, pl.ds(width + QDIM, QDIM)], sems.at[2, d]),
        ]
        stores.append(pltpu.make_async_copy(held_ref.at[d], out_ref.at[d], sems.at[3, d]))
    for load in loads:
        load.start()
    for d in range(parts):
        for load in loads[3 * d : 3 * d + 3]:
            load.wait()
        stores[d].start()
    for store in stores:
        store.wait()


def attend_kernel(place_ref, lengths_ref, far_ref, out_ref, qkv_ref, o_ref, sems, s_ref, m_ref, l_ref, acc_ref):
    copy = pltpu.make_async_copy(far_ref, qkv_ref, sems.at[0])
    copy.start()
    copy.wait()
    length = qkv_ref.shape[0]
    q_width = qkv_ref.shape[1] - 2 * QDIM
    heads = q_width // QDIM
    k_cols, v_cols = slice(q_width, q_width + QDIM), slice(q_width + QDIM, q_width + 2 * QDIM)
    starts = doc_starts(place_ref, lengths_ref)
    lane = lax.broadcasted_iota(jnp.int32, (KEYS, KEYS), 1)
    scaling = QDIM ** (-0.5) * LOG2E

    def one_tile(t, outer):
        base = t * KEYS
        here = pl.ds(pl.multiple_of(base, KEYS), KEYS)
        pos = base + lax.broadcasted_iota(jnp.int32, (KEYS, KEYS), 0)
        first = jnp.maximum(row_starts(starts, pos), pos - (WINDOW - 1))
        last = base + KEYS - 1
        lowest = jnp.maximum(scalar_start(starts, base), base - (WINDOW - 1))
        highest = jnp.maximum(scalar_start(starts, last), last - (WINDOW - 1))
        begin = lowest // KEYS
        clear = jnp.minimum((highest + KEYS - 1) // KEYS, t)
        queries = jnp.concatenate([qkv_ref[here, h * QDIM : (h + 1) * QDIM] for h in range(heads)], axis=0)
        m_ref[...] = jnp.full_like(m_ref, NEGATIVE)

        def score(masked, j, carry):
            k = qkv_ref[pl.ds(pl.multiple_of(j * KEYS, KEYS), KEYS), k_cols]
            s = dot(queries, k, (((1,), (1,)), ((), ())))
            if masked:
                key = j * KEYS + lane
                visible = (key <= pos) & (key >= first)
            for h in range(heads):
                at = slice(h * KEYS, (h + 1) * KEYS)
                part = s[at]
                if masked:
                    part = jnp.where(visible, part, NEGATIVE)
                s_ref[j, at, :] = part
                top = m_ref[at, :]
                for c in range(0, KEYS, 128):
                    top = jnp.maximum(top, part[:, c : c + 128])
                m_ref[at, :] = top
            return carry

        lax.fori_loop(begin, clear, functools.partial(score, True), 0)
        lax.fori_loop(clear, t, functools.partial(score, False), 0)
        score(True, t, 0)
        m_ref[...] = jnp.broadcast_to(jnp.max(m_ref[...], axis=1, keepdims=True), m_ref.shape)
        l_ref[...] = jnp.zeros_like(l_ref)
        acc_ref[...] = jnp.zeros_like(acc_ref)

        def gather(j, carry):
            v = qkv_ref[pl.ds(pl.multiple_of(j * KEYS, KEYS), KEYS), v_cols]
            numerators = []
            for h in range(heads):
                at = slice(h * KEYS, (h + 1) * KEYS)
                top = m_ref[at, :]
                total = l_ref[at, :]
                parts = []
                for c in range(0, KEYS, 128):
                    p = jnp.exp2((s_ref[j, at, c : c + 128] - top) * scaling)
                    total = total + p
                    parts.append(p.astype(BF16))
                l_ref[at, :] = total
                numerators.append(jnp.concatenate(parts, axis=1))
            acc_ref[...] += dot(jnp.concatenate(numerators, axis=0), v)
            return carry

        lax.fori_loop(begin, t + 1, gather, 0)
        for h in range(heads):
            at = slice(h * KEYS, (h + 1) * KEYS)
            total = jnp.sum(l_ref[at, :], axis=1, keepdims=True)
            o_ref[here, h * QDIM : (h + 1) * QDIM] = (acc_ref[at, :] / total).astype(BF16)
        return outer

    lax.fori_loop(0, length // KEYS, one_tile, 0)
    blocks, rows, out_width = out_ref.shape
    sends = [
        pltpu.make_async_copy(
            o_ref.at[pl.ds(r * rows, rows), :],
            out_ref.at[r, :, pl.ds(out_width - q_width, q_width)],
            sems.at[1 + r],
        )
        for r in range(blocks)
    ]
    for send in sends:
        send.start()
    for send in sends:
        send.wait()


def work(microseconds):
    return pl.CostEstimate(flops=0, transcendentals=0, bytes_accessed=int(microseconds * 3.5e6))


def smem():
    return pl.BlockSpec(memory_space=pltpu.SMEM)


def on_device(
    mixer_input, z_gate, time_step, conv_weight, conv_bias, decay_rate, skip_gain,
    norm_gain, doc_lengths, queries, attn_keys, attn_values,
):
    rows = mixer_input.shape[1]
    blocks = lax.axis_size("ctx")
    place = jnp.stack([lax.axis_index("ctx"), lax.axis_index("batch")]).astype(jnp.int32)
    raw = mixer_input[0]
    call = functools.partial(
        pl.pallas_call, compiler_params=pltpu.CompilerParams(vmem_limit_bytes=63 << 20)
    )

    o_width = QHEADS * QDIM // blocks
    qkv = call(
        pack_kernel,
        in_specs=[pl.BlockSpec(memory_space=pl.ANY)] * 3,
        out_specs=pl.BlockSpec(memory_space=pl.ANY),
        scratch_shapes=[
            pltpu.VMEM((blocks, rows, o_width + 2 * QDIM), BF16),
            pltpu.SemaphoreType.DMA((4, blocks)),
        ],
        out_shape=jax.ShapeDtypeStruct((blocks, rows, o_width + 2 * QDIM), BF16),
        name="pack",
        cost_estimate=work(3),
    )(queries[0], attn_keys[0], attn_values[0])
    rim = lax.ppermute(raw[rows - 8 :], "ctx", [(r, r + 1) for r in range(blocks - 1)])
    rim, qkv = lax.optimization_barrier((rim, qkv))
    qkv = lax.all_to_all(qkv, "ctx", split_axis=0, concat_axis=0, tiled=True)

    col, row, trail, keep, thr = call(
        prep_kernel,
        in_specs=[smem(), smem(), pl.BlockSpec(), pl.BlockSpec()],
        out_shape=[
            jax.ShapeDtypeStruct((GROUPS, rows, PER_GROUP), F32),
            jax.ShapeDtypeStruct((HEADS, rows), F32),
            jax.ShapeDtypeStruct((GROUPS, rows, 2 * PER_GROUP), BF16),
            jax.ShapeDtypeStruct((GROUPS, rows, 2 * PER_GROUP), BF16),
            jax.ShapeDtypeStruct((GROUPS, 8, PER_GROUP), BF16),
        ],
        name="prep",
        cost_estimate=work(3),
    )(place, doc_lengths, time_step[0], decay_rate[None])

    wide = lambda n: pl.BlockSpec((n, WIDTH), lambda g: (0, g))
    b_cols = lambda n: pl.BlockSpec((n, STATE), lambda g: (0, INNER // STATE + g))
    c_cols = lambda n: pl.BlockSpec((n, STATE), lambda g: (0, INNER // STATE + GROUPS + g))
    group_cols = lambda n: pl.BlockSpec((n, STATE), lambda g: (0, g))
    per_group = pl.BlockSpec((1, rows, PER_GROUP), lambda g: (g, 0, 0))
    per_group_two = pl.BlockSpec((1, rows, 2 * PER_GROUP), lambda g: (g, 0, 0))
    bias = conv_bias[None]
    half = WIDTH // 2
    x_act, b_act, c_act, fresh = call(
        front_kernel,
        grid=(GROUPS,),
        in_specs=[
            smem(), smem(),
            wide(rows), b_cols(rows), c_cols(rows),
            wide(8), b_cols(8), c_cols(8),
            wide(CONV), b_cols(CONV), c_cols(CONV),
            wide(1), b_cols(1), c_cols(1),
            per_group_two, pl.BlockSpec((1, 8, PER_GROUP), lambda g: (g, 0, 0)),
        ],
        out_specs=[
            wide(rows), group_cols(rows), group_cols(rows),
            pl.BlockSpec((2, STATE + EXTRA, half), lambda g: (g, 0, 0)),
        ],
        out_shape=[
            jax.ShapeDtypeStruct((rows, INNER), BF16),
            jax.ShapeDtypeStruct((rows, GROUPS * STATE), BF16),
            jax.ShapeDtypeStruct((rows, GROUPS * STATE), BF16),
            jax.ShapeDtypeStruct((2 * GROUPS, STATE + EXTRA, half), BF16),
        ],
        scratch_shapes=[pltpu.VMEM((8 + rows, 128), F32)],
        name="front",
        cost_estimate=work(40),
    )(
        place, doc_lengths, raw, raw, raw, rim, rim, rim,
        conv_weight, conv_weight, conv_weight, bias, bias, bias, trail, thr,
    )

    local = call(
        inner_kernel,
        grid=(GROUPS,),
        in_specs=[
            smem(), smem(), wide(rows), group_cols(rows), group_cols(rows), per_group,
            pl.BlockSpec((PER_GROUP, rows), lambda g: (g, 0)), wide(1),
        ],
        out_specs=wide(rows),
        out_shape=jax.ShapeDtypeStruct((rows, INNER), BF16),
        name="inner",
        cost_estimate=work(9),
    )(place, doc_lengths, x_act, b_act, c_act, col, row, jnp.repeat(skip_gain, HEAD_DIM)[None])

    fresh, qkv, local = lax.optimization_barrier((fresh, qkv, local))
    own_fresh = lax.all_to_all(fresh, "ctx", split_axis=0, concat_axis=0, tiled=True)

    tall = o_width // QDIM * KEYS
    attended = call(
        attend_kernel,
        in_specs=[smem(), smem(), pl.BlockSpec(memory_space=pl.ANY)],
        out_specs=pl.BlockSpec(memory_space=pl.ANY),
        out_shape=jax.ShapeDtypeStruct((blocks, rows, half + o_width), BF16),
        scratch_shapes=[
            pltpu.VMEM((blocks * rows, o_width + 2 * QDIM), BF16),
            pltpu.VMEM((blocks * rows, o_width), BF16),
            pltpu.SemaphoreType.DMA((1 + blocks,)),
            pltpu.VMEM((blocks * rows // KEYS, tall, KEYS), F32),
            pltpu.VMEM((tall, 128), F32),
            pltpu.VMEM((tall, 128), F32),
            pltpu.VMEM((tall, QDIM), F32),
        ],
        name="attend",
        cost_estimate=work(30),
    )(place, doc_lengths, qkv.reshape(blocks * rows, o_width + 2 * QDIM))
    own_states = call(
        scan_kernel,
        in_specs=[pl.BlockSpec(memory_space=pl.ANY)] * 2,
        out_specs=pl.BlockSpec(memory_space=pl.ANY),
        out_shape=jax.ShapeDtypeStruct((blocks, STATE, half + o_width), BF16),
        input_output_aliases={1: 0},
        scratch_shapes=[
            pltpu.VMEM((blocks, EXTRA, half), BF16),
            pltpu.VMEM((STATE // PIECE, blocks, PIECE, half), BF16),
            pltpu.VMEM((STATE // PIECE, blocks, PIECE, half), BF16),
            pltpu.SemaphoreType.DMA((STATE // PIECE,)),
            pltpu.SemaphoreType.DMA((STATE // PIECE,)),
            pltpu.SemaphoreType.DMA,
        ],
        name="scan",
        cost_estimate=work(4),
    )(own_fresh, attended)
    states = lax.all_to_all(own_states, "ctx", split_axis=0, concat_axis=0, tiled=True)

    mixer_out, attn_out = call(
        final_kernel,
        in_specs=[pl.BlockSpec(memory_space=pl.ANY)] * 6,
        out_specs=[pl.BlockSpec(memory_space=pl.ANY)] * 2,
        out_shape=[
            jax.ShapeDtypeStruct((rows, INNER), BF16),
            jax.ShapeDtypeStruct((rows, QHEADS * QDIM), BF16),
        ],
        scratch_shapes=[
            pltpu.VMEM((GROUPS, rows, WIDTH), BF16),
            pltpu.VMEM((GROUPS, 2, STATE, half + o_width), BF16),
            pltpu.VMEM((GROUPS, rows, WIDTH), BF16),
            pltpu.VMEM((GROUPS, rows, WIDTH), BF16),
            pltpu.VMEM((rows, GROUPS * STATE), BF16),
            pltpu.VMEM((GROUPS, rows, 2 * PER_GROUP), BF16),
            pltpu.VMEM((1, INNER), F32),
            pltpu.VMEM((GROUPS, rows, WIDTH), F32),
            pltpu.VMEM((rows, WIDTH), F32),
            pltpu.VMEM((rows, WIDTH), F32),
            pltpu.VMEM((rows, 128), F32),
            pltpu.SemaphoreType.DMA((7, GROUPS)),
        ],
        name="final",
        cost_estimate=work(7),
    )(local, states, z_gate[0], c_act, keep, norm_gain[None])
    return (mixer_out[None], attn_out[None])


def solution(mesh):
    placed = P("batch", "ctx", None)
    whole = P()
    return jax.shard_map(
        on_device,
        mesh=mesh,
        in_specs=(placed, placed, placed) + (whole,) * 6 + (placed,) * 3,
        out_specs=(placed, placed),
        check_vma=False,
    )
```

```python
import functools

import jax
import jax.numpy as jnp
from jax import lax
from jax.experimental import pallas as pl
from jax.experimental.pallas import tpu as pltpu
from jax.sharding import PartitionSpec as P

HEADS = 128
HEAD_DIM = 64
STATE = 128
GROUPS = 8
QHEADS = 32
KVHEADS = 8
QDIM = 128
CONV = 4
WINDOW = 2048

PER_GROUP = HEADS // GROUPS
WIDTH = PER_GROUP * HEAD_DIM
INNER = HEADS * HEAD_DIM
DOCS = 6
EPSILON = 1e-05
NEGATIVE = -1e30
LOG2E = 1.4426950408889634
EXTRA = 8
KEYS = 256
PIECE = 32
CHUNK = 16
RIM = 4

F32 = jnp.float32
BF16 = jnp.bfloat16
HIGH = lax.Precision.HIGHEST


def dot(a, b, dims=(((1,), (0,)), ((), ())), precision=None):
    return lax.dot_general(a, b, dims, precision=precision, preferred_element_type=F32)


def doc_starts(place_ref, lengths_ref):
    seq = place_ref[1]
    starts = [jnp.int32(0)]
    for d in range(DOCS - 1):
        starts.append(starts[-1] + lengths_ref[seq, d])
    return starts


def row_starts(starts, pos):
    first = jnp.zeros_like(pos)
    for s in starts[1:]:
        first = jnp.where(pos >= s, s, first)
    return first


def scalar_start(starts, pos):
    first = jnp.int32(0)
    for s in starts[1:]:
        first = jnp.where(pos >= s, s, first)
    return first


def expand_heads(copies):
    shape = (copies * PER_GROUP, WIDTH)
    row = lax.broadcasted_iota(jnp.int32, shape, 0) % PER_GROUP
    lane = lax.broadcasted_iota(jnp.int32, shape, 1)
    return jnp.where(lane // HEAD_DIM == row, 1.0, 0.0).astype(BF16)


def halves(x):
    upper = x.astype(BF16)
    return upper, (x - upper.astype(F32)).astype(BF16)


def silu(x):
    return (0.5 * x) * (1.0 + jnp.tanh(0.5 * x))


def prep_kernel(place_ref, lengths_ref, step_ref, rate_ref, col_ref, row_ref, trail_ref, keep_ref, thr_ref):
    rows = step_ref.shape[0]
    base = place_ref[0] * rows
    starts = doc_starts(place_ref, lengths_ref)
    pos = base + lax.broadcasted_iota(jnp.int32, (rows, HEADS), 0)
    first = row_starts(starts, pos)
    last_first = scalar_start(starts, base + rows - 1)
    t = step_ref[...].astype(F32)
    dt = jnp.maximum(t, 0.0) + jnp.log1p(jnp.exp(-jnp.abs(t)))
    a = dt * rate_ref[...] * (-LOG2E)
    i = lax.broadcasted_iota(jnp.int32, (rows, rows), 0)
    j = lax.broadcasted_iota(jnp.int32, (rows, rows), 1)
    tri = (i >= j).astype(F32)
    cum = dot(tri, a, precision=HIGH)
    total = cum[rows - 1 : rows, :]
    trail = halves(jnp.where(first == last_first, jnp.exp2(total - cum) * dt, 0.0))
    keep = halves(jnp.where(first < base, jnp.exp2(cum), 0.0))
    thr = halves(jnp.where(last_first < base, jnp.exp2(total), 0.0))
    row8 = lax.broadcasted_iota(jnp.int32, (8, HEADS), 0)
    thr_rows = jnp.where(
        row8 == 0, thr[0].astype(F32), jnp.where(row8 == 1, thr[1].astype(F32), 0.0)
    ).astype(BF16)
    row_ref[...] = jnp.transpose(cum - jnp.log2(dt))
    for g in range(GROUPS):
        part = slice(g * PER_GROUP, (g + 1) * PER_GROUP)
        col_ref[g] = cum[:, part]
        trail_ref[g] = jnp.concatenate([trail[0][:, part], trail[1][:, part]], axis=1)
        keep_ref[g] = jnp.concatenate([keep[0][:, part], keep[1][:, part]], axis=1)
        thr_ref[g] = thr_rows[:, part]


def front_kernel(
    place_ref, lengths_ref, x_ref, b_ref, c_ref, hx_ref, hb_ref, hc_ref,
    wx_ref, wb_ref, wc_ref, ox_ref, ob_ref, oc_ref, trail_ref, thr_ref,
    xa_ref, ba_ref, ca_ref, f_ref, pad_ref,
):
    rows = x_ref.shape[0]
    base = place_ref[0] * rows
    starts = doc_starts(place_ref, lengths_ref)
    pos = base + lax.broadcasted_iota(jnp.int32, (rows, 128), 0)
    rel = pos - row_starts(starts, pos)
    masks = [None] + [rel >= d for d in range(1, CONV)]

    def conv(src, rim, weight, bias, dst, lo):
        at = slice(lo, lo + 128)
        pad_ref[8 - RIM : 8, :] = rim[:, at].astype(F32)
        pad_ref[8 : 8 + rows, :] = src[:, at].astype(F32)
        acc = pad_ref[8 : 8 + rows, :] * weight[3:4, at] + bias[:, at]
        for d in range(1, CONV):
            tap = pad_ref[8 - d : 8 - d + rows, :] * weight[3 - d : 4 - d, at]
            acc = acc + jnp.where(masks[d], tap, 0.0)
        dst[:, at] = silu(acc).astype(BF16)

    for lo in range(0, WIDTH, 128):
        conv(x_ref, hx_ref, wx_ref, ox_ref, xa_ref, lo)
    conv(b_ref, hb_ref, wb_ref, ob_ref, ba_ref, 0)
    conv(c_ref, hc_ref, wc_ref, oc_ref, ca_ref, 0)

    scale = dot(trail_ref[0], expand_heads(2))
    weighted = (xa_ref[...].astype(F32) * scale).astype(BF16)
    fresh = dot(ba_ref[...], weighted, (((0,), (0,)), ((), ()))).astype(BF16)
    extra = dot(thr_ref[0], expand_heads(1)).astype(BF16)
    half = WIDTH // 2
    for k in range(2):
        f_ref[k, 0:STATE, :] = fresh[:, k * half : (k + 1) * half]
        f_ref[k, STATE : STATE + EXTRA, :] = extra[:, k * half : (k + 1) * half]


def inner_kernel(place_ref, lengths_ref, xa_ref, ba_ref, ca_ref, col_ref, row_ref, skip_ref, y_ref):
    rows = xa_ref.shape[0]
    base = place_ref[0] * rows
    starts = doc_starts(place_ref, lengths_ref)
    i = base + lax.broadcasted_iota(jnp.int32, (rows, rows), 0)
    j = base + lax.broadcasted_iota(jnp.int32, (rows, rows), 1)
    first = row_starts(starts, i)
    blocked = jnp.where((j <= i) & (j >= first), 0.0, NEGATIVE)
    scores = dot(ca_ref[...], ba_ref[...], (((1,), (1,)), ((), ())))
    lane = lax.broadcasted_iota(jnp.int32, (rows, 128), 1)
    col = col_ref[0]
    for p in range(PER_GROUP // 2):
        weights = []
        for h in (2 * p, 2 * p + 1):
            spread = (col[:, h : h + 1] + blocked) - row_ref[h : h + 1, :]
            weights.append((scores * jnp.exp2(spread)).astype(BF16))
        at = slice(p * 128, (p + 1) * 128)
        x = xa_ref[:, at]
        zero = jnp.zeros_like(x)
        both = jnp.concatenate(
            [jnp.where(lane < HEAD_DIM, x, zero), jnp.where(lane < HEAD_DIM, zero, x)], axis=0
        )
        y = dot(jnp.concatenate(weights, axis=1), both)
        y_ref[:, at] = (y + x.astype(F32) * skip_ref[:, at]).astype(BF16)


def scan_kernel(f_ref, held_out_ref, out_ref, tail_ref, held_ref, state_ref, sems, out_sems, tail_sem):
    blocks, _, width = f_ref.shape
    pieces, _, piece, _ = held_ref.shape
    tail = pltpu.make_async_copy(f_ref.at[:, pl.ds(STATE, EXTRA), :], tail_ref, tail_sem)
    loads = [
        pltpu.make_async_copy(f_ref.at[:, pl.ds(q * piece, piece), :], held_ref.at[q], sems.at[q])
        for q in range(pieces)
    ]
    stores = [
        pltpu.make_async_copy(
            state_ref.at[q], out_ref.at[:, pl.ds(q * piece, piece), pl.ds(0, width)], out_sems.at[q]
        )
        for q in range(pieces)
    ]
    tail.start()
    for load in loads:
        load.start()
    tail.wait()
    for q in range(pieces):
        loads[q].wait()
        state = jnp.zeros((piece, width), F32)
        for r in range(blocks):
            state_ref[q, r] = state.astype(BF16)
            if r + 1 < blocks:
                ends = tail_ref[r].astype(F32)
                state = state * (ends[0:1, :] + ends[1:2, :]) + held_ref[q, r].astype(F32)
        stores[q].start()
    for store in stores:
        store.wait()


def final_kernel(
    y_far, s_far, z_far, ca_far, keep_far, gain_far, o_far, attn_far,
    y_ref, s_ref, z_ref, o_ref, ca_ref, keep_ref, gain_ref, scale_ref, even_ref, odd_ref, square_ref, sems,
):
    rows = y_far.shape[0]
    half = WIDTH // 2
    own = s_ref.shape[3] - half
    small = (
        pltpu.make_async_copy(keep_far, keep_ref, sems.at[6, 0]),
        pltpu.make_async_copy(ca_far, ca_ref, sems.at[6, 1]),
        pltpu.make_async_copy(gain_far, gain_ref, sems.at[6, 2]),
    )
    loads, stores = [], []
    for g in range(GROUPS):
        cols = pl.ds(g * WIDTH, WIDTH)
        loads.append((
            pltpu.make_async_copy(s_far.at[pl.ds(2 * g, 2)], s_ref.at[g], sems.at[0, g]),
            pltpu.make_async_copy(y_far.at[:, cols], y_ref.at[g], sems.at[1, g]),
            pltpu.make_async_copy(z_far.at[:, cols], z_ref.at[g], sems.at[2, g]),
        ))
        stores.append([pltpu.make_async_copy(o_ref.at[g], o_far.at[:, cols], sems.at[3, g])])
        for k in range(2):
            source = s_ref.at[g, k, :, pl.ds(half, own)]
            target = attn_far.at[:, pl.ds((2 * g + k) * own, own)]
            stores[g].append(pltpu.make_async_copy(source, target, sems.at[4 + k, g]))
    for copy in small:
        copy.start()
    for group in loads:
        for copy in group:
            copy.start()
    spread = expand_heads(2)
    for copy in small:
        copy.wait()
    for g in range(GROUPS):
        scale_ref[g] = dot(keep_ref[g], spread)

    def carry(g, into_ref):
        loads[g][0].wait()
        for copy in stores[g][1:]:
            copy.start()
        ca = ca_ref[:, g * STATE : (g + 1) * STATE]
        for k in range(2):
            into_ref[:, k * half : (k + 1) * half] = dot(ca, s_ref[g, k, :, :half])

    carry(0, even_ref)
    for g in range(GROUPS):
        here_ref, next_ref = (even_ref, odd_ref) if g % 2 == 0 else (odd_ref, even_ref)
        if g + 1 < GROUPS:
            carry(g + 1, next_ref)
        for copy in loads[g][1:]:
            copy.wait()
        for lo in range(0, rows, CHUNK):
            at = slice(lo, lo + CHUNK)
            mixed = (y_ref[g, at, :].astype(F32) + scale_ref[g, at, :] * here_ref[at, :]).astype(BF16).astype(F32)
            gated = mixed * silu(z_ref[g, at, :].astype(F32))
            here_ref[at, :] = gated
            total = gated[:, :128] * gated[:, :128]
            for c in range(128, WIDTH, 128):
                total = total + gated[:, c : c + 128] * gated[:, c : c + 128]
            square_ref[at, :] = total
        mean = jnp.sum(square_ref[...], axis=1, keepdims=True) * (1.0 / WIDTH)
        square_ref[...] = jnp.broadcast_to(lax.rsqrt(mean + EPSILON), square_ref.shape)
        for lo in range(0, rows, CHUNK):
            at = slice(lo, lo + CHUNK)
            factor = square_ref[at, :]
            for c in range(0, WIDTH, 128):
                gain = gain_ref[:, g * WIDTH + c : g * WIDTH + c + 128]
                o_ref[g, at, c : c + 128] = (here_ref[at, c : c + 128] * factor * gain).astype(BF16)
        stores[g][0].start()
    for group in stores:
        for copy in group:
            copy.wait()


def pack_kernel(q_ref, k_ref, v_ref, out_ref, held_ref, sems):
    parts = out_ref.shape[0]
    width = q_ref.shape[1] // parts
    loads, stores = [], []
    for d in range(parts):
        at = pl.ds(d * KVHEADS // parts * QDIM, QDIM)
        q_cols = pl.ds(d * width, width)
        loads += [
            pltpu.make_async_copy(q_ref.at[:, q_cols], held_ref.at[d, :, pl.ds(0, width)], sems.at[0, d]),
            pltpu.make_async_copy(k_ref.at[:, at], held_ref.at[d, :, pl.ds(width, QDIM)], sems.at[1, d]),
            pltpu.make_async_copy(v_ref.at[:, at], held_ref.at[d, :, pl.ds(width + QDIM, QDIM)], sems.at[2, d]),
        ]
        stores.append(pltpu.make_async_copy(held_ref.at[d], out_ref.at[d], sems.at[3, d]))
    for load in loads:
        load.start()
    for d in range(parts):
        for load in loads[3 * d : 3 * d + 3]:
            load.wait()
        stores[d].start()
    for store in stores:
        store.wait()


def attend_kernel(place_ref, lengths_ref, far_ref, out_ref, qkv_ref, o_ref, sems, s_ref, m_ref, l_ref, acc_ref):
    copy = pltpu.make_async_copy(far_ref, qkv_ref, sems.at[0])
    copy.start()
    copy.wait()
    length = qkv_ref.shape[0]
    q_width = qkv_ref.shape[1] - 2 * QDIM
    heads = q_width // QDIM
    k_cols, v_cols = slice(q_width, q_width + QDIM), slice(q_width + QDIM, q_width + 2 * QDIM)
    starts = doc_starts(place_ref, lengths_ref)
    lane = lax.broadcasted_iota(jnp.int32, (KEYS, KEYS), 1)
    scaling = QDIM ** (-0.5) * LOG2E

    def one_tile(t, outer):
        base = t * KEYS
        here = pl.ds(pl.multiple_of(base, KEYS), KEYS)
        pos = base + lax.broadcasted_iota(jnp.int32, (KEYS, KEYS), 0)
        first = jnp.maximum(row_starts(starts, pos), pos - (WINDOW - 1))
        last = base + KEYS - 1
        lowest = jnp.maximum(scalar_start(starts, base), base - (WINDOW - 1))
        highest = jnp.maximum(scalar_start(starts, last), last - (WINDOW - 1))
        begin = lowest // KEYS
        clear = jnp.minimum((highest + KEYS - 1) // KEYS, t)
        queries = jnp.concatenate([qkv_ref[here, h * QDIM : (h + 1) * QDIM] for h in range(heads)], axis=0)
        m_ref[...] = jnp.full_like(m_ref, NEGATIVE)

        def score(masked, j, carry):
            k = qkv_ref[pl.ds(pl.multiple_of(j * KEYS, KEYS), KEYS), k_cols]
            s = dot(queries, k, (((1,), (1,)), ((), ())))
            if masked:
                key = j * KEYS + lane
                visible = (key <= pos) & (key >= first)
            for h in range(heads):
                at = slice(h * KEYS, (h + 1) * KEYS)
                part = s[at]
                if masked:
                    part = jnp.where(visible, part, NEGATIVE)
                s_ref[j, at, :] = part
                top = m_ref[at, :]
                for c in range(0, KEYS, 128):
                    top = jnp.maximum(top, part[:, c : c + 128])
                m_ref[at, :] = top
            return carry

        lax.fori_loop(begin, clear, functools.partial(score, True), 0)
        lax.fori_loop(clear, t, functools.partial(score, False), 0)
        score(True, t, 0)
        m_ref[...] = jnp.broadcast_to(jnp.max(m_ref[...], axis=1, keepdims=True), m_ref.shape)
        l_ref[...] = jnp.zeros_like(l_ref)
        acc_ref[...] = jnp.zeros_like(acc_ref)

        def gather(j, carry):
            v = qkv_ref[pl.ds(pl.multiple_of(j * KEYS, KEYS), KEYS), v_cols]
            numerators = []
            for h in range(heads):
                at = slice(h * KEYS, (h + 1) * KEYS)
                top = m_ref[at, :]
                total = l_ref[at, :]
                parts = []
                for c in range(0, KEYS, 128):
                    p = jnp.exp2((s_ref[j, at, c : c + 128] - top) * scaling)
                    total = total + p
                    parts.append(p.astype(BF16))
                l_ref[at, :] = total
                numerators.append(jnp.concatenate(parts, axis=1))
            acc_ref[...] += dot(jnp.concatenate(numerators, axis=0), v)
            return carry

        lax.fori_loop(begin, t + 1, gather, 0)
        for h in range(heads):
            at = slice(h * KEYS, (h + 1) * KEYS)
            total = jnp.sum(l_ref[at, :], axis=1, keepdims=True)
            o_ref[here, h * QDIM : (h + 1) * QDIM] = (acc_ref[at, :] / total).astype(BF16)
        return outer

    lax.fori_loop(0, length // KEYS, one_tile, 0)
    blocks, rows, out_width = out_ref.shape
    sends = [
        pltpu.make_async_copy(
            o_ref.at[pl.ds(r * rows, rows), :],
            out_ref.at[r, :, pl.ds(out_width - q_width, q_width)],
            sems.at[1 + r],
        )
        for r in range(blocks)
    ]
    for send in sends:
        send.start()
    for send in sends:
        send.wait()


def work(microseconds):
    return pl.CostEstimate(flops=0, transcendentals=0, bytes_accessed=int(microseconds * 3.5e6))


def smem():
    return pl.BlockSpec(memory_space=pltpu.SMEM)


def on_device(
    mixer_input, z_gate, time_step, conv_weight, conv_bias, decay_rate, skip_gain,
    norm_gain, doc_lengths, queries, attn_keys, attn_values,
):
    rows = mixer_input.shape[1]
    blocks = lax.axis_size("ctx")
    place = jnp.stack([lax.axis_index("ctx"), lax.axis_index("batch")]).astype(jnp.int32)
    raw = mixer_input[0]
    call = functools.partial(
        pl.pallas_call, compiler_params=pltpu.CompilerParams(vmem_limit_bytes=63 << 20)
    )

    o_width = QHEADS * QDIM // blocks
    qkv = call(
        pack_kernel,
        in_specs=[pl.BlockSpec(memory_space=pl.ANY)] * 3,
        out_specs=pl.BlockSpec(memory_space=pl.ANY),
        scratch_shapes=[
            pltpu.VMEM((blocks, rows, o_width + 2 * QDIM), BF16),
            pltpu.SemaphoreType.DMA((4, blocks)),
        ],
        out_shape=jax.ShapeDtypeStruct((blocks, rows, o_width + 2 * QDIM), BF16),
        name="pack",
        cost_estimate=work(3),
    )(queries[0], attn_keys[0], attn_values[0])
    rim = lax.ppermute(raw[rows - RIM :], "ctx", [(r, r + 1) for r in range(blocks - 1)])
    rim, qkv = lax.optimization_barrier((rim, qkv))
    qkv = lax.all_to_all(qkv, "ctx", split_axis=0, concat_axis=0, tiled=True)

    col, row, trail, keep, thr = call(
        prep_kernel,
        in_specs=[smem(), smem(), pl.BlockSpec(), pl.BlockSpec()],
        out_shape=[
            jax.ShapeDtypeStruct((GROUPS, rows, PER_GROUP), F32),
            jax.ShapeDtypeStruct((HEADS, rows), F32),
            jax.ShapeDtypeStruct((GROUPS, rows, 2 * PER_GROUP), BF16),
            jax.ShapeDtypeStruct((GROUPS, rows, 2 * PER_GROUP), BF16),
            jax.ShapeDtypeStruct((GROUPS, 8, PER_GROUP), BF16),
        ],
        name="prep",
        cost_estimate=work(3),
    )(place, doc_lengths, time_step[0], decay_rate[None])

    wide = lambda n: pl.BlockSpec((n, WIDTH), lambda g: (0, g))
    b_cols = lambda n: pl.BlockSpec((n, STATE), lambda g: (0, INNER // STATE + g))
    c_cols = lambda n: pl.BlockSpec((n, STATE), lambda g: (0, INNER // STATE + GROUPS + g))
    group_cols = lambda n: pl.BlockSpec((n, STATE), lambda g: (0, g))
    per_group = pl.BlockSpec((1, rows, PER_GROUP), lambda g: (g, 0, 0))
    per_group_two = pl.BlockSpec((1, rows, 2 * PER_GROUP), lambda g: (g, 0, 0))
    bias = conv_bias[None]
    half = WIDTH // 2
    x_act, b_act, c_act, fresh = call(
        front_kernel,
        grid=(GROUPS,),
        in_specs=[
            smem(), smem(),
            wide(rows), b_cols(rows), c_cols(rows),
            wide(RIM), b_cols(RIM), c_cols(RIM),
            wide(CONV), b_cols(CONV), c_cols(CONV),
            wide(1), b_cols(1), c_cols(1),
            per_group_two, pl.BlockSpec((1, 8, PER_GROUP), lambda g: (g, 0, 0)),
        ],
        out_specs=[
            wide(rows), group_cols(rows), group_cols(rows),
            pl.BlockSpec((2, STATE + EXTRA, half), lambda g: (g, 0, 0)),
        ],
        out_shape=[
            jax.ShapeDtypeStruct((rows, INNER), BF16),
            jax.ShapeDtypeStruct((rows, GROUPS * STATE), BF16),
            jax.ShapeDtypeStruct((rows, GROUPS * STATE), BF16),
            jax.ShapeDtypeStruct((2 * GROUPS, STATE + EXTRA, half), BF16),
        ],
        scratch_shapes=[pltpu.VMEM((8 + rows, 128), F32)],
        name="front",
        cost_estimate=work(40),
    )(
        place, doc_lengths, raw, raw, raw, rim, rim, rim,
        conv_weight, conv_weight, conv_weight, bias, bias, bias, trail, thr,
    )

    local = call(
        inner_kernel,
        grid=(GROUPS,),
        in_specs=[
            smem(), smem(), wide(rows), group_cols(rows), group_cols(rows), per_group,
            pl.BlockSpec((PER_GROUP, rows), lambda g: (g, 0)), wide(1),
        ],
        out_specs=wide(rows),
        out_shape=jax.ShapeDtypeStruct((rows, INNER), BF16),
        name="inner",
        cost_estimate=work(9),
    )(place, doc_lengths, x_act, b_act, c_act, col, row, jnp.repeat(skip_gain, HEAD_DIM)[None])

    fresh, qkv, local = lax.optimization_barrier((fresh, qkv, local))
    own_fresh = lax.all_to_all(fresh, "ctx", split_axis=0, concat_axis=0, tiled=True)

    tall = o_width // QDIM * KEYS
    attended = call(
        attend_kernel,
        in_specs=[smem(), smem(), pl.BlockSpec(memory_space=pl.ANY)],
        out_specs=pl.BlockSpec(memory_space=pl.ANY),
        out_shape=jax.ShapeDtypeStruct((blocks, rows, half + o_width), BF16),
        scratch_shapes=[
            pltpu.VMEM((blocks * rows, o_width + 2 * QDIM), BF16),
            pltpu.VMEM((blocks * rows, o_width), BF16),
            pltpu.SemaphoreType.DMA((1 + blocks,)),
            pltpu.VMEM((blocks * rows // KEYS, tall, KEYS), F32),
            pltpu.VMEM((tall, 128), F32),
            pltpu.VMEM((tall, 128), F32),
            pltpu.VMEM((tall, QDIM), F32),
        ],
        name="attend",
        cost_estimate=work(30),
    )(place, doc_lengths, qkv.reshape(blocks * rows, o_width + 2 * QDIM))
    own_states = call(
        scan_kernel,
        in_specs=[pl.BlockSpec(memory_space=pl.ANY)] * 2,
        out_specs=pl.BlockSpec(memory_space=pl.ANY),
        out_shape=jax.ShapeDtypeStruct((blocks, STATE, half + o_width), BF16),
        input_output_aliases={1: 0},
        scratch_shapes=[
            pltpu.VMEM((blocks, EXTRA, half), BF16),
            pltpu.VMEM((STATE // PIECE, blocks, PIECE, half), BF16),
            pltpu.VMEM((STATE // PIECE, blocks, PIECE, half), BF16),
            pltpu.SemaphoreType.DMA((STATE // PIECE,)),
            pltpu.SemaphoreType.DMA((STATE // PIECE,)),
            pltpu.SemaphoreType.DMA,
        ],
        name="scan",
        cost_estimate=work(4),
    )(own_fresh, attended)
    states = lax.all_to_all(own_states, "ctx", split_axis=0, concat_axis=0, tiled=True)

    mixer_out, attn_out = call(
        final_kernel,
        in_specs=[pl.BlockSpec(memory_space=pl.ANY)] * 6,
        out_specs=[pl.BlockSpec(memory_space=pl.ANY)] * 2,
        out_shape=[
            jax.ShapeDtypeStruct((rows, INNER), BF16),
            jax.ShapeDtypeStruct((rows, QHEADS * QDIM), BF16),
        ],
        scratch_shapes=[
            pltpu.VMEM((GROUPS, rows, WIDTH), BF16),
            pltpu.VMEM((GROUPS, 2, STATE, half + o_width), BF16),
            pltpu.VMEM((GROUPS, rows, WIDTH), BF16),
            pltpu.VMEM((GROUPS, rows, WIDTH), BF16),
            pltpu.VMEM((rows, GROUPS * STATE), BF16),
            pltpu.VMEM((GROUPS, rows, 2 * PER_GROUP), BF16),
            pltpu.VMEM((1, INNER), F32),
            pltpu.VMEM((GROUPS, rows, WIDTH), F32),
            pltpu.VMEM((rows, WIDTH), F32),
            pltpu.VMEM((rows, WIDTH), F32),
            pltpu.VMEM((rows, 128), F32),
            pltpu.SemaphoreType.DMA((7, GROUPS)),
        ],
        name="final",
        cost_estimate=work(7),
    )(local, states, z_gate[0], c_act, keep, norm_gain[None])
    return (mixer_out[None], attn_out[None])


def solution(mesh):
    placed = P("batch", "ctx", None)
    whole = P()
    return jax.shard_map(
        on_device,
        mesh=mesh,
        in_specs=(placed, placed, placed) + (whole,) * 6 + (placed,) * 3,
        out_specs=(placed, placed),
        check_vma=False,
    )
```

```python
import functools

import jax
import jax.numpy as jnp
from jax import lax
from jax.experimental import pallas as pl
from jax.experimental.pallas import tpu as pltpu
from jax.sharding import PartitionSpec as P

HEADS = 128
HEAD_DIM = 64
STATE = 128
GROUPS = 8
QHEADS = 32
KVHEADS = 8
QDIM = 128
CONV = 4
WINDOW = 2048

PER_GROUP = HEADS // GROUPS
WIDTH = PER_GROUP * HEAD_DIM
INNER = HEADS * HEAD_DIM
DOCS = 6
EPSILON = 1e-05
NEGATIVE = -1e30
LOG2E = 1.4426950408889634
EXTRA = 8
KEYS = 256
PIECE = 16
CHUNK = 16
RIM = 4

F32 = jnp.float32
BF16 = jnp.bfloat16
HIGH = lax.Precision.HIGHEST


def dot(a, b, dims=(((1,), (0,)), ((), ())), precision=None):
    return lax.dot_general(a, b, dims, precision=precision, preferred_element_type=F32)


def doc_starts(place_ref, lengths_ref):
    seq = place_ref[1]
    starts = [jnp.int32(0)]
    for d in range(DOCS - 1):
        starts.append(starts[-1] + lengths_ref[seq, d])
    return starts


def row_starts(starts, pos):
    first = jnp.zeros_like(pos)
    for s in starts[1:]:
        first = jnp.where(pos >= s, s, first)
    return first


def scalar_start(starts, pos):
    first = jnp.int32(0)
    for s in starts[1:]:
        first = jnp.where(pos >= s, s, first)
    return first


def expand_heads(copies):
    shape = (copies * PER_GROUP, WIDTH)
    row = lax.broadcasted_iota(jnp.int32, shape, 0) % PER_GROUP
    lane = lax.broadcasted_iota(jnp.int32, shape, 1)
    return jnp.where(lane // HEAD_DIM == row, 1.0, 0.0).astype(BF16)


def halves(x):
    upper = x.astype(BF16)
    return upper, (x - upper.astype(F32)).astype(BF16)


def silu(x):
    return (0.5 * x) * (1.0 + jnp.tanh(0.5 * x))


def prep_kernel(place_ref, lengths_ref, step_ref, rate_ref, col_ref, row_ref, trail_ref, keep_ref, thr_ref):
    rows = step_ref.shape[0]
    base = place_ref[0] * rows
    starts = doc_starts(place_ref, lengths_ref)
    pos = base + lax.broadcasted_iota(jnp.int32, (rows, HEADS), 0)
    first = row_starts(starts, pos)
    last_first = scalar_start(starts, base + rows - 1)
    t = step_ref[...].astype(F32)
    dt = jnp.maximum(t, 0.0) + jnp.log1p(jnp.exp(-jnp.abs(t)))
    a = dt * rate_ref[...] * (-LOG2E)
    i = lax.broadcasted_iota(jnp.int32, (rows, rows), 0)
    j = lax.broadcasted_iota(jnp.int32, (rows, rows), 1)
    tri = (i >= j).astype(F32)
    cum = dot(tri, a, precision=HIGH)
    total = cum[rows - 1 : rows, :]
    trail = halves(jnp.where(first == last_first, jnp.exp2(total - cum) * dt, 0.0))
    keep = halves(jnp.where(first < base, jnp.exp2(cum), 0.0))
    thr = halves(jnp.where(last_first < base, jnp.exp2(total), 0.0))
    row8 = lax.broadcasted_iota(jnp.int32, (8, HEADS), 0)
    thr_rows = jnp.where(
        row8 == 0, thr[0].astype(F32), jnp.where(row8 == 1, thr[1].astype(F32), 0.0)
    ).astype(BF16)
    row_ref[...] = jnp.transpose(cum - jnp.log2(dt))
    for g in range(GROUPS):
        part = slice(g * PER_GROUP, (g + 1) * PER_GROUP)
        col_ref[g] = cum[:, part]
        trail_ref[g] = jnp.concatenate([trail[0][:, part], trail[1][:, part]], axis=1)
        keep_ref[g] = jnp.concatenate([keep[0][:, part], keep[1][:, part]], axis=1)
        thr_ref[g] = thr_rows[:, part]


def front_kernel(
    place_ref, lengths_ref, x_ref, b_ref, c_ref, hx_ref, hb_ref, hc_ref,
    wx_ref, wb_ref, wc_ref, ox_ref, ob_ref, oc_ref, trail_ref, thr_ref,
    xa_ref, ba_ref, ca_ref, f_ref, pad_ref,
):
    rows = x_ref.shape[0]
    base = place_ref[0] * rows
    starts = doc_starts(place_ref, lengths_ref)
    pos = base + lax.broadcasted_iota(jnp.int32, (rows, 128), 0)
    rel = pos - row_starts(starts, pos)
    masks = [None] + [rel >= d for d in range(1, CONV)]

    def conv(src, rim, weight, bias, dst, lo):
        at = slice(lo, lo + 128)
        pad_ref[8 - RIM : 8, :] = rim[:, at].astype(F32)
        pad_ref[8 : 8 + rows, :] = src[:, at].astype(F32)
        acc = pad_ref[8 : 8 + rows, :] * weight[3:4, at] + bias[:, at]
        for d in range(1, CONV):
            tap = pad_ref[8 - d : 8 - d + rows, :] * weight[3 - d : 4 - d, at]
            acc = acc + jnp.where(masks[d], tap, 0.0)
        dst[:, at] = silu(acc).astype(BF16)

    for lo in range(0, WIDTH, 128):
        conv(x_ref, hx_ref, wx_ref, ox_ref, xa_ref, lo)
    conv(b_ref, hb_ref, wb_ref, ob_ref, ba_ref, 0)
    conv(c_ref, hc_ref, wc_ref, oc_ref, ca_ref, 0)

    scale = dot(trail_ref[0], expand_heads(2))
    weighted = (xa_ref[...].astype(F32) * scale).astype(BF16)
    fresh = dot(ba_ref[...], weighted, (((0,), (0,)), ((), ()))).astype(BF16)
    extra = dot(thr_ref[0], expand_heads(1)).astype(BF16)
    half = WIDTH // 2
    for k in range(2):
        f_ref[k, 0:STATE, :] = fresh[:, k * half : (k + 1) * half]
        f_ref[k, STATE : STATE + EXTRA, :] = extra[:, k * half : (k + 1) * half]


def inner_kernel(place_ref, lengths_ref, xa_ref, ba_ref, ca_ref, col_ref, row_ref, skip_ref, y_ref):
    rows = xa_ref.shape[0]
    base = place_ref[0] * rows
    starts = doc_starts(place_ref, lengths_ref)
    i = base + lax.broadcasted_iota(jnp.int32, (rows, rows), 0)
    j = base + lax.broadcasted_iota(jnp.int32, (rows, rows), 1)
    first = row_starts(starts, i)
    blocked = jnp.where((j <= i) & (j >= first), 0.0, NEGATIVE)
    scores = dot(ca_ref[...], ba_ref[...], (((1,), (1,)), ((), ())))
    lane = lax.broadcasted_iota(jnp.int32, (rows, 128), 1)
    col = col_ref[0]
    for p in range(PER_GROUP // 2):
        weights = []
        for h in (2 * p, 2 * p + 1):
            spread = (col[:, h : h + 1] + blocked) - row_ref[h : h + 1, :]
            weights.append((scores * jnp.exp2(spread)).astype(BF16))
        at = slice(p * 128, (p + 1) * 128)
        x = xa_ref[:, at]
        zero = jnp.zeros_like(x)
        both = jnp.concatenate(
            [jnp.where(lane < HEAD_DIM, x, zero), jnp.where(lane < HEAD_DIM, zero, x)], axis=0
        )
        y = dot(jnp.concatenate(weights, axis=1), both)
        y_ref[:, at] = (y + x.astype(F32) * skip_ref[:, at]).astype(BF16)


def scan_kernel(f_ref, held_out_ref, out_ref, tail_ref, held_ref, state_ref, sems, out_sems, tail_sem):
    blocks, _, width = f_ref.shape
    pieces, _, piece, _ = held_ref.shape
    tail = pltpu.make_async_copy(f_ref.at[:, pl.ds(STATE, EXTRA), :], tail_ref, tail_sem)
    loads = [
        pltpu.make_async_copy(f_ref.at[:, pl.ds(q * piece, piece), :], held_ref.at[q], sems.at[q])
        for q in range(pieces)
    ]
    stores = [
        pltpu.make_async_copy(
            state_ref.at[q], out_ref.at[:, pl.ds(q * piece, piece), pl.ds(0, width)], out_sems.at[q]
        )
        for q in range(pieces)
    ]
    tail.start()
    for load in loads:
        load.start()
    tail.wait()
    for q in range(pieces):
        loads[q].wait()
        state = jnp.zeros((piece, width), F32)
        for r in range(blocks):
            state_ref[q, r] = state.astype(BF16)
            if r + 1 < blocks:
                ends = tail_ref[r].astype(F32)
                state = state * (ends[0:1, :] + ends[1:2, :]) + held_ref[q, r].astype(F32)
        stores[q].start()
    for store in stores:
        store.wait()


def final_kernel(
    y_far, s_far, z_far, ca_far, keep_far, gain_far, o_far, attn_far,
    y_ref, s_ref, z_ref, o_ref, ca_ref, keep_ref, gain_ref, scale_ref, even_ref, odd_ref, square_ref, sems,
):
    rows = y_far.shape[0]
    half = WIDTH // 2
    own = s_ref.shape[3] - half
    small = (
        pltpu.make_async_copy(keep_far, keep_ref, sems.at[6, 0]),
        pltpu.make_async_copy(ca_far, ca_ref, sems.at[6, 1]),
        pltpu.make_async_copy(gain_far, gain_ref, sems.at[6, 2]),
    )
    loads, stores = [], []
    for g in range(GROUPS):
        cols = pl.ds(g * WIDTH, WIDTH)
        loads.append((
            pltpu.make_async_copy(s_far.at[pl.ds(2 * g, 2)], s_ref.at[g], sems.at[0, g]),
            pltpu.make_async_copy(y_far.at[:, cols], y_ref.at[g], sems.at[1, g]),
            pltpu.make_async_copy(z_far.at[:, cols], z_ref.at[g], sems.at[2, g]),
        ))
        stores.append([pltpu.make_async_copy(o_ref.at[g], o_far.at[:, cols], sems.at[3, g])])
        for k in range(2):
            source = s_ref.at[g, k, :, pl.ds(half, own)]
            target = attn_far.at[:, pl.ds((2 * g + k) * own, own)]
            stores[g].append(pltpu.make_async_copy(source, target, sems.at[4 + k, g]))
    for copy in small:
        copy.start()
    for group in loads:
        for copy in group:
            copy.start()
    spread = expand_heads(2)
    for copy in small:
        copy.wait()
    for g in range(GROUPS):
        scale_ref[g] = dot(keep_ref[g], spread)

    def carry(g, into_ref):
        loads[g][0].wait()
        for copy in stores[g][1:]:
            copy.start()
        ca = ca_ref[:, g * STATE : (g + 1) * STATE]
        for k in range(2):
            into_ref[:, k * half : (k + 1) * half] = dot(ca, s_ref[g, k, :, :half])

    carry(0, even_ref)
    for g in range(GROUPS):
        here_ref, next_ref = (even_ref, odd_ref) if g % 2 == 0 else (odd_ref, even_ref)
        if g + 1 < GROUPS:
            carry(g + 1, next_ref)
        for copy in loads[g][1:]:
            copy.wait()
        for lo in range(0, rows, CHUNK):
            at = slice(lo, lo + CHUNK)
            mixed = (y_ref[g, at, :].astype(F32) + scale_ref[g, at, :] * here_ref[at, :]).astype(BF16).astype(F32)
            gated = mixed * silu(z_ref[g, at, :].astype(F32))
            here_ref[at, :] = gated
            total = gated[:, :128] * gated[:, :128]
            for c in range(128, WIDTH, 128):
                total = total + gated[:, c : c + 128] * gated[:, c : c + 128]
            square_ref[at, :] = total
        mean = jnp.sum(square_ref[...], axis=1, keepdims=True) * (1.0 / WIDTH)
        square_ref[...] = jnp.broadcast_to(lax.rsqrt(mean + EPSILON), square_ref.shape)
        for lo in range(0, rows, CHUNK):
            at = slice(lo, lo + CHUNK)
            factor = square_ref[at, :]
            for c in range(0, WIDTH, 128):
                gain = gain_ref[:, g * WIDTH + c : g * WIDTH + c + 128]
                o_ref[g, at, c : c + 128] = (here_ref[at, c : c + 128] * factor * gain).astype(BF16)
        stores[g][0].start()
    for group in stores:
        for copy in group:
            copy.wait()


def pack_kernel(q_ref, k_ref, v_ref, out_ref, held_ref, sems):
    parts = out_ref.shape[0]
    width = q_ref.shape[1] // parts
    loads, stores = [], []
    for d in range(parts):
        at = pl.ds(d * KVHEADS // parts * QDIM, QDIM)
        q_cols = pl.ds(d * width, width)
        loads += [
            pltpu.make_async_copy(q_ref.at[:, q_cols], held_ref.at[d, :, pl.ds(0, width)], sems.at[0, d]),
            pltpu.make_async_copy(k_ref.at[:, at], held_ref.at[d, :, pl.ds(width, QDIM)], sems.at[1, d]),
            pltpu.make_async_copy(v_ref.at[:, at], held_ref.at[d, :, pl.ds(width + QDIM, QDIM)], sems.at[2, d]),
        ]
        stores.append(pltpu.make_async_copy(held_ref.at[d], out_ref.at[d], sems.at[3, d]))
    for load in loads:
        load.start()
    for d in range(parts):
        for load in loads[3 * d : 3 * d + 3]:
            load.wait()
        stores[d].start()
    for store in stores:
        store.wait()


def attend_kernel(place_ref, lengths_ref, far_ref, out_ref, qkv_ref, o_ref, sems, s_ref, m_ref, l_ref, acc_ref):
    copy = pltpu.make_async_copy(far_ref, qkv_ref, sems.at[0])
    copy.start()
    copy.wait()
    length = qkv_ref.shape[0]
    q_width = qkv_ref.shape[1] - 2 * QDIM
    heads = q_width // QDIM
    k_cols, v_cols = slice(q_width, q_width + QDIM), slice(q_width + QDIM, q_width + 2 * QDIM)
    starts = doc_starts(place_ref, lengths_ref)
    lane = lax.broadcasted_iota(jnp.int32, (KEYS, KEYS), 1)
    scaling = QDIM ** (-0.5) * LOG2E

    def one_tile(t, outer):
        base = t * KEYS
        here = pl.ds(pl.multiple_of(base, KEYS), KEYS)
        pos = base + lax.broadcasted_iota(jnp.int32, (KEYS, KEYS), 0)
        first = jnp.maximum(row_starts(starts, pos), pos - (WINDOW - 1))
        last = base + KEYS - 1
        lowest = jnp.maximum(scalar_start(starts, base), base - (WINDOW - 1))
        highest = jnp.maximum(scalar_start(starts, last), last - (WINDOW - 1))
        begin = lowest // KEYS
        clear = jnp.minimum((highest + KEYS - 1) // KEYS, t)
        queries = jnp.concatenate([qkv_ref[here, h * QDIM : (h + 1) * QDIM] for h in range(heads)], axis=0)
        m_ref[...] = jnp.full_like(m_ref, NEGATIVE)

        def score(masked, j, carry):
            k = qkv_ref[pl.ds(pl.multiple_of(j * KEYS, KEYS), KEYS), k_cols]
            s = dot(queries, k, (((1,), (1,)), ((), ())))
            if masked:
                key = j * KEYS + lane
                visible = (key <= pos) & (key >= first)
            for h in range(heads):
                at = slice(h * KEYS, (h + 1) * KEYS)
                part = s[at]
                if masked:
                    part = jnp.where(visible, part, NEGATIVE)
                s_ref[j, at, :] = part
                top = m_ref[at, :]
                for c in range(0, KEYS, 128):
                    top = jnp.maximum(top, part[:, c : c + 128])
                m_ref[at, :] = top
            return carry

        lax.fori_loop(begin, clear, functools.partial(score, True), 0)
        lax.fori_loop(clear, t, functools.partial(score, False), 0)
        score(True, t, 0)
        m_ref[...] = jnp.broadcast_to(jnp.max(m_ref[...], axis=1, keepdims=True), m_ref.shape)
        l_ref[...] = jnp.zeros_like(l_ref)
        acc_ref[...] = jnp.zeros_like(acc_ref)

        def gather(j, carry):
            v = qkv_ref[pl.ds(pl.multiple_of(j * KEYS, KEYS), KEYS), v_cols]
            numerators = []
            for h in range(heads):
                at = slice(h * KEYS, (h + 1) * KEYS)
                top = m_ref[at, :]
                total = l_ref[at, :]
                parts = []
                for c in range(0, KEYS, 128):
                    p = jnp.exp2((s_ref[j, at, c : c + 128] - top) * scaling)
                    total = total + p
                    parts.append(p.astype(BF16))
                l_ref[at, :] = total
                numerators.append(jnp.concatenate(parts, axis=1))
            acc_ref[...] += dot(jnp.concatenate(numerators, axis=0), v)
            return carry

        lax.fori_loop(begin, t + 1, gather, 0)
        for h in range(heads):
            at = slice(h * KEYS, (h + 1) * KEYS)
            total = jnp.sum(l_ref[at, :], axis=1, keepdims=True)
            o_ref[here, h * QDIM : (h + 1) * QDIM] = (acc_ref[at, :] / total).astype(BF16)
        return outer

    lax.fori_loop(0, length // KEYS, one_tile, 0)
    blocks, rows, out_width = out_ref.shape
    sends = [
        pltpu.make_async_copy(
            o_ref.at[pl.ds(r * rows, rows), :],
            out_ref.at[r, :, pl.ds(out_width - q_width, q_width)],
            sems.at[1 + r],
        )
        for r in range(blocks)
    ]
    for send in sends:
        send.start()
    for send in sends:
        send.wait()


def work(microseconds):
    return pl.CostEstimate(flops=0, transcendentals=0, bytes_accessed=int(microseconds * 3.5e6))


def smem():
    return pl.BlockSpec(memory_space=pltpu.SMEM)


def on_device(
    mixer_input, z_gate, time_step, conv_weight, conv_bias, decay_rate, skip_gain,
    norm_gain, doc_lengths, queries, attn_keys, attn_values,
):
    rows = mixer_input.shape[1]
    blocks = lax.axis_size("ctx")
    place = jnp.stack([lax.axis_index("ctx"), lax.axis_index("batch")]).astype(jnp.int32)
    raw = mixer_input[0]
    call = functools.partial(
        pl.pallas_call, compiler_params=pltpu.CompilerParams(vmem_limit_bytes=63 << 20)
    )

    o_width = QHEADS * QDIM // blocks
    qkv = call(
        pack_kernel,
        in_specs=[pl.BlockSpec(memory_space=pl.ANY)] * 3,
        out_specs=pl.BlockSpec(memory_space=pl.ANY),
        scratch_shapes=[
            pltpu.VMEM((blocks, rows, o_width + 2 * QDIM), BF16),
            pltpu.SemaphoreType.DMA((4, blocks)),
        ],
        out_shape=jax.ShapeDtypeStruct((blocks, rows, o_width + 2 * QDIM), BF16),
        name="pack",
        cost_estimate=work(3),
    )(queries[0], attn_keys[0], attn_values[0])
    rim = lax.ppermute(raw[rows - RIM :], "ctx", [(r, r + 1) for r in range(blocks - 1)])
    rim, qkv = lax.optimization_barrier((rim, qkv))
    qkv = lax.all_to_all(qkv, "ctx", split_axis=0, concat_axis=0, tiled=True)

    col, row, trail, keep, thr = call(
        prep_kernel,
        in_specs=[smem(), smem(), pl.BlockSpec(), pl.BlockSpec()],
        out_shape=[
            jax.ShapeDtypeStruct((GROUPS, rows, PER_GROUP), F32),
            jax.ShapeDtypeStruct((HEADS, rows), F32),
            jax.ShapeDtypeStruct((GROUPS, rows, 2 * PER_GROUP), BF16),
            jax.ShapeDtypeStruct((GROUPS, rows, 2 * PER_GROUP), BF16),
            jax.ShapeDtypeStruct((GROUPS, 8, PER_GROUP), BF16),
        ],
        name="prep",
        cost_estimate=work(3),
    )(place, doc_lengths, time_step[0], decay_rate[None])

    wide = lambda n: pl.BlockSpec((n, WIDTH), lambda g: (0, g))
    b_cols = lambda n: pl.BlockSpec((n, STATE), lambda g: (0, INNER // STATE + g))
    c_cols = lambda n: pl.BlockSpec((n, STATE), lambda g: (0, INNER // STATE + GROUPS + g))
    group_cols = lambda n: pl.BlockSpec((n, STATE), lambda g: (0, g))
    per_group = pl.BlockSpec((1, rows, PER_GROUP), lambda g: (g, 0, 0))
    per_group_two = pl.BlockSpec((1, rows, 2 * PER_GROUP), lambda g: (g, 0, 0))
    bias = conv_bias[None]
    half = WIDTH // 2
    x_act, b_act, c_act, fresh = call(
        front_kernel,
        grid=(GROUPS,),
        in_specs=[
            smem(), smem(),
            wide(rows), b_cols(rows), c_cols(rows),
            wide(RIM), b_cols(RIM), c_cols(RIM),
            wide(CONV), b_cols(CONV), c_cols(CONV),
            wide(1), b_cols(1), c_cols(1),
            per_group_two, pl.BlockSpec((1, 8, PER_GROUP), lambda g: (g, 0, 0)),
        ],
        out_specs=[
            wide(rows), group_cols(rows), group_cols(rows),
            pl.BlockSpec((2, STATE + EXTRA, half), lambda g: (g, 0, 0)),
        ],
        out_shape=[
            jax.ShapeDtypeStruct((rows, INNER), BF16),
            jax.ShapeDtypeStruct((rows, GROUPS * STATE), BF16),
            jax.ShapeDtypeStruct((rows, GROUPS * STATE), BF16),
            jax.ShapeDtypeStruct((2 * GROUPS, STATE + EXTRA, half), BF16),
        ],
        scratch_shapes=[pltpu.VMEM((8 + rows, 128), F32)],
        name="front",
        cost_estimate=work(40),
    )(
        place, doc_lengths, raw, raw, raw, rim, rim, rim,
        conv_weight, conv_weight, conv_weight, bias, bias, bias, trail, thr,
    )

    local = call(
        inner_kernel,
        grid=(GROUPS,),
        in_specs=[
            smem(), smem(), wide(rows), group_cols(rows), group_cols(rows), per_group,
            pl.BlockSpec((PER_GROUP, rows), lambda g: (g, 0)), wide(1),
        ],
        out_specs=wide(rows),
        out_shape=jax.ShapeDtypeStruct((rows, INNER), BF16),
        name="inner",
        cost_estimate=work(9),
    )(place, doc_lengths, x_act, b_act, c_act, col, row, jnp.repeat(skip_gain, HEAD_DIM)[None])

    fresh, qkv, local = lax.optimization_barrier((fresh, qkv, local))
    own_fresh = lax.all_to_all(fresh, "ctx", split_axis=0, concat_axis=0, tiled=True)

    tall = o_width // QDIM * KEYS
    attended = call(
        attend_kernel,
        in_specs=[smem(), smem(), pl.BlockSpec(memory_space=pl.ANY)],
        out_specs=pl.BlockSpec(memory_space=pl.ANY),
        out_shape=jax.ShapeDtypeStruct((blocks, rows, half + o_width), BF16),
        scratch_shapes=[
            pltpu.VMEM((blocks * rows, o_width + 2 * QDIM), BF16),
            pltpu.VMEM((blocks * rows, o_width), BF16),
            pltpu.SemaphoreType.DMA((1 + blocks,)),
            pltpu.VMEM((blocks * rows // KEYS, tall, KEYS), F32),
            pltpu.VMEM((tall, 128), F32),
            pltpu.VMEM((tall, 128), F32),
            pltpu.VMEM((tall, QDIM), F32),
        ],
        name="attend",
        cost_estimate=work(30),
    )(place, doc_lengths, qkv.reshape(blocks * rows, o_width + 2 * QDIM))
    own_states = call(
        scan_kernel,
        in_specs=[pl.BlockSpec(memory_space=pl.ANY)] * 2,
        out_specs=pl.BlockSpec(memory_space=pl.ANY),
        out_shape=jax.ShapeDtypeStruct((blocks, STATE, half + o_width), BF16),
        input_output_aliases={1: 0},
        scratch_shapes=[
            pltpu.VMEM((blocks, EXTRA, half), BF16),
            pltpu.VMEM((STATE // PIECE, blocks, PIECE, half), BF16),
            pltpu.VMEM((STATE // PIECE, blocks, PIECE, half), BF16),
            pltpu.SemaphoreType.DMA((STATE // PIECE,)),
            pltpu.SemaphoreType.DMA((STATE // PIECE,)),
            pltpu.SemaphoreType.DMA,
        ],
        name="scan",
        cost_estimate=work(4),
    )(own_fresh, attended)
    states = lax.all_to_all(own_states, "ctx", split_axis=0, concat_axis=0, tiled=True)

    mixer_out, attn_out = call(
        final_kernel,
        in_specs=[pl.BlockSpec(memory_space=pl.ANY)] * 6,
        out_specs=[pl.BlockSpec(memory_space=pl.ANY)] * 2,
        out_shape=[
            jax.ShapeDtypeStruct((rows, INNER), BF16),
            jax.ShapeDtypeStruct((rows, QHEADS * QDIM), BF16),
        ],
        scratch_shapes=[
            pltpu.VMEM((GROUPS, rows, WIDTH), BF16),
            pltpu.VMEM((GROUPS, 2, STATE, half + o_width), BF16),
            pltpu.VMEM((GROUPS, rows, WIDTH), BF16),
            pltpu.VMEM((GROUPS, rows, WIDTH), BF16),
            pltpu.VMEM((rows, GROUPS * STATE), BF16),
            pltpu.VMEM((GROUPS, rows, 2 * PER_GROUP), BF16),
            pltpu.VMEM((1, INNER), F32),
            pltpu.VMEM((GROUPS, rows, WIDTH), F32),
            pltpu.VMEM((rows, WIDTH), F32),
            pltpu.VMEM((rows, WIDTH), F32),
            pltpu.VMEM((rows, 128), F32),
            pltpu.SemaphoreType.DMA((7, GROUPS)),
        ],
        name="final",
        cost_estimate=work(7),
    )(local, states, z_gate[0], c_act, keep, norm_gain[None])
    return (mixer_out[None], attn_out[None])


def solution(mesh):
    placed = P("batch", "ctx", None)
    whole = P()
    return jax.shard_map(
        on_device,
        mesh=mesh,
        in_specs=(placed, placed, placed) + (whole,) * 6 + (placed,) * 3,
        out_specs=(placed, placed),
        check_vma=False,
    )
```
